32 devices in a mesh: dp: 2 (over x), expert: 16 (over z, y, core).
Axes of the slice: x: 2, y: 2, z: 4, core: 2. Of those that a mesh axis runs over, the one named last changes fastest.
Arguments:
- saved_inputs: bfloat16 [1024, 3584], P('expert'), may hold values from -6 to 6
- output_grad: bfloat16 [1024, 3584], P('expert'), may hold values from -6 to 6
- routes: int32 [1024, 8], P('expert'), may hold values from 0 to 15, all different within a row; in each aligned block of 64 rows (0 to 63, 64 to 127, ...) at most 36 rows name the same one
- route_gates: bfloat16 [1024, 8], P('expert'), may hold values from 0.099609375 to 1
- expert_gate: bfloat16 [16, 3584, 1024], P('expert', None, 'dp'), may hold values from -0.09375 to 0.09375
- expert_up: bfloat16 [16, 3584, 1024], P('expert', None, 'dp'), may hold values from -0.09375 to 0.09375
- expert_down: bfloat16 [16, 1024, 3584], P('expert', 'dp'), may hold values from -0.1875 to 0.1875
- proj_basis: bfloat16 [16, 1024, 128], P('expert', 'dp'), may hold values from -0.1875 to 0.1875
Outputs:
- input_grad: bfloat16 [1024, 3584], P('expert', 'dp')
- projected: float32 [16, 3584, 3, 128], P('expert', 'dp')
The draws below stay inside these ranges and needn't reach their ends.
Inputs may be any that keep to these rules, and one draw needn't show every extreme that they name: Within each aligned block of 64 tokens no expert is named by more than 36 routes, and in every draw some expert is named by exactly 36.
All inputs are finite; a program needn't handle non-finite values.
Results may differ from the reference program's by a relative error of at most 0.009.
Values may be sent and summed in bfloat16 or wider, within the bound.
A program may use at most 128 MiB of HBM per device.

```python
import math
import jax
import jax.numpy as jnp
import numpy as np
from jax import lax

D = 3584
FF = 1024
TOPK = 8
RANK = 128
TOK_DEV = 64
EXPERTS = 16
TOKENS = 1024
CAP = 36
FF_DEV = 512
N_DP = 2


def block_scale(rng, shape, cuts, smallest, largest):
    factor_of = 1.0
    for axis_at, shards_of in cuts:
        steps = jax.random.uniform(jax.random.fold_in(jax.random.fold_in(rng, 6), axis_at), (shards_of,), jnp.float32, smallest / len(cuts), largest / len(cuts))
        factor_of = factor_of * jnp.repeat(jnp.exp(steps), shape[axis_at] // shards_of).reshape((-1,) + (1,) * (len(shape) - 1 - axis_at))
    return factor_of


def routed_block(stream_key, own, number, rows, count, top, limit, slope):
    sequence = jax.random.permutation(stream_key, count)
    crowded, ordinary = load_shares(count, rows * top, limit, slope, True), load_shares(count, rows * top, limit, slope, False)
    places = jnp.arange(count)

    def named(tallies, offset_by):
        used = int((tallies > 0).sum())
        fixed = max(1, used // 4)
        moved = fixed + (places - fixed + offset_by * (used - fixed)) % max(1, count - fixed)
        return jnp.zeros((count,), jnp.int32).at[sequence[jnp.where(places < fixed, places, moved)]].set(jnp.asarray(tallies, jnp.int32))

    tallies = jnp.where(number % 4 == 0, named(crowded, number // 4), named(ordinary, number - number // 4 - 1))
    mixed = jax.random.permutation(jax.random.fold_in(own, 3), count)
    donor, receiver = mixed[0:count // 2 * 2:2], mixed[1:count // 2 * 2:2]
    room = jnp.minimum(tallies[donor] - 1, limit - tallies[receiver]) // 2
    room = jnp.where((donor == sequence[0]) | (receiver == sequence[0]) | (tallies[receiver] == 0), 0, jnp.maximum(room, 0))
    moved = jax.random.randint(jax.random.fold_in(own, 4), (count // 2,), 0, 1 << 20) % (room + 1)
    tallies = tallies.at[donor].add(-moved).at[receiver].add(moved)
    items = jnp.searchsorted(jnp.cumsum(tallies), jnp.arange(rows * top), side="right").astype(jnp.int32)
    grid = items.reshape(top, rows).T
    grid = grid[jax.random.permutation(jax.random.fold_in(own, 1), rows)]
    offset_by = jax.random.randint(jax.random.fold_in(own, 2), (rows, 1), 0, top)
    return jnp.take_along_axis(grid, (jnp.arange(top)[None, :] + offset_by) % top, axis=1)


def load_shares(count, total, limit, lean, full):
    portions = [(1 << 20) // math.isqrt(grade ** lean) + 1 for grade in range(1, count + 1)]
    largest = limit if full else min(limit, max(-(-total // count), total * portions[0] // sum(portions)))
    least = 1 if total - largest >= count - 1 else 0
    given, spare = [largest] + [least] * (count - 1), total - largest - least * (count - 1)
    while spare > 0:
        free = [i for i in range(1, count) if given[i] < largest] or [i for i in range(1, count) if given[i] < limit]
        whole, budget = sum([portions[i] for i in free]), spare
        for i in free:
            extra = min(limit - given[i], max(1, budget * portions[i] // whole), spare)
            given[i] = given[i] + extra
            spare = spare - extra
    return np.array(given)


def gaussian(stream_key, dims, deviation, most, split=(), held_as=jnp.bfloat16):
    result = deviation * jax.random.normal(stream_key, dims, jnp.float32)
    if split:
        result = result * block_scale(stream_key, dims, split, -0.22, 0.18)
    return jnp.clip(result, -most, most).astype(held_as)


def setup_inputs(seed: int = 0) -> dict:
    streams_of = jax.random.split(jax.random.key(seed), 9)
    saved_inputs = gaussian(streams_of[0], (TOKENS, D), 1.0, 6.0, ((0, 16),))
    output_grad = gaussian(streams_of[1], (TOKENS, D), 1.0, 6.0, ((0, 16),))
    routes_keys = jax.random.split(jax.random.fold_in(streams_of[2], 1), TOKENS // TOK_DEV)
    routes_turns = jax.random.permutation(jax.random.fold_in(streams_of[2], 3), TOKENS // TOK_DEV)
    routes = jax.vmap(lambda own, number: routed_block(jax.random.fold_in(streams_of[2], 2), own, number, TOK_DEV, EXPERTS, TOPK, CAP, 2))(routes_keys, routes_turns).reshape((TOKENS, TOPK))
    route_gates = jnp.clip(jnp.exp(math.log(1.0) - 2.306499 * jax.random.uniform(streams_of[3], (TOKENS, TOPK), jnp.float32) ** block_scale(streams_of[3], (TOKENS, TOPK), ((0, 16),), -0.2, 0.2)), 0.099609375, 1.0).astype(jnp.bfloat16)
    expert_gate = gaussian(streams_of[4], (EXPERTS, D, FF), D ** -0.5, 0.09375, ((0, 16), (2, 2)))
    expert_up = gaussian(streams_of[5], (EXPERTS, D, FF), D ** -0.5, 0.09375, ((0, 16), (2, 2)))
    expert_down = gaussian(streams_of[6], (EXPERTS, FF, D), FF ** -0.5, 0.1875, ((0, 16), (1, 2)))
    proj_basis = gaussian(streams_of[7], (EXPERTS, FF, RANK), FF ** -0.5, 0.1875, ((0, 16), (1, 2)))
    return dict(saved_inputs=saved_inputs, output_grad=output_grad, routes=routes, route_gates=route_gates, expert_gate=expert_gate, expert_up=expert_up, expert_down=expert_down, proj_basis=proj_basis)


def reference(saved_inputs, output_grad, routes, route_gates, expert_gate, expert_up, expert_down, proj_basis):
    sources = EXPERTS
    flat_routes = routes.reshape(sources, TOK_DEV * TOPK)
    one_hot = (flat_routes[:, :, None] == jnp.arange(EXPERTS, dtype=jnp.int32)[None, None, :]).astype(jnp.int32)
    earlier = jnp.sum((jnp.cumsum(one_hot, axis=1) - one_hot) * one_hot, axis=2)
    source_ids = jnp.arange(sources, dtype=jnp.int32)[:, None]
    per_expert = sources * CAP
    target_row = (flat_routes * per_expert + source_ids * CAP + earlier).reshape(-1).astype(jnp.int32)
    token_ids = jnp.repeat(jnp.arange(TOKENS, dtype=jnp.int32), TOPK)
    total_rows = EXPERTS * per_expert
    input_rows = jnp.zeros((total_rows, D), jnp.bfloat16).at[target_row].set(saved_inputs[token_ids])
    grad_rows = jnp.zeros((total_rows, D), jnp.bfloat16).at[target_row].set(output_grad[token_ids])
    gate_rows = jnp.zeros((total_rows,), jnp.bfloat16).at[target_row].set(route_gates.reshape(-1))
    owner_rows = jnp.full((total_rows,), TOKENS, jnp.int32).at[target_row].set(token_ids)
    input_rows = input_rows.reshape(EXPERTS, per_expert, D)
    grad_rows = grad_rows.reshape(EXPERTS, per_expert, D)
    gate_rows = gate_rows.reshape(EXPERTS, per_expert)
    owner_rows = owner_rows.reshape(EXPERTS, per_expert)

    def expert_step(accum, items):
        xin, yin, gin, owners, gate_w, up_w, down_w, basis = items
        gain = gin.astype(jnp.float32)[:, None]
        part_total = jnp.zeros((per_expert, D), jnp.float32)
        terms = jnp.zeros((D, 3, RANK), jnp.float32)
        for block in range(N_DP):
            lower = block * FF_DEV
            gate_b = gate_w[:, lower:lower + FF_DEV]
            up_b = up_w[:, lower:lower + FF_DEV]
            down_b = down_w[lower:lower + FF_DEV, :]
            basis_b = basis[lower:lower + FF_DEV, :]
            pre_gate = jnp.dot(xin, gate_b, preferred_element_type=jnp.float32)
            pre_up = jnp.dot(xin, up_b, preferred_element_type=jnp.float32)
            grad_hidden = jnp.dot(yin, down_b.T, preferred_element_type=jnp.float32)
            sigma = jax.nn.sigmoid(pre_gate)
            silu_val = pre_gate * sigma
            scaled = gain * grad_hidden
            grad_up = (scaled * silu_val).astype(jnp.bfloat16)
            grad_gate = (scaled * pre_up * sigma * (1.0 + pre_gate * (1.0 - sigma))).astype(jnp.bfloat16)
            hidden = (silu_val * pre_up).astype(jnp.bfloat16)
            part_b = (jnp.dot(grad_gate, gate_b.T, preferred_element_type=jnp.float32)
                      + jnp.dot(grad_up, up_b.T, preferred_element_type=jnp.float32)).astype(jnp.bfloat16)
            part_total = part_total + part_b.astype(jnp.float32)
            coef_gate = jnp.dot(grad_gate, basis_b, preferred_element_type=jnp.float32).astype(jnp.bfloat16)
            coef_up = jnp.dot(grad_up, basis_b, preferred_element_type=jnp.float32).astype(jnp.bfloat16)
            coef_down = (gain * jnp.dot(hidden, basis_b, preferred_element_type=jnp.float32)).astype(jnp.bfloat16)
            term_b = jnp.stack([
                jnp.dot(xin.T, coef_gate, preferred_element_type=jnp.float32),
                jnp.dot(xin.T, coef_up, preferred_element_type=jnp.float32),
                jnp.dot(yin.T, coef_down, preferred_element_type=jnp.float32)], axis=1).astype(jnp.bfloat16)
            terms = terms + term_b.astype(jnp.float32)
        accum = accum.at[owners].add(part_total, mode="drop")
        return accum, terms

    start_grad = jnp.zeros((TOKENS, D), jnp.float32)
    grads, projected = lax.scan(expert_step, start_grad, (input_rows, grad_rows, gate_rows, owner_rows, expert_gate, expert_up, expert_down, proj_basis))
    return grads.astype(jnp.bfloat16), projected
```

```python
import functools

import jax
import jax.numpy as jnp
from jax import lax
from jax.experimental import pallas as pl
from jax.experimental.pallas import tpu as pltpu
from jax.sharding import PartitionSpec as P


def slot_form(
    saved_inputs, output_grad, routes, route_gates, expert_gate, expert_up, expert_down, proj_basis
):
    token_count, model_width = saved_inputs.shape
    top_count = routes.shape[1]
    expert_count = lax.axis_size("expert")
    group_count = lax.axis_size("dp")
    capacity = token_count * top_count * 9 // (8 * expert_count)
    slot_count = expert_count * capacity
    column_width = model_width // group_count
    route_count = token_count * top_count
    flat_routes = routes.reshape(-1)
    position = jnp.arange(route_count, dtype=jnp.int32)
    earlier = jnp.sum(
        (
            (flat_routes[:, None] == flat_routes[None, :])
            & (position[None, :] < position[:, None])
        ).astype(jnp.int32),
        axis=1,
    )
    target_slot = flat_routes * capacity + earlier
    slot_owner = (
        jnp.full((slot_count,), route_count, jnp.int32)
        .at[target_slot]
        .set(jnp.arange(route_count, dtype=jnp.int32))
    )
    filled = slot_owner < route_count
    safe_route = jnp.minimum(slot_owner, route_count - 1)
    source_token = safe_route // top_count
    zero_half = jnp.zeros((), jnp.bfloat16)
    gate_slots = jnp.where(filled, route_gates.reshape(-1)[safe_route], zero_half).reshape(
        expert_count, capacity
    )
    token_map = (
        (source_token[None, :] == jnp.arange(token_count, dtype=jnp.int32)[:, None])
        & filled[None, :]
    ).astype(jnp.bfloat16)
    contract_first = (((0,), (0,)), ((), ()))

    def to_slots(source_rows):
        picked = lax.dot_general(
            token_map, source_rows, contract_first, preferred_element_type=jnp.float32
        ).astype(jnp.bfloat16)
        return picked.reshape(expert_count, capacity * source_rows.shape[1])

    recv_inputs, recv_grads, recv_gates = (
        lax.all_to_all(to_slots(saved_inputs), "expert", split_axis=0, concat_axis=0, tiled=True),
        lax.all_to_all(to_slots(output_grad), "expert", split_axis=0, concat_axis=0, tiled=True),
        lax.all_to_all(gate_slots, "expert", split_axis=0, concat_axis=0, tiled=True),
    )
    input_rows = recv_inputs.reshape(slot_count, model_width)
    grad_rows = recv_grads.reshape(slot_count, model_width)
    gain = recv_gates.reshape(slot_count, 1).astype(jnp.float32)
    gate_w = expert_gate[0]
    up_w = expert_up[0]
    down_w = expert_down[0]
    basis = proj_basis[0]
    rank_width = basis.shape[1]
    contract_last = (((1,), (1,)), ((), ()))
    pre_gate = jnp.dot(input_rows, gate_w, preferred_element_type=jnp.float32)
    pre_up = jnp.dot(input_rows, up_w, preferred_element_type=jnp.float32)
    grad_hidden = lax.dot_general(
        grad_rows, down_w, contract_last, preferred_element_type=jnp.float32
    )
    sigma = jax.nn.sigmoid(pre_gate)
    silu_val = pre_gate * sigma
    scaled = gain * grad_hidden
    grad_up = (scaled * silu_val).astype(jnp.bfloat16)
    grad_gate = (scaled * pre_up * sigma * (1.0 + pre_gate * (1.0 - sigma))).astype(jnp.bfloat16)
    hidden = (silu_val * pre_up).astype(jnp.bfloat16)
    part_rows = (
        lax.dot_general(grad_gate, gate_w, contract_last, preferred_element_type=jnp.float32)
        + lax.dot_general(grad_up, up_w, contract_last, preferred_element_type=jnp.float32)
    ).astype(jnp.bfloat16)
    coef_gate = jnp.dot(grad_gate, basis, preferred_element_type=jnp.float32).astype(jnp.bfloat16)
    coef_up = jnp.dot(grad_up, basis, preferred_element_type=jnp.float32).astype(jnp.bfloat16)
    coef_down = (gain * jnp.dot(hidden, basis, preferred_element_type=jnp.float32)).astype(
        jnp.bfloat16
    )
    coef_pair = jnp.concatenate([coef_gate, coef_up], axis=1)
    front = lax.dot_general(
        input_rows, coef_pair, contract_first, preferred_element_type=jnp.float32
    )
    rear = lax.dot_general(grad_rows, coef_down, contract_first, preferred_element_type=jnp.float32)
    summed_terms = lax.psum_scatter(
        jnp.concatenate([front, rear], axis=1).astype(jnp.bfloat16),
        "dp",
        scatter_dimension=0,
        tiled=True,
    ).astype(jnp.float32)
    projected = summed_terms.reshape(1, column_width, 3, rank_width)
    returned = lax.all_to_all(
        part_rows.reshape(expert_count, capacity * model_width),
        "expert",
        split_axis=0,
        concat_axis=0,
        tiled=True,
    )
    spread = jnp.dot(
        token_map, returned.reshape(slot_count, model_width), preferred_element_type=jnp.float32
    )
    token_grad = lax.psum_scatter(
        spread.astype(jnp.bfloat16), "dp", scatter_dimension=1, tiled=True
    )
    return (token_grad, projected)

MESH = pl.DeviceIdType.MESH
LANES = 128
TILE = 256
CONTRACT_LAST = (((1,), (1,)), ((), ()))


def column_chunks(half):
    tiles = half // TILE
    crossed = max(1, tiles // 7)
    straight = tiles - crossed
    sizes = [straight // 3 + (1 if i < straight % 3 else 0) for i in range(3)]
    chunks = []
    for side in range(2):
        start = side * half
        for size in [crossed] + sizes:
            chunks.append((start, size * TILE, start == side * half))
            start += size * TILE
    return chunks


def fused_kernel(
    depth, split, chunks, x_in, y_in, routes, gates, gate_in, up_in, down_in, basis_in,
    grad_out, proj_out,
    x_all, y_all, g_all, gate_w, up_w, down_w, basis, pre_gate, pre_up, grad_gate, grad_up, hidden,
    coef, coef_half, far_coef, coef_t, part, from_core, from_side, from_z, from_zb, from_plane,
    recv_sem, up_sem, down_sem, side_sem, plane_sem, core_sem, local_sem, coef_sem,
    sum_core_sem, sum_side_sem, sum_z_sem, sum_plane_sem,
):
    dp = lax.axis_index("dp")
    me = lax.axis_index("expert")
    z, y, core = me // 4, (me // 2) % 2, me % 2
    rows, width = x_in.shape
    half = width // 2
    hidden_width = gate_w.shape[1]
    rank = basis.shape[1]
    plane_rows = 4 * rows
    core_device = (dp, z * 4 + y * 2 + 1 - core)
    side_device = (dp, z * 4 + (1 - y) * 2 + core)
    plane_device = (1 - dp, me)
    order = [sorted(range(depth), key=lambda q, p=p: (abs(q - p), q)) for p in range(depth)]
    seq = [
        sum(jnp.where(z == p, order[p][i], 0) for p in range(depth)) for i in range(depth)
    ]

    own_cols = pl.ds(pl.multiple_of(dp * split, LANES), split)
    far_cols = pl.ds(pl.multiple_of((1 - dp) * split, LANES), split)
    rest_cols = pl.ds(2 * split, width - 2 * split)
    all_cols = pl.ds(0, g_all.shape[1])
    pieces = (
        (x_in, x_all, own_cols), (y_in, y_all, own_cols),
        (x_in, x_all, rest_cols), (y_in, y_all, rest_cols),
        (None, g_all, all_cols),
        (x_in, x_all, far_cols), (y_in, y_all, far_cols),
    )
    planar = range(5)

    def index(zz, yy, cc):
        return zz * 4 + yy * 2 + cc

    def item_rows(item):
        return pl.ds(pl.multiple_of(item * rows, rows), rows)

    def landed(piece, item):
        _, whole, cols = pieces[piece]
        return whole.at[item_rows(item), cols]

    def copy(piece, item, own, sem, device, recv_piece):
        start, _, cols = pieces[piece]
        src = start.at[:, cols] if own and start is not None else landed(piece, item)
        return pltpu.make_async_remote_copy(
            src_ref=src,
            dst_ref=landed(piece, item),
            send_sem=sem,
            recv_sem=recv_sem.at[recv_piece, item],
            device_id=device,
            device_id_type=MESH,
        )

    def up(piece, zz, own=False):
        return copy(piece, index(zz, y, core), own, up_sem.at[piece, zz], (dp, me + 4), piece)

    def down(piece, zz, own=False):
        return copy(piece, index(zz, y, core), own, down_sem.at[piece, zz], (dp, me - 4), piece)

    def side(piece, zz, own=False):
        return copy(piece, index(zz, y, core), own, side_sem.at[piece, zz], side_device, piece)

    def plane(piece, zz, yy):
        item = index(zz, yy, core)
        return copy(piece, item, False, plane_sem.at[piece, item // 2], plane_device, piece + 5)

    def other(piece, zz, yy, own=False):
        item = index(zz, yy, core)
        return copy(piece, item, own, core_sem.at[piece, item // 2], core_device, piece)

    def arrive(piece, item):
        copy(piece, item, False, core_sem.at[0, 0], (dp, me), piece).wait_recv()

    lane = lax.broadcasted_iota(jnp.int32, (rows, LANES), 1)
    table = jnp.zeros((rows, LANES), jnp.float32)
    for k in range(routes.shape[1]):
        table = table + jnp.where(
            routes[:, k : k + 1] == lane, gates[:, k : k + 1].astype(jnp.float32), 0.0
        )
    g_all[item_rows(me), :] = table.astype(jnp.bfloat16)

    barrier = pltpu.get_barrier_semaphore()

    def greet(device):
        pl.semaphore_signal(barrier, inc=1, device_id=device, device_id_type=MESH)

    greet(plane_device)
    greet(side_device)
    greet(core_device)
    pl.when(z > 0)(lambda: greet((dp, me - 4)))
    pl.when(z < depth - 1)(lambda: greet((dp, me + 4)))
    pl.semaphore_wait(barrier, 3 + jnp.minimum(z, 1) + jnp.minimum(depth - 1 - z, 1))

    for piece in planar:
        side(piece, z, True).start()
        pl.when(z < depth - 1)(lambda piece=piece: up(piece, z, True).start())
        pl.when(z > 0)(lambda piece=piece: down(piece, z, True).start())
    for piece in range(7):
        other(piece, z, y, True).start()
    own_loads = [
        pltpu.make_async_copy(a, b, local_sem.at[i])
        for i, (a, b) in enumerate((
            (x_in, x_all.at[item_rows(me), :]), (y_in, y_all.at[item_rows(me), :]),
            (gate_in, gate_w), (up_in, up_w), (down_in, down_w), (basis_in, basis),
        ))
    ]
    for one in own_loads:
        one.start()

    def spots(away):
        if away == 0:
            return [(z, None)]
        return [(z - away, z >= away), (z + away, z + away < depth)]

    def guarded(condition, act):
        act() if condition is None else pl.when(condition)(act)

    def along_z(piece, zz, from_below):
        def act():
            arrive(piece, index(zz, y, core))
            side(piece, zz).start()
            if from_below:
                pl.when(z < depth - 1)(lambda: up(piece, zz).start())
            else:
                pl.when(z > 0)(lambda: down(piece, zz).start())
            if piece < 2:
                plane(piece, zz, y).start()
            other(piece, zz, y).start()
        return act

    def from_side_of(piece, zz):
        def act():
            arrive(piece, index(zz, 1 - y, core))
            if piece < 2:
                plane(piece, zz, 1 - y).start()
            other(piece, zz, 1 - y).start()
        return act

    def from_plane_of(piece, zz, yy):
        def act():
            arrive(piece, index(zz, yy, core))
            other(piece, zz, yy).start()
        return act

    def from_core_of(piece, zz):
        def act():
            arrive(piece, index(zz, 0, 1 - core))
            arrive(piece, index(zz, 1, 1 - core))
        return act

    def rows_of(zz):
        return pl.ds(pl.multiple_of(zz * plane_rows, plane_rows), plane_rows)

    def coef_copy(i):
        return pltpu.make_async_remote_copy(
            src_ref=coef_half.at[rows_of(seq[i]), :],
            dst_ref=far_coef.at[rows_of(seq[i]), :],
            send_sem=coef_sem.at[0, i],
            recv_sem=coef_sem.at[1, i],
            device_id=plane_device,
            device_id_type=MESH,
        )

    def inner_forward(i):
        at = rows_of(seq[i])

        @pl.loop(0, hidden_width // TILE)
        def _(n):
            cols = pl.ds(pl.multiple_of(n * TILE, TILE), TILE)
            pre_gate[:, cols] = jnp.dot(
                x_all[at, :], gate_w[:, cols], preferred_element_type=jnp.float32
            )
            pre_up[:, cols] = jnp.dot(
                x_all[at, :], up_w[:, cols], preferred_element_type=jnp.float32
            )

    def inner_backward(i):
        at = rows_of(seq[i])
        expert = lax.broadcasted_iota(jnp.int32, (plane_rows, LANES), 1)
        gain = jnp.sum(
            jnp.where(expert == me, g_all[at, :].astype(jnp.float32), 0.0), axis=1, keepdims=True
        )

        @pl.loop(0, hidden_width // TILE)
        def _(n):
            cols = pl.ds(pl.multiple_of(n * TILE, TILE), TILE)
            grad_hidden = lax.dot_general(
                y_all[at, :], down_w[cols, :], CONTRACT_LAST, preferred_element_type=jnp.float32
            )
            a = pre_gate[:, cols]
            u = pre_up[:, cols]
            sigma = jax.nn.sigmoid(a)
            silu = a * sigma
            scaled = gain * grad_hidden
            grad_up[at, cols] = (scaled * silu).astype(jnp.bfloat16)
            grad_gate[at, cols] = (scaled * u * sigma * (1.0 + a * (1.0 - sigma))).astype(
                jnp.bfloat16
            )
            hidden[:, cols] = (silu * u).astype(jnp.bfloat16)

        low = jnp.dot(grad_gate[at, :], basis[...], preferred_element_type=jnp.float32)
        mid = jnp.dot(grad_up[at, :], basis[...], preferred_element_type=jnp.float32)
        top = gain * jnp.dot(hidden[...], basis[...], preferred_element_type=jnp.float32)
        for j, value in enumerate((low, mid, top)):
            coef[at, j * rank : (j + 1) * rank] = value
            coef_half[at, j * rank : (j + 1) * rank] = value.astype(jnp.bfloat16)
        coef_copy(i).start()

    pending = []

    def work():
        if pending:
            pending.pop(0)()

    for step in range(1, depth + 2):
        for piece in planar:
            if step < depth:
                for below, (zz, there) in zip((True, False), spots(step)):
                    guarded(there, along_z(piece, zz, below))
            if step <= depth:
                for zz, there in spots(step - 1):
                    guarded(there, from_side_of(piece, zz))
            work()
        if step == 1:
            for one in own_loads:
                one.wait()
        last = step == depth + 1
        for piece in (5, 6):
            if 1 <= step - 1 < depth:
                for zz, there in spots(step - 1):
                    guarded(there, from_plane_of(piece, zz, y))
            if step >= 2:
                for zz, there in spots(step - 2):
                    guarded(there, from_plane_of(piece, zz, 1 - y))
            if last:
                for each in ((0, 2, 5) if piece == 5 else (1, 3, 4, 6)):
                    for zz, there in spots(step - 2):
                        guarded(there, from_core_of(each, zz))
                while pending:
                    work()
                (inner_forward if piece == 5 else inner_backward)(step - 2)
        if step >= 2 and not last:
            for each in range(7):
                for zz, there in spots(step - 2):
                    guarded(there, from_core_of(each, zz))
            pending.append(lambda i=step - 2: inner_forward(i))
            pending.append(lambda i=step - 2: inner_backward(i))

    def remote(src, dst, send, recv, device):
        return pltpu.make_async_remote_copy(
            src_ref=src, dst_ref=dst, send_sem=send, recv_sem=recv,
            device_id=device, device_id_type=MESH,
        )

    crossed = [k for k, chunk in enumerate(chunks) if chunk[2]]

    def cols_of(k):
        return pl.ds(chunks[k][0], chunks[k][1])

    def sum_core_copy(k):
        return remote(
            part.at[:, 1 - core, :, cols_of(k)], from_core.at[:, :, cols_of(k)],
            sum_core_sem.at[0, k], sum_core_sem.at[1, k], core_device,
        )

    def sum_side_copy(k, zz):
        return remote(
            part.at[zz * 2 + 1 - y, core, :, cols_of(k)], from_side.at[zz, :, cols_of(k)],
            sum_side_sem.at[0, k, zz], sum_side_sem.at[1, k, zz], side_device,
        )

    def sum_z_copy(k, zz, upward, flipped=False):
        way = 0 if upward else 1
        if flipped:
            number = crossed.index(k)
            landing = from_zb.at[way, zz, :, pl.ds(number * chunks[k][1], chunks[k][1])]
            number += len(chunks)
        else:
            number = k
            landing = from_z.at[way, zz, :, cols_of(k)]
        slot = zz * 2 + (1 - y if flipped else y)
        return remote(
            part.at[slot, core, :, cols_of(k)], landing,
            sum_z_sem.at[0, way, number, zz], sum_z_sem.at[1, way, number, zz],
            (dp, me + 4 if upward else me - 4),
        )

    def sum_plane_copy(k):
        start, size, _ = chunks[k]
        return remote(
            part.at[z * 2 + y, core, :, cols_of(k)], from_plane.at[:, pl.ds(start % half, size)],
            sum_plane_sem.at[0, k], sum_plane_sem.at[1, k], plane_device,
        )

    def add_into(slot, k, term):
        total = part[slot, core, :, cols_of(k)].astype(jnp.float32) + term.astype(jnp.float32)
        part[slot, core, :, cols_of(k)] = total.astype(jnp.bfloat16)

    def multiply(k):
        start, size, _ = chunks[k]

        @pl.loop(0, depth)
        def _(zz):
            at = rows_of(zz)
            for first in range(start, start + size, TILE):
                cols = pl.ds(first, TILE)
                rows_out = lax.dot_general(
                    grad_gate[at, :], gate_w[cols, :], CONTRACT_LAST,
                    preferred_element_type=jnp.float32,
                ) + lax.dot_general(
                    grad_up[at, :], up_w[cols, :], CONTRACT_LAST,
                    preferred_element_type=jnp.float32,
                )
                part[pl.ds(zz * 2, 2), :, :, cols] = rows_out.astype(jnp.bfloat16).reshape(
                    2, 2, rows, TILE
                )

        sum_core_copy(k).start()

    def over_cores(k):
        sum_core_copy(k).wait_recv()
        for zz in seq[::-1]:
            slot = zz * 2 + 1 - y
            add_into(slot, k, from_core[slot, :, cols_of(k)])
            if not chunks[k][2]:
                sum_side_copy(k, zz).start()
        for i, zz in reversed(list(enumerate(seq))):
            slot = zz * 2 + y
            add_into(slot, k, from_core[slot, :, cols_of(k)])
        if chunks[k][2]:
            for flipped in (True, False):
                for zz in reversed(range(1, depth)):
                    pl.when(z == 0)(
                        lambda zz=zz, f=flipped: sum_z_copy(k, zz, True, f).start()
                    )
                for zz in range(depth - 1):
                    pl.when(z == depth - 1)(
                        lambda zz=zz, f=flipped: sum_z_copy(k, zz, False, f).start()
                    )

    def z_term(k, zz, upward, flipped):
        sum_z_copy(k, zz, upward, flipped).wait_recv()
        if flipped:
            size = chunks[k][1]
            at = pl.ds(crossed.index(k) * size, size)
            term = from_zb[0 if upward else 1, zz, :, at]
        else:
            term = from_z[0 if upward else 1, zz, :, cols_of(k)]
        add_into(zz * 2 + (1 - y if flipped else y), k, term)

    def pass_on(k, flipped=False):
        for far in reversed(range(1, depth)):
            def rise(zz=far):
                z_term(k, zz, True, flipped)
                sum_z_copy(k, zz, True, flipped).start()

            def fall(zz=depth - 1 - far):
                z_term(k, zz, False, flipped)
                sum_z_copy(k, zz, False, flipped).start()

            pl.when((z > 0) & (z < far))(rise)
            pl.when((z < depth - 1) & (z > depth - 1 - far))(fall)

    def own_plane(k, flipped=False):
        pl.when(z > 0)(lambda: z_term(k, z, True, flipped))
        pl.when(z < depth - 1)(lambda: z_term(k, z, False, flipped))

    def over_side(k):
        for zz in seq[::-1]:
            sum_side_copy(k, zz).wait_recv()
            add_into(zz * 2 + y, k, from_side[zz, :, cols_of(k)])
            pl.when((z == 0) & (zz > 0))(lambda zz=zz: sum_z_copy(k, zz, True).start())
            pl.when((z == depth - 1) & (zz < z))(lambda zz=zz: sum_z_copy(k, zz, False).start())

    def leave(k):
        pl.when(dp != chunks[k][0] // half)(lambda: sum_plane_copy(k).start())

    def finish(k):
        own_plane(k)
        leave(k)

    def crossed_z(k):
        for flipped in (True, False):
            pass_on(k, flipped)
        own_plane(k, True)
        sum_side_copy(k, z).start()
        own_plane(k, False)

    def crossed_side(k):
        sum_side_copy(k, z).wait_recv()
        add_into(z * 2 + y, k, from_side[z, :, cols_of(k)])
        leave(k)

    def turn_coef():
        for i in range(depth):
            coef_copy(i).wait_recv()
        coef_t[...] = (coef[...] + far_coef[...].astype(jnp.float32)).T.astype(jnp.bfloat16)

    def project():
        @pl.loop(0, half // TILE)
        def _(n):
            cols = pl.ds(pl.multiple_of(dp * half + n * TILE, TILE), TILE)
            at = pl.ds(pl.multiple_of(n * TILE, TILE), TILE)
            front = jnp.dot(
                coef_t[0 : 2 * rank, :], x_all[:, cols], preferred_element_type=jnp.float32
            ).T
            proj_out[0, at, :] = front[:, 0:rank]
            proj_out[1, at, :] = front[:, rank : 2 * rank]
            proj_out[2, at, :] = jnp.dot(
                coef_t[2 * rank : 3 * rank, :], y_all[:, cols], preferred_element_type=jnp.float32
            ).T

    per_half = len(chunks) // 2
    straight = [side * per_half + n for n in range(1, per_half) for side in range(2)]
    b0, b1 = crossed
    a0, a1, a2, a3, a4, a5 = straight
    plan = [
        (multiply, a0), (multiply, a1), (over_cores, a0), (multiply, b0), (over_cores, a1),
        (multiply, b1), (over_cores, b0), (over_cores, b1), (multiply, a2), (over_cores, a2),
        (crossed_z, b0), (over_side, a0), (multiply, a3), (crossed_z, b1), (pass_on, a0),
        (over_cores, a3), (over_side, a1), (pass_on, a1), (multiply, a4), (over_cores, a4),
        (multiply, a5), (over_side, a2), (pass_on, a2), (over_cores, a5), (finish, a0),
        (turn_coef, None), (project, None),
        (finish, a1), (over_side, a3), (pass_on, a3), (crossed_side, b0), (crossed_side, b1),
        (finish, a2), (over_side, a4), (pass_on, a4), (finish, a3),
        (over_side, a5), (pass_on, a5), (finish, a4), (finish, a5),
    ]
    for stage, k in plan:
        stage() if k is None else stage(k)

    for k, (start, size, z_first) in enumerate(chunks):
        def take_plane(k=k, start=start, size=size):
            sum_plane_copy(k).wait_recv()
            at = pl.ds(start % half, size)
            total = part[z * 2 + y, core, :, cols_of(k)].astype(jnp.float32) + from_plane[
                :, at
            ].astype(jnp.float32)
            grad_out[:, at] = total.astype(jnp.bfloat16)

        pl.when(dp == start // half)(take_plane)
        pl.when(dp != start // half)(lambda k=k: sum_plane_copy(k).wait_send())
        sum_core_copy(k).wait_send()
        if z_first:
            sum_side_copy(k, z).wait_send()
        for zz in range(depth):
            if not z_first:
                sum_side_copy(k, zz).wait_send()
            for flipped in ((False, True) if z_first else (False,)):
                pl.when(zz > z)(
                    lambda k=k, zz=zz, f=flipped: sum_z_copy(k, zz, True, f).wait_send()
                )
                pl.when(zz < z)(
                    lambda k=k, zz=zz, f=flipped: sum_z_copy(k, zz, False, f).wait_send()
                )

    for i in range(depth):
        coef_copy(i).wait_send()
    for piece in planar:
        for zz in range(depth):
            pl.when((zz <= z) & (z < depth - 1))(lambda p=piece, q=zz: up(p, q).wait_send())
            pl.when((zz >= z) & (z > 0))(lambda p=piece, q=zz: down(p, q).wait_send())
            side(piece, zz).wait_send()
    for piece in range(2):
        for pair in range(2 * depth):
            pl.when(pair != me // 2)(
                lambda p=piece, q=pair: plane(p, q // 2, q % 2).wait_send()
            )
    for piece in range(7):
        for pair in range(2 * depth):
            other(piece, pair // 2, pair % 2).wait_send()


def dense_form(
    saved_inputs, output_grad, routes, route_gates, expert_gate, expert_up, expert_down, proj_basis
):
    expert_count = lax.axis_size("expert")
    group_count = lax.axis_size("dp")
    rows, width = saved_inputs.shape
    all_rows = rows * expert_count
    hidden_width = expert_gate.shape[2]
    rank = proj_basis.shape[2]
    depth = expert_count // 4
    half = width // group_count
    split = width * 5 // 14 // LANES * LANES
    chunks = column_chunks(half)
    crossed_width = sum(size for _, size, z_first in chunks if z_first)
    dma = pltpu.SemaphoreType.DMA
    bf16, f32 = jnp.bfloat16, jnp.float32
    whole = pl.BlockSpec(memory_space=pl.ANY)
    held = pl.BlockSpec(memory_space=pltpu.VMEM)
    token_grad, terms = pl.pallas_call(
        functools.partial(fused_kernel, depth, split, chunks),
        out_shape=[
            jax.ShapeDtypeStruct((rows, half), bf16),
            jax.ShapeDtypeStruct((3, half, rank), f32),
        ],
        in_specs=[whole, whole, held, held, whole, whole, whole, whole],
        out_specs=[held] * 2,
        scratch_shapes=[
            pltpu.VMEM((all_rows, width), bf16),
            pltpu.VMEM((all_rows, width), bf16),
            pltpu.VMEM((all_rows, LANES), bf16),
            pltpu.VMEM((width, hidden_width), bf16),
            pltpu.VMEM((width, hidden_width), bf16),
            pltpu.VMEM((hidden_width, width), bf16),
            pltpu.VMEM((hidden_width, rank), bf16),
            pltpu.VMEM((4 * rows, hidden_width), f32),
            pltpu.VMEM((4 * rows, hidden_width), f32),
            pltpu.VMEM((all_rows, hidden_width), bf16),
            pltpu.VMEM((all_rows, hidden_width), bf16),
            pltpu.VMEM((4 * rows, hidden_width), bf16),
            pltpu.VMEM((all_rows, 3 * rank), f32),
            pltpu.VMEM((all_rows, 3 * rank), bf16),
            pltpu.VMEM((all_rows, 3 * rank), bf16),
            pltpu.VMEM((3 * rank, all_rows), bf16),
            pltpu.VMEM((2 * depth, 2, rows, width), bf16),
            pltpu.VMEM((2 * depth, rows, width), bf16),
            pltpu.VMEM((depth, rows, width), bf16),
            pltpu.VMEM((2, depth, rows, width), bf16),
            pltpu.VMEM((2, depth, rows, crossed_width), bf16),
            pltpu.VMEM((rows, half), bf16),
            dma((7, expert_count)),
            dma((5, depth)),
            dma((5, depth)),
            dma((5, depth)),
            dma((2, 2 * depth)),
            dma((7, 2 * depth)),
            dma((6,)),
            dma((2, depth)),
            dma((2, len(chunks))),
            dma((2, len(chunks), depth)),
            dma((2, 2, len(chunks) + 2, depth)),
            dma((2, len(chunks))),
        ],
        compiler_params=pltpu.CompilerParams(
            collective_id=0, has_side_effects=True, vmem_limit_bytes=60 * 1024 * 1024
        ),
    )(
        saved_inputs, output_grad, routes, route_gates,
        expert_gate[0], expert_up[0], expert_down[0], proj_basis[0],
    )
    return (token_grad, terms.transpose(1, 0, 2)[None])


def on_device(*arrays):
    if lax.axis_size("expert") <= 2 * arrays[2].shape[1]:
        return dense_form(*arrays)
    return slot_form(*arrays)


def solution(mesh):
    placed = (
        P("expert", None),
        P("expert", None),
        P("expert", None),
        P("expert", None),
        P("expert", None, "dp"),
        P("expert", None, "dp"),
        P("expert", "dp", None),
        P("expert", "dp", None),
    )
    return jax.shard_map(
        on_device,
        mesh=mesh,
        in_specs=placed,
        out_specs=(P("expert", "dp"), P("expert", "dp", None, None)),
        check_vma=False,
    )
```

```python
import functools

import jax
import jax.numpy as jnp
from jax import lax
from jax.experimental import pallas as pl
from jax.experimental.pallas import tpu as pltpu
from jax.sharding import PartitionSpec as P


def slot_form(
    saved_inputs, output_grad, routes, route_gates, expert_gate, expert_up, expert_down, proj_basis
):
    token_count, model_width = saved_inputs.shape
    top_count = routes.shape[1]
    expert_count = lax.axis_size("expert")
    group_count = lax.axis_size("dp")
    capacity = token_count * top_count * 9 // (8 * expert_count)
    slot_count = expert_count * capacity
    column_width = model_width // group_count
    route_count = token_count * top_count
    flat_routes = routes.reshape(-1)
    position = jnp.arange(route_count, dtype=jnp.int32)
    earlier = jnp.sum(
        (
            (flat_routes[:, None] == flat_routes[None, :])
            & (position[None, :] < position[:, None])
        ).astype(jnp.int32),
        axis=1,
    )
    target_slot = flat_routes * capacity + earlier
    slot_owner = (
        jnp.full((slot_count,), route_count, jnp.int32)
        .at[target_slot]
        .set(jnp.arange(route_count, dtype=jnp.int32))
    )
    filled = slot_owner < route_count
    safe_route = jnp.minimum(slot_owner, route_count - 1)
    source_token = safe_route // top_count
    zero_half = jnp.zeros((), jnp.bfloat16)
    gate_slots = jnp.where(filled, route_gates.reshape(-1)[safe_route], zero_half).reshape(
        expert_count, capacity
    )
    token_map = (
        (source_token[None, :] == jnp.arange(token_count, dtype=jnp.int32)[:, None])
        & filled[None, :]
    ).astype(jnp.bfloat16)
    contract_first = (((0,), (0,)), ((), ()))

    def to_slots(source_rows):
        picked = lax.dot_general(
            token_map, source_rows, contract_first, preferred_element_type=jnp.float32
        ).astype(jnp.bfloat16)
        return picked.reshape(expert_count, capacity * source_rows.shape[1])

    recv_inputs, recv_grads, recv_gates = (
        lax.all_to_all(to_slots(saved_inputs), "expert", split_axis=0, concat_axis=0, tiled=True),
        lax.all_to_all(to_slots(output_grad), "expert", split_axis=0, concat_axis=0, tiled=True),
        lax.all_to_all(gate_slots, "expert", split_axis=0, concat_axis=0, tiled=True),
    )
    input_rows = recv_inputs.reshape(slot_count, model_width)
    grad_rows = recv_grads.reshape(slot_count, model_width)
    gain = recv_gates.reshape(slot_count, 1).astype(jnp.float32)
    gate_w = expert_gate[0]
    up_w = expert_up[0]
    down_w = expert_down[0]
    basis = proj_basis[0]
    rank_width = basis.shape[1]
    contract_last = (((1,), (1,)), ((), ()))
    pre_gate = jnp.dot(input_rows, gate_w, preferred_element_type=jnp.float32)
    pre_up = jnp.dot(input_rows, up_w, preferred_element_type=jnp.float32)
    grad_hidden = lax.dot_general(
        grad_rows, down_w, contract_last, preferred_element_type=jnp.float32
    )
    sigma = jax.nn.sigmoid(pre_gate)
    silu_val = pre_gate * sigma
    scaled = gain * grad_hidden
    grad_up = (scaled * silu_val).astype(jnp.bfloat16)
    grad_gate = (scaled * pre_up * sigma * (1.0 + pre_gate * (1.0 - sigma))).astype(jnp.bfloat16)
    hidden = (silu_val * pre_up).astype(jnp.bfloat16)
    part_rows = (
        lax.dot_general(grad_gate, gate_w, contract_last, preferred_element_type=jnp.float32)
        + lax.dot_general(grad_up, up_w, contract_last, preferred_element_type=jnp.float32)
    ).astype(jnp.bfloat16)
    coef_gate = jnp.dot(grad_gate, basis, preferred_element_type=jnp.float32).astype(jnp.bfloat16)
    coef_up = jnp.dot(grad_up, basis, preferred_element_type=jnp.float32).astype(jnp.bfloat16)
    coef_down = (gain * jnp.dot(hidden, basis, preferred_element_type=jnp.float32)).astype(
        jnp.bfloat16
    )
    coef_pair = jnp.concatenate([coef_gate, coef_up], axis=1)
    front = lax.dot_general(
        input_rows, coef_pair, contract_first, preferred_element_type=jnp.float32
    )
    rear = lax.dot_general(grad_rows, coef_down, contract_first, preferred_element_type=jnp.float32)
    summed_terms = lax.psum_scatter(
        jnp.concatenate([front, rear], axis=1).astype(jnp.bfloat16),
        "dp",
        scatter_dimension=0,
        tiled=True,
    ).astype(jnp.float32)
    projected = summed_terms.reshape(1, column_width, 3, rank_width)
    returned = lax.all_to_all(
        part_rows.reshape(expert_count, capacity * model_width),
        "expert",
        split_axis=0,
        concat_axis=0,
        tiled=True,
    )
    spread = jnp.dot(
        token_map, returned.reshape(slot_count, model_width), preferred_element_type=jnp.float32
    )
    token_grad = lax.psum_scatter(
        spread.astype(jnp.bfloat16), "dp", scatter_dimension=1, tiled=True
    )
    return (token_grad, projected)

MESH = pl.DeviceIdType.MESH
LANES = 128
TILE = 256
CONTRACT_LAST = (((1,), (1,)), ((), ()))


def column_chunks(half):
    tiles = half // TILE
    crossed = max(1, tiles // 7)
    straight = tiles - crossed
    sizes = [straight // 3 + (1 if i < straight % 3 else 0) for i in range(3)]
    chunks = []
    for side in range(2):
        start = side * half
        for size in [crossed] + sizes:
            chunks.append((start, size * TILE, start == side * half))
            start += size * TILE
    return chunks

PLAN = (
    ("mm", 2), ("mm", 4), ("mm", 0), ("co", 2), ("co", 4), ("mm", 3), ("mm", 7), ("co", 3),
    ("co", 0), ("sd", 2, 3), ("mm", 6), ("co", 7), ("mm", 1), ("sd", 2, 2), ("sd", 3, 3),
    ("bz", 0, 1, False), ("bz", 4, 1, True), ("sd", 2, 1), ("bz", 0, 1, True), ("mm", 5),
    ("sd", 3, 2), ("pz", 2, 1), ("sd", 3, 1), ("sd", 7, 3), ("co", 1), ("bz", 4, 1, False),
    ("co", 6), ("sd", 7, 2), ("tc",), ("bz", 0, 2, False), ("bz", 4, 2, True), ("pz", 3, 1),
    ("bz", 0, 2, True), ("sd", 1, 3), ("pj",), ("sd", 1, 2), ("sd", 7, 1), ("pz", 7, 1),
    ("pz", 2, 2), ("co", 5), ("sd", 6, 3), ("pz", 1, 1), ("bo", 0, False), ("bz", 4, 2, False),
    ("pz", 7, 2), ("sd", 2, 0), ("sd", 7, 0), ("bo", 4, True), ("sd", 6, 2), ("sd", 1, 1),
    ("sd", 3, 0), ("sd", 1, 0), ("fi", 2), ("pz", 6, 1), ("pz", 3, 2), ("sd", 5, 3), ("fi", 7),
    ("pz", 1, 2), ("bo", 0, True), ("sd", 5, 2), ("sd", 6, 1), ("pz", 6, 2), ("fi", 3),
    ("sd", 6, 0), ("fi", 1), ("pz", 5, 1), ("sd", 5, 1), ("pz", 5, 2), ("fi", 6), ("sd", 5, 0),
    ("bo", 4, False), ("bs", 4), ("fi", 5), ("bs", 0),
)

def return_plan(depth, chunks):
    steps = [("tc",), ("pj",)]
    for k, (_, _, z_first) in enumerate(chunks):
        steps += [("mm", k), ("co", k)]
        hops = range(1, depth - 1)
        if z_first:
            steps += [("bz", k, hop, flipped) for flipped in (True, False) for hop in hops]
            steps += [("bo", k, True), ("bo", k, False), ("bs", k)]
        else:
            steps += [("sd", k, i) for i in reversed(range(depth))]
            steps += [("pz", k, hop) for hop in hops] + [("fi", k)]
    return PLAN if sorted(map(str, PLAN)) == sorted(map(str, steps)) else steps


def fused_kernel(
    depth, split, chunks, plan, x_in, y_in, routes, gates, gate_in, up_in, down_in, basis_in,
    grad_out, proj_out,
    x_all, y_all, g_all, gate_w, up_w, down_w, basis, pre_gate, pre_up, grad_gate, grad_up, hidden,
    coef, coef_half, far_coef, coef_t, part, from_core, from_side, from_z, from_zb, from_plane,
    recv_sem, up_sem, down_sem, side_sem, plane_sem, core_sem, local_sem, coef_sem,
    sum_core_sem, sum_side_sem, sum_z_sem, sum_plane_sem,
):
    dp = lax.axis_index("dp")
    me = lax.axis_index("expert")
    z, y, core = me // 4, (me // 2) % 2, me % 2
    rows, width = x_in.shape
    half = width // 2
    hidden_width = gate_w.shape[1]
    rank = basis.shape[1]
    plane_rows = 4 * rows
    core_device = (dp, z * 4 + y * 2 + 1 - core)
    side_device = (dp, z * 4 + (1 - y) * 2 + core)
    plane_device = (1 - dp, me)
    order = [
        sorted(range(depth), key=lambda q, p=p: (abs(q - p), q if 2 * p < depth else -q))
        for p in range(depth)
    ]
    seq = [
        sum(jnp.where(z == p, order[p][i], 0) for p in range(depth)) for i in range(depth)
    ]

    own_cols = pl.ds(pl.multiple_of(dp * split, LANES), split)
    far_cols = pl.ds(pl.multiple_of((1 - dp) * split, LANES), split)
    rest_cols = pl.ds(2 * split, width - 2 * split)
    all_cols = pl.ds(0, g_all.shape[1])
    pieces = (
        (x_in, x_all, own_cols), (y_in, y_all, own_cols),
        (x_in, x_all, rest_cols), (y_in, y_all, rest_cols),
        (None, g_all, all_cols),
        (x_in, x_all, far_cols), (y_in, y_all, far_cols),
    )
    planar = range(5)

    def index(zz, yy, cc):
        return zz * 4 + yy * 2 + cc

    def item_rows(item):
        return pl.ds(pl.multiple_of(item * rows, rows), rows)

    def landed(piece, item):
        _, whole, cols = pieces[piece]
        return whole.at[item_rows(item), cols]

    def copy(piece, item, own, sem, device, recv_piece):
        start, _, cols = pieces[piece]
        src = start.at[:, cols] if own and start is not None else landed(piece, item)
        return pltpu.make_async_remote_copy(
            src_ref=src,
            dst_ref=landed(piece, item),
            send_sem=sem,
            recv_sem=recv_sem.at[recv_piece, item],
            device_id=device,
            device_id_type=MESH,
        )

    def up(piece, zz, own=False):
        return copy(piece, index(zz, y, core), own, up_sem.at[piece, zz], (dp, me + 4), piece)

    def down(piece, zz, own=False):
        return copy(piece, index(zz, y, core), own, down_sem.at[piece, zz], (dp, me - 4), piece)

    def side(piece, zz, own=False):
        return copy(piece, index(zz, y, core), own, side_sem.at[piece, zz], side_device, piece)

    def plane(piece, zz, yy):
        item = index(zz, yy, core)
        return copy(piece, item, False, plane_sem.at[piece, item // 2], plane_device, piece + 5)

    def other(piece, zz, yy, own=False):
        item = index(zz, yy, core)
        return copy(piece, item, own, core_sem.at[piece, item // 2], core_device, piece)

    def arrive(piece, item):
        copy(piece, item, False, core_sem.at[0, 0], (dp, me), piece).wait_recv()

    lane = lax.broadcasted_iota(jnp.int32, (rows, LANES), 1)
    table = jnp.zeros((rows, LANES), jnp.float32)
    for k in range(routes.shape[1]):
        table = table + jnp.where(
            routes[:, k : k + 1] == lane, gates[:, k : k + 1].astype(jnp.float32), 0.0
        )
    g_all[item_rows(me), :] = table.astype(jnp.bfloat16)

    barrier = pltpu.get_barrier_semaphore()

    def greet(device):
        pl.semaphore_signal(barrier, inc=1, device_id=device, device_id_type=MESH)

    greet(plane_device)
    greet(side_device)
    greet(core_device)
    pl.when(z > 0)(lambda: greet((dp, me - 4)))
    pl.when(z < depth - 1)(lambda: greet((dp, me + 4)))
    pl.semaphore_wait(barrier, 3 + jnp.minimum(z, 1) + jnp.minimum(depth - 1 - z, 1))

    for piece in planar:
        side(piece, z, True).start()
        pl.when(z < depth - 1)(lambda piece=piece: up(piece, z, True).start())
        pl.when(z > 0)(lambda piece=piece: down(piece, z, True).start())
    for piece in range(7):
        other(piece, z, y, True).start()
    own_loads = [
        pltpu.make_async_copy(a, b, local_sem.at[i])
        for i, (a, b) in enumerate((
            (x_in, x_all.at[item_rows(me), :]), (y_in, y_all.at[item_rows(me), :]),
            (gate_in, gate_w), (up_in, up_w), (down_in, down_w), (basis_in, basis),
        ))
    ]
    for one in own_loads:
        one.start()

    def spots(away):
        if away == 0:
            return [(z, None)]
        return [(z - away, z >= away), (z + away, z + away < depth)]

    def guarded(condition, act):
        act() if condition is None else pl.when(condition)(act)

    def along_z(piece, zz, from_below):
        def act():
            arrive(piece, index(zz, y, core))
            side(piece, zz).start()
            if from_below:
                pl.when(z < depth - 1)(lambda: up(piece, zz).start())
            else:
                pl.when(z > 0)(lambda: down(piece, zz).start())
            if piece < 2:
                plane(piece, zz, y).start()
            other(piece, zz, y).start()
        return act

    def from_side_of(piece, zz):
        def act():
            arrive(piece, index(zz, 1 - y, core))
            if piece < 2:
                plane(piece, zz, 1 - y).start()
            other(piece, zz, 1 - y).start()
        return act

    def from_plane_of(piece, zz, yy):
        def act():
            arrive(piece, index(zz, yy, core))
            other(piece, zz, yy).start()
        return act

    def from_core_of(piece, zz):
        def act():
            arrive(piece, index(zz, 0, 1 - core))
            arrive(piece, index(zz, 1, 1 - core))
        return act

    def rows_of(zz):
        return pl.ds(pl.multiple_of(zz * plane_rows, plane_rows), plane_rows)

    def coef_copy(i):
        return pltpu.make_async_remote_copy(
            src_ref=coef_half.at[rows_of(seq[i]), :],
            dst_ref=far_coef.at[rows_of(seq[i]), :],
            send_sem=coef_sem.at[0, i],
            recv_sem=coef_sem.at[1, i],
            device_id=plane_device,
            device_id_type=MESH,
        )

    def inner_forward(i):
        at = rows_of(seq[i])

        @pl.loop(0, hidden_width // TILE)
        def _(n):
            cols = pl.ds(pl.multiple_of(n * TILE, TILE), TILE)
            pre_gate[:, cols] = jnp.dot(
                x_all[at, :], gate_w[:, cols], preferred_element_type=jnp.float32
            )
            pre_up[:, cols] = jnp.dot(
                x_all[at, :], up_w[:, cols], preferred_element_type=jnp.float32
            )

    def inner_backward(i):
        at = rows_of(seq[i])
        expert = lax.broadcasted_iota(jnp.int32, (plane_rows, LANES), 1)
        gain = jnp.sum(
            jnp.where(expert == me, g_all[at, :].astype(jnp.float32), 0.0), axis=1, keepdims=True
        )

        @pl.loop(0, hidden_width // TILE)
        def _(n):
            cols = pl.ds(pl.multiple_of(n * TILE, TILE), TILE)
            grad_hidden = lax.dot_general(
                y_all[at, :], down_w[cols, :], CONTRACT_LAST, preferred_element_type=jnp.float32
            )
            a = pre_gate[:, cols]
            u = pre_up[:, cols]
            sigma = jax.nn.sigmoid(a)
            silu = a * sigma
            scaled = gain * grad_hidden
            grad_up[at, cols] = (scaled * silu).astype(jnp.bfloat16)
            grad_gate[at, cols] = (scaled * u * sigma * (1.0 + a * (1.0 - sigma))).astype(
                jnp.bfloat16
            )
            hidden[:, cols] = (silu * u).astype(jnp.bfloat16)

        low = jnp.dot(grad_gate[at, :], basis[...], preferred_element_type=jnp.float32)
        mid = jnp.dot(grad_up[at, :], basis[...], preferred_element_type=jnp.float32)
        top = gain * jnp.dot(hidden[...], basis[...], preferred_element_type=jnp.float32)
        for j, value in enumerate((low, mid, top)):
            coef[at, j * rank : (j + 1) * rank] = value
            coef_half[at, j * rank : (j + 1) * rank] = value.astype(jnp.bfloat16)

    pending = []

    def work():
        if pending:
            pending.pop(0)()

    for step in range(1, depth + 2):
        for piece in planar:
            if step < depth:
                for below, (zz, there) in zip((True, False), spots(step)):
                    guarded(there, along_z(piece, zz, below))
            if step <= depth:
                for zz, there in spots(step - 1):
                    guarded(there, from_side_of(piece, zz))
            work()
        if step == 1:
            for one in own_loads:
                one.wait()
        last = step == depth + 1
        for piece in (5, 6):
            if 1 <= step - 1 < depth:
                for zz, there in spots(step - 1):
                    guarded(there, from_plane_of(piece, zz, y))
            if step >= 2:
                for zz, there in spots(step - 2):
                    guarded(there, from_plane_of(piece, zz, 1 - y))
            if last:
                for each in ((0, 2, 5) if piece == 5 else (1, 3, 4, 6)):
                    for zz, there in spots(step - 2):
                        guarded(there, from_core_of(each, zz))
                while pending:
                    work()
                (inner_forward if piece == 5 else inner_backward)(step - 2)
        if step >= 2 and not last:
            for each in range(7):
                for zz, there in spots(step - 2):
                    guarded(there, from_core_of(each, zz))
            pending.append(lambda i=step - 2: inner_forward(i))
            pending.append(lambda i=step - 2: inner_backward(i))

    def remote(src, dst, send, recv, device):
        return pltpu.make_async_remote_copy(
            src_ref=src, dst_ref=dst, send_sem=send, recv_sem=recv,
            device_id=device, device_id_type=MESH,
        )

    crossed = [k for k, chunk in enumerate(chunks) if chunk[2]]

    def cols_of(k):
        return pl.ds(chunks[k][0], chunks[k][1])

    def sum_core_copy(k):
        return remote(
            part.at[:, 1 - core, :, cols_of(k)], from_core.at[:, :, cols_of(k)],
            sum_core_sem.at[0, k], sum_core_sem.at[1, k], core_device,
        )

    def sum_side_copy(k, zz):
        return remote(
            part.at[zz * 2 + 1 - y, core, :, cols_of(k)], from_side.at[zz, :, cols_of(k)],
            sum_side_sem.at[0, k, zz], sum_side_sem.at[1, k, zz], side_device,
        )

    def sum_z_copy(k, zz, upward, flipped=False):
        way = 0 if upward else 1
        if flipped:
            number = crossed.index(k)
            landing = from_zb.at[way, zz, :, pl.ds(number * chunks[k][1], chunks[k][1])]
            number += len(chunks)
        else:
            number = k
            landing = from_z.at[way, zz, :, cols_of(k)]
        slot = zz * 2 + (1 - y if flipped else y)
        return remote(
            part.at[slot, core, :, cols_of(k)], landing,
            sum_z_sem.at[0, way, number, zz], sum_z_sem.at[1, way, number, zz],
            (dp, me + 4 if upward else me - 4),
        )

    def sum_plane_copy(k):
        start, size, _ = chunks[k]
        return remote(
            part.at[z * 2 + y, core, :, cols_of(k)], from_plane.at[:, pl.ds(start % half, size)],
            sum_plane_sem.at[0, k], sum_plane_sem.at[1, k], plane_device,
        )

    def add_into(slot, k, term):
        total = part[slot, core, :, cols_of(k)].astype(jnp.float32) + term.astype(jnp.float32)
        part[slot, core, :, cols_of(k)] = total.astype(jnp.bfloat16)

    def multiply(k):
        start, size, _ = chunks[k]

        @pl.loop(0, depth)
        def _(zz):
            at = rows_of(zz)
            for first in range(start, start + size, TILE):
                cols = pl.ds(first, TILE)
                rows_out = lax.dot_general(
                    grad_gate[at, :], gate_w[cols, :], CONTRACT_LAST,
                    preferred_element_type=jnp.float32,
                ) + lax.dot_general(
                    grad_up[at, :], up_w[cols, :], CONTRACT_LAST,
                    preferred_element_type=jnp.float32,
                )
                part[pl.ds(zz * 2, 2), :, :, cols] = rows_out.astype(jnp.bfloat16).reshape(
                    2, 2, rows, TILE
                )

        sum_core_copy(k).start()

    def over_cores(k):
        sum_core_copy(k).wait_recv()
        for zz in seq[::-1]:
            slot = zz * 2 + 1 - y
            add_into(slot, k, from_core[slot, :, cols_of(k)])
            if not chunks[k][2]:
                sum_side_copy(k, zz).start()
        for i, zz in reversed(list(enumerate(seq))):
            slot = zz * 2 + y
            add_into(slot, k, from_core[slot, :, cols_of(k)])
        if chunks[k][2]:
            for flipped in (True, False):
                for zz in reversed(range(1, depth)):
                    pl.when(z == 0)(
                        lambda zz=zz, f=flipped: sum_z_copy(k, zz, True, f).start()
                    )
                for zz in range(depth - 1):
                    pl.when(z == depth - 1)(
                        lambda zz=zz, f=flipped: sum_z_copy(k, zz, False, f).start()
                    )

    def z_term(k, zz, upward, flipped):
        sum_z_copy(k, zz, upward, flipped).wait_recv()
        if flipped:
            size = chunks[k][1]
            at = pl.ds(crossed.index(k) * size, size)
            term = from_zb[0 if upward else 1, zz, :, at]
        else:
            term = from_z[0 if upward else 1, zz, :, cols_of(k)]
        add_into(zz * 2 + (1 - y if flipped else y), k, term)

    def pass_on(k, hop, flipped=False):
        def rise():
            for zz in reversed(range(hop + 1, depth)):
                z_term(k, zz, True, flipped)
                sum_z_copy(k, zz, True, flipped).start()

        def fall():
            for zz in range(depth - 1 - hop):
                z_term(k, zz, False, flipped)
                sum_z_copy(k, zz, False, flipped).start()

        pl.when(z == hop)(rise)
        pl.when(z == depth - 1 - hop)(fall)

    def own_plane(k, flipped=False):
        pl.when(z > 0)(lambda: z_term(k, z, True, flipped))
        pl.when(z < depth - 1)(lambda: z_term(k, z, False, flipped))

    def over_side(k, i):
        zz = seq[i]
        sum_side_copy(k, zz).wait_recv()
        add_into(zz * 2 + y, k, from_side[zz, :, cols_of(k)])
        pl.when((z == 0) & (zz > 0))(lambda: sum_z_copy(k, zz, True).start())
        pl.when((z == depth - 1) & (zz < z))(lambda: sum_z_copy(k, zz, False).start())

    def leave(k):
        pl.when(dp != chunks[k][0] // half)(lambda: sum_plane_copy(k).start())

    def finish(k):
        own_plane(k)
        leave(k)

    def crossed_own(k, flipped):
        own_plane(k, flipped)
        if flipped:
            sum_side_copy(k, z).start()

    def crossed_side(k):
        sum_side_copy(k, z).wait_recv()
        add_into(z * 2 + y, k, from_side[z, :, cols_of(k)])
        leave(k)

    def turn_coef():
        for i in range(depth):
            coef_copy(i).wait_recv()
        coef_t[...] = (coef[...] + far_coef[...].astype(jnp.float32)).T.astype(jnp.bfloat16)

    def project():
        @pl.loop(0, half // TILE)
        def _(n):
            cols = pl.ds(pl.multiple_of(dp * half + n * TILE, TILE), TILE)
            at = pl.ds(pl.multiple_of(n * TILE, TILE), TILE)
            front = jnp.dot(
                coef_t[0 : 2 * rank, :], x_all[:, cols], preferred_element_type=jnp.float32
            ).T
            proj_out[0, at, :] = front[:, 0:rank]
            proj_out[1, at, :] = front[:, rank : 2 * rank]
            proj_out[2, at, :] = jnp.dot(
                coef_t[2 * rank : 3 * rank, :], y_all[:, cols], preferred_element_type=jnp.float32
            ).T

    stages = {
        "mm": multiply, "co": over_cores, "sd": over_side, "pz": pass_on, "fi": finish,
        "bz": pass_on, "bo": crossed_own, "bs": crossed_side, "tc": turn_coef, "pj": project,
    }
    for i in range(depth):
        coef_copy(i).start()
    for stage, *at in plan:
        stages[stage](*at)

    for k, (start, size, z_first) in enumerate(chunks):
        def take_plane(k=k, start=start, size=size):
            sum_plane_copy(k).wait_recv()
            at = pl.ds(start % half, size)
            total = part[z * 2 + y, core, :, cols_of(k)].astype(jnp.float32) + from_plane[
                :, at
            ].astype(jnp.float32)
            grad_out[:, at] = total.astype(jnp.bfloat16)

        pl.when(dp == start // half)(take_plane)
        pl.when(dp != start // half)(lambda k=k: sum_plane_copy(k).wait_send())
        sum_core_copy(k).wait_send()
        if z_first:
            sum_side_copy(k, z).wait_send()
        for zz in range(depth):
            if not z_first:
                sum_side_copy(k, zz).wait_send()
            for flipped in ((False, True) if z_first else (False,)):
                pl.when(zz > z)(
                    lambda k=k, zz=zz, f=flipped: sum_z_copy(k, zz, True, f).wait_send()
                )
                pl.when(zz < z)(
                    lambda k=k, zz=zz, f=flipped: sum_z_copy(k, zz, False, f).wait_send()
                )

    for i in range(depth):
        coef_copy(i).wait_send()
    for piece in planar:
        for zz in range(depth):
            pl.when((zz <= z) & (z < depth - 1))(lambda p=piece, q=zz: up(p, q).wait_send())
            pl.when((zz >= z) & (z > 0))(lambda p=piece, q=zz: down(p, q).wait_send())
            side(piece, zz).wait_send()
    for piece in range(2):
        for pair in range(2 * depth):
            pl.when(pair != me // 2)(
                lambda p=piece, q=pair: plane(p, q // 2, q % 2).wait_send()
            )
    for piece in range(7):
        for pair in range(2 * depth):
            other(piece, pair // 2, pair % 2).wait_send()


def dense_form(
    saved_inputs, output_grad, routes, route_gates, expert_gate, expert_up, expert_down, proj_basis
):
    expert_count = lax.axis_size("expert")
    group_count = lax.axis_size("dp")
    rows, width = saved_inputs.shape
    all_rows = rows * expert_count
    hidden_width = expert_gate.shape[2]
    rank = proj_basis.shape[2]
    depth = expert_count // 4
    half = width // group_count
    split = width * 5 // 14 // LANES * LANES
    chunks = column_chunks(half)
    crossed_width = sum(size for _, size, z_first in chunks if z_first)
    dma = pltpu.SemaphoreType.DMA
    bf16, f32 = jnp.bfloat16, jnp.float32
    whole = pl.BlockSpec(memory_space=pl.ANY)
    held = pl.BlockSpec(memory_space=pltpu.VMEM)
    token_grad, terms = pl.pallas_call(
        functools.partial(fused_kernel, depth, split, chunks, return_plan(depth, chunks)),
        out_shape=[
            jax.ShapeDtypeStruct((rows, half), bf16),
            jax.ShapeDtypeStruct((3, half, rank), f32),
        ],
        in_specs=[whole, whole, held, held, whole, whole, whole, whole],
        out_specs=[held] * 2,
        scratch_shapes=[
            pltpu.VMEM((all_rows, width), bf16),
            pltpu.VMEM((all_rows, width), bf16),
            pltpu.VMEM((all_rows, LANES), bf16),
            pltpu.VMEM((width, hidden_width), bf16),
            pltpu.VMEM((width, hidden_width), bf16),
            pltpu.VMEM((hidden_width, width), bf16),
            pltpu.VMEM((hidden_width, rank), bf16),
            pltpu.VMEM((4 * rows, hidden_width), f32),
            pltpu.VMEM((4 * rows, hidden_width), f32),
            pltpu.VMEM((all_rows, hidden_width), bf16),
            pltpu.VMEM((all_rows, hidden_width), bf16),
            pltpu.VMEM((4 * rows, hidden_width), bf16),
            pltpu.VMEM((all_rows, 3 * rank), f32),
            pltpu.VMEM((all_rows, 3 * rank), bf16),
            pltpu.VMEM((all_rows, 3 * rank), bf16),
            pltpu.VMEM((3 * rank, all_rows), bf16),
            pltpu.VMEM((2 * depth, 2, rows, width), bf16),
            pltpu.VMEM((2 * depth, rows, width), bf16),
            pltpu.VMEM((depth, rows, width), bf16),
            pltpu.VMEM((2, depth, rows, width), bf16),
            pltpu.VMEM((2, depth, rows, crossed_width), bf16),
            pltpu.VMEM((rows, half), bf16),
            dma((7, expert_count)),
            dma((5, depth)),
            dma((5, depth)),
            dma((5, depth)),
            dma((2, 2 * depth)),
            dma((7, 2 * depth)),
            dma((6,)),
            dma((2, depth)),
            dma((2, len(chunks))),
            dma((2, len(chunks), depth)),
            dma((2, 2, len(chunks) + 2, depth)),
            dma((2, len(chunks))),
        ],
        compiler_params=pltpu.CompilerParams(
            collective_id=0, has_side_effects=True, vmem_limit_bytes=60 * 1024 * 1024
        ),
    )(
        saved_inputs, output_grad, routes, route_gates,
        expert_gate[0], expert_up[0], expert_down[0], proj_basis[0],
    )
    return (token_grad, terms.transpose(1, 0, 2)[None])


def on_device(*arrays):
    if lax.axis_size("expert") <= 2 * arrays[2].shape[1]:
        return dense_form(*arrays)
    return slot_form(*arrays)


def solution(mesh):
    placed = (
        P("expert", None),
        P("expert", None),
        P("expert", None),
        P("expert", None),
        P("expert", None, "dp"),
        P("expert", None, "dp"),
        P("expert", "dp", None),
        P("expert", "dp", None),
    )
    return jax.shard_map(
        on_device,
        mesh=mesh,
        in_specs=placed,
        out_specs=(P("expert", "dp"), P("expert", "dp", None, None)),
        check_vma=False,
    )
```

```python
import functools

import jax
import jax.numpy as jnp
from jax import lax
from jax.experimental import pallas as pl
from jax.experimental.pallas import tpu as pltpu
from jax.sharding import PartitionSpec as P


def slot_form(
    saved_inputs, output_grad, routes, route_gates, expert_gate, expert_up, expert_down, proj_basis
):
    token_count, model_width = saved_inputs.shape
    top_count = routes.shape[1]
    expert_count = lax.axis_size("expert")
    group_count = lax.axis_size("dp")
    capacity = token_count * top_count * 9 // (8 * expert_count)
    slot_count = expert_count * capacity
    column_width = model_width // group_count
    route_count = token_count * top_count
    flat_routes = routes.reshape(-1)
    position = jnp.arange(route_count, dtype=jnp.int32)
    earlier = jnp.sum(
        (
            (flat_routes[:, None] == flat_routes[None, :])
            & (position[None, :] < position[:, None])
        ).astype(jnp.int32),
        axis=1,
    )
    target_slot = flat_routes * capacity + earlier
    slot_owner = (
        jnp.full((slot_count,), route_count, jnp.int32)
        .at[target_slot]
        .set(jnp.arange(route_count, dtype=jnp.int32))
    )
    filled = slot_owner < route_count
    safe_route = jnp.minimum(slot_owner, route_count - 1)
    source_token = safe_route // top_count
    zero_half = jnp.zeros((), jnp.bfloat16)
    gate_slots = jnp.where(filled, route_gates.reshape(-1)[safe_route], zero_half).reshape(
        expert_count, capacity
    )
    token_map = (
        (source_token[None, :] == jnp.arange(token_count, dtype=jnp.int32)[:, None])
        & filled[None, :]
    ).astype(jnp.bfloat16)
    contract_first = (((0,), (0,)), ((), ()))

    def to_slots(source_rows):
        picked = lax.dot_general(
            token_map, source_rows, contract_first, preferred_element_type=jnp.float32
        ).astype(jnp.bfloat16)
        return picked.reshape(expert_count, capacity * source_rows.shape[1])

    recv_inputs, recv_grads, recv_gates = (
        lax.all_to_all(to_slots(saved_inputs), "expert", split_axis=0, concat_axis=0, tiled=True),
        lax.all_to_all(to_slots(output_grad), "expert", split_axis=0, concat_axis=0, tiled=True),
        lax.all_to_all(gate_slots, "expert", split_axis=0, concat_axis=0, tiled=True),
    )
    input_rows = recv_inputs.reshape(slot_count, model_width)
    grad_rows = recv_grads.reshape(slot_count, model_width)
    gain = recv_gates.reshape(slot_count, 1).astype(jnp.float32)
    gate_w = expert_gate[0]
    up_w = expert_up[0]
    down_w = expert_down[0]
    basis = proj_basis[0]
    rank_width = basis.shape[1]
    contract_last = (((1,), (1,)), ((), ()))
    pre_gate = jnp.dot(input_rows, gate_w, preferred_element_type=jnp.float32)
    pre_up = jnp.dot(input_rows, up_w, preferred_element_type=jnp.float32)
    grad_hidden = lax.dot_general(
        grad_rows, down_w, contract_last, preferred_element_type=jnp.float32
    )
    sigma = jax.nn.sigmoid(pre_gate)
    silu_val = pre_gate * sigma
    scaled = gain * grad_hidden
    grad_up = (scaled * silu_val).astype(jnp.bfloat16)
    grad_gate = (scaled * pre_up * sigma * (1.0 + pre_gate * (1.0 - sigma))).astype(jnp.bfloat16)
    hidden = (silu_val * pre_up).astype(jnp.bfloat16)
    part_rows = (
        lax.dot_general(grad_gate, gate_w, contract_last, preferred_element_type=jnp.float32)
        + lax.dot_general(grad_up, up_w, contract_last, preferred_element_type=jnp.float32)
    ).astype(jnp.bfloat16)
    coef_gate = jnp.dot(grad_gate, basis, preferred_element_type=jnp.float32).astype(jnp.bfloat16)
    coef_up = jnp.dot(grad_up, basis, preferred_element_type=jnp.float32).astype(jnp.bfloat16)
    coef_down = (gain * jnp.dot(hidden, basis, preferred_element_type=jnp.float32)).astype(
        jnp.bfloat16
    )
    coef_pair = jnp.concatenate([coef_gate, coef_up], axis=1)
    front = lax.dot_general(
        input_rows, coef_pair, contract_first, preferred_element_type=jnp.float32
    )
    rear = lax.dot_general(grad_rows, coef_down, contract_first, preferred_element_type=jnp.float32)
    summed_terms = lax.psum_scatter(
        jnp.concatenate([front, rear], axis=1).astype(jnp.bfloat16),
        "dp",
        scatter_dimension=0,
        tiled=True,
    ).astype(jnp.float32)
    projected = summed_terms.reshape(1, column_width, 3, rank_width)
    returned = lax.all_to_all(
        part_rows.reshape(expert_count, capacity * model_width),
        "expert",
        split_axis=0,
        concat_axis=0,
        tiled=True,
    )
    spread = jnp.dot(
        token_map, returned.reshape(slot_count, model_width), preferred_element_type=jnp.float32
    )
    token_grad = lax.psum_scatter(
        spread.astype(jnp.bfloat16), "dp", scatter_dimension=1, tiled=True
    )
    return (token_grad, projected)

MESH = pl.DeviceIdType.MESH
LANES = 128
TILE = 256
CONTRACT_LAST = (((1,), (1,)), ((), ()))


def column_chunks(half):
    tiles = half // TILE
    crossed = max(1, tiles // 7)
    straight = tiles - crossed
    sizes = [straight // 3 + (1 if i < straight % 3 else 0) for i in range(3)]
    chunks = []
    for side in range(2):
        start = side * half
        for size in [crossed] + sizes:
            chunks.append((start, size * TILE, start == side * half))
            start += size * TILE
    return chunks

PLAN = (
    ("ow", 0), ("ow", 1), ("ow", 4), ("ow", 2), ("sa", 0, 0), ("sa", 1, 0), ("za", 0, 1),
    ("fa", 1, True, 0), ("ow", 3), ("sa", 2, 0), ("fa", 0, True, 0), ("fx", 0), ("sa", 4, 0),
    ("za", 4, 1), ("sa", 0, 1), ("za", 1, 1), ("sa", 3, 0), ("za", 3, 1), ("fy", 0),
    ("za", 2, 1), ("mm", 4, 0), ("sa", 1, 1), ("za", 4, 2), ("mm", 5, 0), ("sa", 4, 1),
    ("fa", 0, True, 1), ("za", 0, 2), ("mm", 0, 0), ("mm", 2, 0), ("za", 1, 2),
    ("fa", 0, False, 1), ("fa", 1, False, 1), ("mm", 6, 0), ("mm", 7, 0), ("fx", 1),
    ("za", 3, 2), ("sa", 3, 1), ("mm", 1, 0), ("fa", 1, True, 1), ("co", 5, 0), ("fy", 1),
    ("sa", 0, 2), ("co", 1, 0), ("za", 2, 2), ("mm", 4, 1), ("mm", 0, 1), ("co", 2, 0),
    ("mm", 1, 1), ("sa", 4, 2), ("sa", 1, 2), ("mm", 6, 1), ("fa", 1, False, 2), ("co", 0, 0),
    ("mm", 7, 1), ("fa", 0, False, 2), ("co", 6, 1), ("mm", 3, 1), ("mm", 2, 1), ("co", 0, 1),
    ("za", 4, 3), ("fa", 0, True, 2), ("sa", 3, 2), ("za", 0, 3), ("za", 1, 3), ("co", 1, 1),
    ("co", 7, 0), ("co", 4, 1), ("fx", 2), ("fa", 1, True, 2), ("co", 4, 0), ("za", 3, 3),
    ("co", 7, 1), ("sa", 0, 3), ("sd", 1, 0), ("co", 6, 0), ("fy", 2), ("mm", 6, 2),
    ("fa", 0, False, 3), ("mm", 4, 2), ("sa", 1, 3), ("mm", 1, 2), ("fa", 0, True, 3),
    ("za", 2, 3), ("mm", 3, 2), ("mm", 0, 2), ("sa", 4, 3), ("fa", 1, False, 3), ("fx", 3),
    ("co", 0, 2), ("fa", 1, True, 3), ("co", 4, 2), ("sa", 3, 3), ("cf", 1), ("sd", 6, 1),
    ("co", 6, 2), ("fy", 3), ("co", 1, 2), ("mm", 0, 3), ("sd", 6, 2), ("mm", 6, 3),
    ("mm", 4, 3), ("co", 3, 2), ("co", 0, 3), ("mm", 7, 2), ("bz", 0, 1, True), ("co", 6, 3),
    ("co", 4, 3), ("sd", 1, 2), ("cf", 2), ("mm", 7, 3), ("bz", 4, 1, False), ("mm", 1, 3),
    ("co", 7, 2), ("bz", 4, 1, True), ("mm", 2, 2), ("sd", 7, 0), ("sd", 6, 3), ("co", 1, 3),
    ("sd", 3, 2), ("bz", 0, 1, False), ("sd", 5, 0), ("mm", 5, 2), ("co", 7, 3), ("mm", 3, 3),
    ("sd", 7, 1), ("pz", 6, 1), ("bz", 4, 2, False), ("co", 5, 2), ("sd", 1, 3), ("mm", 5, 3),
    ("mm", 2, 3), ("co", 3, 3), ("pz", 1, 1), ("co", 5, 3), ("pz", 6, 2), ("sd", 7, 3),
    ("mm", 5, 1), ("sd", 7, 2), ("co", 2, 1), ("co", 2, 3), ("co", 3, 1), ("pz", 7, 1),
    ("sd", 3, 3), ("sd", 1, 1), ("co", 2, 2), ("pz", 1, 2), ("cf", 0), ("bz", 0, 2, False),
    ("sd", 5, 3), ("sd", 5, 2), ("bz", 0, 2, True), ("pz", 3, 1), ("gw",), ("pz", 5, 1),
    ("co", 5, 1), ("pz", 7, 2), ("cf", 3), ("mm", 3, 0), ("sd", 2, 2), ("sd", 2, 3),
    ("bo", 0, True), ("sd", 3, 1), ("bz", 4, 2, True), ("pz", 3, 2), ("pz", 2, 1),
    ("bo", 4, False), ("co", 3, 0), ("sd", 2, 1), ("sd", 6, 0), ("sd", 5, 1), ("pz", 5, 2),
    ("fi", 7), ("bo", 4, True), ("fi", 1), ("bo", 0, False), ("fi", 6), ("pz", 2, 2), ("bs", 0),
    ("sd", 2, 0), ("sd", 3, 0), ("tc",), ("fi", 3), ("bs", 4), ("fi", 5), ("fi", 2), ("pj",),
)


def step_order(depth, layout, chunks):
    planar = range(len(layout))
    hops = range(1, depth - 1)
    steps = [("ow", p) for p in planar]
    for d in range(depth):
        steps += [("za", p, d) for p in planar if d]
        steps += [("sa", p, d) for p in planar if d == 0 or layout[p][0][0] != "b"]
        steps += [("fa", p, f, d) for p in range(2) for f in (False, True) if d or f]
        steps += [("fx", d), ("fy", d)]
    steps += [("gw",)] + [("cf", i) for i in range(depth)] + [("tc",), ("pj",)]
    for k, (_, _, z_first) in enumerate(chunks):
        steps += [("mm", k, i) for i in range(depth)] + [("co", k, i) for i in range(depth)]
        if z_first:
            steps += [("bz", k, hop, flipped) for flipped in (True, False) for hop in hops]
            steps += [("bo", k, True), ("bo", k, False), ("bs", k)]
        else:
            steps += [("sd", k, i) for i in reversed(range(depth))]
            steps += [("pz", k, hop) for hop in hops] + [("fi", k)]
    return PLAN if sorted(map(str, PLAN)) == sorted(map(str, steps)) else steps


def gather_layout(width):
    tiles = width // LANES
    shares = (
        (("o", 0), 0, 10),
        (("o", 1), 0, 8),
        (("b", 0), 20, 8),
        (("a", 1), 16, 12),
        (("a", 2), 0, 0),
    )
    unit = tiles // 28
    pieces = []
    for kind, start, size in shares:
        last = kind[0] != "o" and start + size == 28
        pieces.append((kind, start * unit * LANES, (tiles - start * unit if last else size * unit) * LANES))
    return pieces


def fused_kernel(
    depth, layout, chunks, plan, x_in, y_in, routes, gates, gate_in, up_in, down_in, basis_in,
    grad_out, proj_out,
    x_all, y_all, g_all, gate_w, up_w, down_w, basis, pre_gate, pre_up, grad_gate, grad_up, hidden,
    coef, coef_half, far_coef, coef_t, part, from_core, from_side, from_z, from_zb, from_plane,
    recv_sem, up_sem, down_sem, side_sem, plane_sem, core_sem, local_sem, coef_sem,
    sum_core_sem, sum_side_sem, sum_z_sem, sum_plane_sem,
):
    dp = lax.axis_index("dp")
    me = lax.axis_index("expert")
    z, y, core = me // 4, (me // 2) % 2, me % 2
    rows, width = x_in.shape
    half = width // 2
    hidden_width = gate_w.shape[1]
    rank = basis.shape[1]
    plane_rows = 4 * rows
    core_device = (dp, z * 4 + y * 2 + 1 - core)
    side_device = (dp, z * 4 + (1 - y) * 2 + core)
    plane_device = (1 - dp, me)
    order = [
        sorted(range(depth), key=lambda q, p=p: (abs(q - p), q if 2 * p < depth else -q))
        for p in range(depth)
    ]
    seq = [
        sum(jnp.where(z == p, order[p][i], 0) for p in range(depth)) for i in range(depth)
    ]

    all_cols = pl.ds(0, g_all.shape[1])
    pieces = []
    for kind, start, size in layout:
        source, whole = ((x_in, x_all), (y_in, y_all), (None, g_all))[kind[1]]
        if kind[0] == "o":
            cols = pl.ds(pl.multiple_of(dp * size, LANES), size)
        else:
            cols = all_cols if source is None else pl.ds(start, size)
        pieces.append((source, whole, cols))
    for kind, start, size in layout[:2]:
        source, whole = ((x_in, x_all), (y_in, y_all))[kind[1]]
        pieces.append((source, whole, pl.ds(pl.multiple_of((1 - dp) * size, LANES), size)))
    planar = range(len(layout))
    relayed = range(2)
    far = len(layout)
    y_first = [kind[0] == "b" for kind, _, _ in layout]

    def index(zz, yy, cc):
        return zz * 4 + yy * 2 + cc

    def item_rows(item):
        return pl.ds(pl.multiple_of(item * rows, rows), rows)

    def landed(piece, item):
        _, whole, cols = pieces[piece]
        return whole.at[item_rows(item), cols]

    def copy(piece, item, own, sem, device, recv_piece):
        start, _, cols = pieces[piece]
        src = start.at[:, cols] if own and start is not None else landed(piece, item)
        return pltpu.make_async_remote_copy(
            src_ref=src,
            dst_ref=landed(piece, item),
            send_sem=sem,
            recv_sem=recv_sem.at[recv_piece, item],
            device_id=device,
            device_id_type=MESH,
        )

    def up(piece, zz, yy, own=False):
        item = index(zz, yy, core)
        return copy(piece, item, own, up_sem.at[piece, item // 2], (dp, me + 4), piece)

    def down(piece, zz, yy, own=False):
        item = index(zz, yy, core)
        return copy(piece, item, own, down_sem.at[piece, item // 2], (dp, me - 4), piece)

    def side(piece, zz, own=False):
        return copy(piece, index(zz, y, core), own, side_sem.at[piece, zz], side_device, piece)

    def plane(piece, zz, yy):
        item = index(zz, yy, core)
        return copy(piece, item, False, plane_sem.at[piece, item // 2], plane_device, far + piece)

    def other(piece, zz, yy, own=False):
        item = index(zz, yy, core)
        return copy(piece, item, own, core_sem.at[piece, item // 2], core_device, piece)

    def arrive(piece, item):
        copy(piece, item, False, core_sem.at[0, 0], (dp, me), piece).wait_recv()

    lane = lax.broadcasted_iota(jnp.int32, (rows, LANES), 1)
    table = jnp.zeros((rows, LANES), jnp.float32)
    for k in range(routes.shape[1]):
        table = table + jnp.where(
            routes[:, k : k + 1] == lane, gates[:, k : k + 1].astype(jnp.float32), 0.0
        )
    g_all[item_rows(me), :] = table.astype(jnp.bfloat16)

    barrier = pltpu.get_barrier_semaphore()

    def greet(device):
        pl.semaphore_signal(barrier, inc=1, device_id=device, device_id_type=MESH)

    greet(plane_device)
    greet(side_device)
    greet(core_device)
    pl.when(z > 0)(lambda: greet((dp, me - 4)))
    pl.when(z < depth - 1)(lambda: greet((dp, me + 4)))
    pl.semaphore_wait(barrier, 3 + jnp.minimum(z, 1) + jnp.minimum(depth - 1 - z, 1))

    own_loads = [
        pltpu.make_async_copy(a, b, local_sem.at[i])
        for i, (a, b) in enumerate((
            (x_in, x_all.at[item_rows(me), :]), (y_in, y_all.at[item_rows(me), :]),
            (gate_in, gate_w), (up_in, up_w), (down_in, down_w), (basis_in, basis),
        ))
    ]
    for one in own_loads:
        one.start()

    def spots(away):
        if away == 0:
            return [(z, None)]
        return [(z - away, z >= away), (z + away, z + away < depth)]

    def guarded(condition, act):
        act() if condition is None else pl.when(condition)(act)

    def rise(piece, zz, yy, own=False):
        pl.when(z < depth - 1)(lambda: up(piece, zz, yy, own).start())

    def fall(piece, zz, yy, own=False):
        pl.when(z > 0)(lambda: down(piece, zz, yy, own).start())

    def send_own(piece):
        side(piece, z, True).start()
        rise(piece, z, y, True)
        fall(piece, z, y, True)
        other(piece, z, y, True).start()
        if piece in relayed:
            other(far + piece, z, y, True).start()

    def take_z(piece, away):
        for (zz, there), onward in zip(spots(away), (rise, fall)):
            def act(zz=zz, onward=onward):
                for yy in (y, 1 - y) if y_first[piece] else (y,):
                    arrive(piece, index(zz, yy, core))
                    if not y_first[piece]:
                        side(piece, zz).start()
                    onward(piece, zz, yy)
                    if piece in relayed:
                        plane(piece, zz, yy).start()
                    other(piece, zz, yy).start()

            guarded(there, act)

    def take_side(piece, away):
        for zz, there in spots(away):
            def act(zz=zz):
                arrive(piece, index(zz, 1 - y, core))
                if y_first[piece]:
                    rise(piece, zz, 1 - y)
                    fall(piece, zz, 1 - y)
                if piece in relayed:
                    plane(piece, zz, 1 - y).start()
                other(piece, zz, 1 - y).start()

            guarded(there, act)

    def take_far(piece, flipped, away):
        yy = 1 - y if flipped else y
        for zz, there in spots(away):
            def act(zz=zz):
                arrive(far + piece, index(zz, yy, core))
                other(far + piece, zz, yy).start()

            guarded(there, act)

    def take_core(kinds, away):
        numbers = [p for p, (kind, _, _) in enumerate(layout) if kind[1] in kinds]
        numbers += [far + p for p in numbers if p in relayed]
        for zz, there in spots(away):
            def act(zz=zz):
                for each in numbers:
                    arrive(each, index(zz, 0, 1 - core))
                    arrive(each, index(zz, 1, 1 - core))

            guarded(there, act)

    def rows_of(zz):
        return pl.ds(pl.multiple_of(zz * plane_rows, plane_rows), plane_rows)

    def coef_copy(i):
        return pltpu.make_async_remote_copy(
            src_ref=coef_half.at[rows_of(seq[i]), :],
            dst_ref=far_coef.at[rows_of(seq[i]), :],
            send_sem=coef_sem.at[0, i],
            recv_sem=coef_sem.at[1, i],
            device_id=plane_device,
            device_id_type=MESH,
        )

    def inner_forward(i):
        if i == 0:
            for one in own_loads:
                one.wait()
        take_core((0,), i)
        at = rows_of(seq[i])

        @pl.loop(0, hidden_width // TILE)
        def _(n):
            cols = pl.ds(pl.multiple_of(n * TILE, TILE), TILE)
            pre_gate[:, cols] = jnp.dot(
                x_all[at, :], gate_w[:, cols], preferred_element_type=jnp.float32
            )
            pre_up[:, cols] = jnp.dot(
                x_all[at, :], up_w[:, cols], preferred_element_type=jnp.float32
            )

    def inner_backward(i):
        take_core((1, 2), i)
        at = rows_of(seq[i])
        expert = lax.broadcasted_iota(jnp.int32, (plane_rows, LANES), 1)
        gain = jnp.sum(
            jnp.where(expert == me, g_all[at, :].astype(jnp.float32), 0.0), axis=1, keepdims=True
        )

        @pl.loop(0, hidden_width // TILE)
        def _(n):
            cols = pl.ds(pl.multiple_of(n * TILE, TILE), TILE)
            grad_hidden = lax.dot_general(
                y_all[at, :], down_w[cols, :], CONTRACT_LAST, preferred_element_type=jnp.float32
            )
            a = pre_gate[:, cols]
            u = pre_up[:, cols]
            sigma = jax.nn.sigmoid(a)
            silu = a * sigma
            scaled = gain * grad_hidden
            grad_up[at, cols] = (scaled * silu).astype(jnp.bfloat16)
            grad_gate[at, cols] = (scaled * u * sigma * (1.0 + a * (1.0 - sigma))).astype(
                jnp.bfloat16
            )
            hidden[:, cols] = (silu * u).astype(jnp.bfloat16)

        low = jnp.dot(grad_gate[at, :], basis[...], preferred_element_type=jnp.float32)
        mid = jnp.dot(grad_up[at, :], basis[...], preferred_element_type=jnp.float32)
        top = gain * jnp.dot(hidden[...], basis[...], preferred_element_type=jnp.float32)
        for j, value in enumerate((low, mid, top)):
            coef[at, j * rank : (j + 1) * rank] = value
            coef_half[at, j * rank : (j + 1) * rank] = value.astype(jnp.bfloat16)

    def send_coef(i):
        coef_copy(i).start()

    def gather_sent():
        for piece in planar:
            for zz in range(depth):
                if not y_first[piece]:
                    side(piece, zz).wait_send()
                for yy in (y, 1 - y) if y_first[piece] else (y,):
                    pl.when((zz <= z) & (z < depth - 1))(
                        lambda p=piece, q=zz, yy=yy: up(p, q, yy).wait_send()
                    )
                    pl.when((zz >= z) & (z > 0))(
                        lambda p=piece, q=zz, yy=yy: down(p, q, yy).wait_send()
                    )
            if y_first[piece]:
                side(piece, z).wait_send()
        for piece in relayed:
            for pair in range(2 * depth):
                pl.when(pair != me // 2)(
                    lambda p=piece, q=pair: plane(p, q // 2, q % 2).wait_send()
                )
        for piece in range(len(pieces)):
            for pair in range(2 * depth):
                other(piece, pair // 2, pair % 2).wait_send()

    def remote(src, dst, send, recv, device):
        return pltpu.make_async_remote_copy(
            src_ref=src, dst_ref=dst, send_sem=send, recv_sem=recv,
            device_id=device, device_id_type=MESH,
        )

    crossed = [k for k, chunk in enumerate(chunks) if chunk[2]]

    def cols_of(k):
        return pl.ds(chunks[k][0], chunks[k][1])

    def sum_core_copy(k, i):
        pair = pl.ds(seq[i] * 2, 2)
        return remote(
            part.at[pair, 1 - core, :, cols_of(k)], from_core.at[pair, :, cols_of(k)],
            sum_core_sem.at[0, k, i], sum_core_sem.at[1, k, i], core_device,
        )

    def sum_side_copy(k, zz):
        return remote(
            part.at[zz * 2 + 1 - y, core, :, cols_of(k)], from_side.at[zz, :, cols_of(k)],
            sum_side_sem.at[0, k, zz], sum_side_sem.at[1, k, zz], side_device,
        )

    def sum_z_copy(k, zz, upward, flipped=False):
        way = 0 if upward else 1
        if flipped:
            number = crossed.index(k)
            landing = from_zb.at[way, zz, :, pl.ds(number * chunks[k][1], chunks[k][1])]
            number += len(chunks)
        else:
            number = k
            landing = from_z.at[way, zz, :, cols_of(k)]
        slot = zz * 2 + (1 - y if flipped else y)
        return remote(
            part.at[slot, core, :, cols_of(k)], landing,
            sum_z_sem.at[0, way, number, zz], sum_z_sem.at[1, way, number, zz],
            (dp, me + 4 if upward else me - 4),
        )

    def sum_plane_copy(k):
        start, size, _ = chunks[k]
        return remote(
            part.at[z * 2 + y, core, :, cols_of(k)], from_plane.at[:, pl.ds(start % half, size)],
            sum_plane_sem.at[0, k], sum_plane_sem.at[1, k], plane_device,
        )

    def add_into(slot, k, term):
        total = part[slot, core, :, cols_of(k)].astype(jnp.float32) + term.astype(jnp.float32)
        part[slot, core, :, cols_of(k)] = total.astype(jnp.bfloat16)

    def multiply(k, i):
        start, size, _ = chunks[k]
        at = rows_of(seq[i])

        @pl.loop(0, size // TILE)
        def _(n):
            cols = pl.ds(pl.multiple_of(start + n * TILE, TILE), TILE)
            rows_out = lax.dot_general(
                grad_gate[at, :], gate_w[cols, :], CONTRACT_LAST,
                preferred_element_type=jnp.float32,
            ) + lax.dot_general(
                grad_up[at, :], up_w[cols, :], CONTRACT_LAST,
                preferred_element_type=jnp.float32,
            )
            part[pl.ds(seq[i] * 2, 2), :, :, cols] = rows_out.astype(jnp.bfloat16).reshape(
                2, 2, rows, TILE
            )

        sum_core_copy(k, i).start()

    def over_cores(k, i):
        zz = seq[i]
        sum_core_copy(k, i).wait_recv()
        slot = zz * 2 + 1 - y
        add_into(slot, k, from_core[slot, :, cols_of(k)])
        if not chunks[k][2]:
            sum_side_copy(k, zz).start()
        slot = zz * 2 + y
        add_into(slot, k, from_core[slot, :, cols_of(k)])
        if chunks[k][2]:
            for flipped in (True, False):
                pl.when((z == 0) & (zz > 0))(
                    lambda f=flipped: sum_z_copy(k, zz, True, f).start()
                )
                pl.when((z == depth - 1) & (zz < z))(
                    lambda f=flipped: sum_z_copy(k, zz, False, f).start()
                )

    def z_term(k, zz, upward, flipped):
        sum_z_copy(k, zz, upward, flipped).wait_recv()
        if flipped:
            size = chunks[k][1]
            at = pl.ds(crossed.index(k) * size, size)
            term = from_zb[0 if upward else 1, zz, :, at]
        else:
            term = from_z[0 if upward else 1, zz, :, cols_of(k)]
        add_into(zz * 2 + (1 - y if flipped else y), k, term)

    def pass_on(k, hop, flipped=False):
        def climb():
            for zz in reversed(range(hop + 1, depth)):
                z_term(k, zz, True, flipped)
                sum_z_copy(k, zz, True, flipped).start()

        def sink():
            for zz in range(depth - 1 - hop):
                z_term(k, zz, False, flipped)
                sum_z_copy(k, zz, False, flipped).start()

        pl.when(z == hop)(climb)
        pl.when(z == depth - 1 - hop)(sink)

    def own_plane(k, flipped=False):
        pl.when(z > 0)(lambda: z_term(k, z, True, flipped))
        pl.when(z < depth - 1)(lambda: z_term(k, z, False, flipped))

    def over_side(k, i):
        zz = seq[i]
        sum_side_copy(k, zz).wait_recv()
        add_into(zz * 2 + y, k, from_side[zz, :, cols_of(k)])
        pl.when((z == 0) & (zz > 0))(lambda: sum_z_copy(k, zz, True).start())
        pl.when((z == depth - 1) & (zz < z))(lambda: sum_z_copy(k, zz, False).start())

    def leave(k):
        pl.when(dp != chunks[k][0] // half)(lambda: sum_plane_copy(k).start())

    def finish(k):
        own_plane(k)
        leave(k)

    def crossed_own(k, flipped):
        own_plane(k, flipped)
        if flipped:
            sum_side_copy(k, z).start()

    def crossed_side(k):
        sum_side_copy(k, z).wait_recv()
        add_into(z * 2 + y, k, from_side[z, :, cols_of(k)])
        leave(k)

    def turn_coef():
        for i in range(depth):
            coef_copy(i).wait_recv()
        coef_t[...] = (coef[...] + far_coef[...].astype(jnp.float32)).T.astype(jnp.bfloat16)

    def project():
        @pl.loop(0, half // TILE)
        def _(n):
            cols = pl.ds(pl.multiple_of(dp * half + n * TILE, TILE), TILE)
            at = pl.ds(pl.multiple_of(n * TILE, TILE), TILE)
            front = jnp.dot(
                coef_t[0 : 2 * rank, :], x_all[:, cols], preferred_element_type=jnp.float32
            ).T
            proj_out[0, at, :] = front[:, 0:rank]
            proj_out[1, at, :] = front[:, rank : 2 * rank]
            proj_out[2, at, :] = jnp.dot(
                coef_t[2 * rank : 3 * rank, :], y_all[:, cols], preferred_element_type=jnp.float32
            ).T

    stages = {
        "ow": send_own, "za": take_z, "sa": take_side, "fa": take_far, "fx": inner_forward,
        "fy": inner_backward, "cf": send_coef, "gw": gather_sent,
        "mm": multiply, "co": over_cores, "sd": over_side, "pz": pass_on, "fi": finish,
        "bz": pass_on, "bo": crossed_own, "bs": crossed_side, "tc": turn_coef, "pj": project,
    }
    for stage, *at in plan:
        stages[stage](*at)

    for k, (start, size, z_first) in enumerate(chunks):
        def take_plane(k=k, start=start, size=size):
            sum_plane_copy(k).wait_recv()
            at = pl.ds(start % half, size)
            total = part[z * 2 + y, core, :, cols_of(k)].astype(jnp.float32) + from_plane[
                :, at
            ].astype(jnp.float32)
            grad_out[:, at] = total.astype(jnp.bfloat16)

        pl.when(dp == start // half)(take_plane)
        pl.when(dp != start // half)(lambda k=k: sum_plane_copy(k).wait_send())
        for i in range(depth):
            sum_core_copy(k, i).wait_send()
        if z_first:
            sum_side_copy(k, z).wait_send()
        for zz in range(depth):
            if not z_first:
                sum_side_copy(k, zz).wait_send()
            for flipped in ((False, True) if z_first else (False,)):
                pl.when(zz > z)(
                    lambda k=k, zz=zz, f=flipped: sum_z_copy(k, zz, True, f).wait_send()
                )
                pl.when(zz < z)(
                    lambda k=k, zz=zz, f=flipped: sum_z_copy(k, zz, False, f).wait_send()
                )

    for i in range(depth):
        coef_copy(i).wait_send()


def dense_form(
    saved_inputs, output_grad, routes, route_gates, expert_gate, expert_up, expert_down, proj_basis
):
    expert_count = lax.axis_size("expert")
    group_count = lax.axis_size("dp")
    rows, width = saved_inputs.shape
    all_rows = rows * expert_count
    hidden_width = expert_gate.shape[2]
    rank = proj_basis.shape[2]
    depth = expert_count // 4
    half = width // group_count
    layout = gather_layout(width)
    chunks = column_chunks(half)
    crossed_width = sum(size for _, size, z_first in chunks if z_first)
    dma = pltpu.SemaphoreType.DMA
    bf16, f32 = jnp.bfloat16, jnp.float32
    whole = pl.BlockSpec(memory_space=pl.ANY)
    held = pl.BlockSpec(memory_space=pltpu.VMEM)
    token_grad, terms = pl.pallas_call(
        functools.partial(
            fused_kernel, depth, layout, chunks, step_order(depth, layout, chunks)
        ),
        out_shape=[
            jax.ShapeDtypeStruct((rows, half), bf16),
            jax.ShapeDtypeStruct((3, half, rank), f32),
        ],
        in_specs=[whole, whole, held, held, whole, whole, whole, whole],
        out_specs=[held] * 2,
        scratch_shapes=[
            pltpu.VMEM((all_rows, width), bf16),
            pltpu.VMEM((all_rows, width), bf16),
            pltpu.VMEM((all_rows, LANES), bf16),
            pltpu.VMEM((width, hidden_width), bf16),
            pltpu.VMEM((width, hidden_width), bf16),
            pltpu.VMEM((hidden_width, width), bf16),
            pltpu.VMEM((hidden_width, rank), bf16),
            pltpu.VMEM((4 * rows, hidden_width), f32),
            pltpu.VMEM((4 * rows, hidden_width), f32),
            pltpu.VMEM((all_rows, hidden_width), bf16),
            pltpu.VMEM((all_rows, hidden_width), bf16),
            pltpu.VMEM((4 * rows, hidden_width), bf16),
            pltpu.VMEM((all_rows, 3 * rank), f32),
            pltpu.VMEM((all_rows, 3 * rank), bf16),
            pltpu.VMEM((all_rows, 3 * rank), bf16),
            pltpu.VMEM((3 * rank, all_rows), bf16),
            pltpu.VMEM((2 * depth, 2, rows, width), bf16),
            pltpu.VMEM((2 * depth, rows, width), bf16),
            pltpu.VMEM((depth, rows, width), bf16),
            pltpu.VMEM((2, depth, rows, width), bf16),
            pltpu.VMEM((2, depth, rows, crossed_width), bf16),
            pltpu.VMEM((rows, half), bf16),
            dma((len(layout) + 2, expert_count)),
            dma((len(layout), 2 * depth)),
            dma((len(layout), 2 * depth)),
            dma((len(layout), depth)),
            dma((2, 2 * depth)),
            dma((len(layout) + 2, 2 * depth)),
            dma((6,)),
            dma((2, depth)),
            dma((2, len(chunks), depth)),
            dma((2, len(chunks), depth)),
            dma((2, 2, len(chunks) + 2, depth)),
            dma((2, len(chunks))),
        ],
        compiler_params=pltpu.CompilerParams(
            collective_id=0, has_side_effects=True, vmem_limit_bytes=60 * 1024 * 1024
        ),
    )(
        saved_inputs, output_grad, routes, route_gates,
        expert_gate[0], expert_up[0], expert_down[0], proj_basis[0],
    )
    return (token_grad, terms.transpose(1, 0, 2)[None])


def on_device(*arrays):
    if lax.axis_size("expert") <= 2 * arrays[2].shape[1]:
        return dense_form(*arrays)
    return slot_form(*arrays)


def solution(mesh):
    placed = (
        P("expert", None),
        P("expert", None),
        P("expert", None),
        P("expert", None),
        P("expert", None, "dp"),
        P("expert", None, "dp"),
        P("expert", "dp", None),
        P("expert", "dp", None),
    )
    return jax.shard_map(
        on_device,
        mesh=mesh,
        in_specs=placed,
        out_specs=(P("expert", "dp"), P("expert", "dp", None, None)),
        check_vma=False,
    )
```

```python
import functools

import jax
import jax.numpy as jnp
from jax import lax
from jax.experimental import pallas as pl
from jax.experimental.pallas import tpu as pltpu
from jax.sharding import PartitionSpec as P


def slot_form(
    saved_inputs, output_grad, routes, route_gates, expert_gate, expert_up, expert_down, proj_basis
):
    token_count, model_width = saved_inputs.shape
    top_count = routes.shape[1]
    expert_count = lax.axis_size("expert")
    group_count = lax.axis_size("dp")
    capacity = token_count * top_count * 9 // (8 * expert_count)
    slot_count = expert_count * capacity
    column_width = model_width // group_count
    route_count = token_count * top_count
    flat_routes = routes.reshape(-1)
    position = jnp.arange(route_count, dtype=jnp.int32)
    earlier = jnp.sum(
        (
            (flat_routes[:, None] == flat_routes[None, :])
            & (position[None, :] < position[:, None])
        ).astype(jnp.int32),
        axis=1,
    )
    target_slot = flat_routes * capacity + earlier
    slot_owner = (
        jnp.full((slot_count,), route_count, jnp.int32)
        .at[target_slot]
        .set(jnp.arange(route_count, dtype=jnp.int32))
    )
    filled = slot_owner < route_count
    safe_route = jnp.minimum(slot_owner, route_count - 1)
    source_token = safe_route // top_count
    zero_half = jnp.zeros((), jnp.bfloat16)
    gate_slots = jnp.where(filled, route_gates.reshape(-1)[safe_route], zero_half).reshape(
        expert_count, capacity
    )
    token_map = (
        (source_token[None, :] == jnp.arange(token_count, dtype=jnp.int32)[:, None])
        & filled[None, :]
    ).astype(jnp.bfloat16)
    contract_first = (((0,), (0,)), ((), ()))

    def to_slots(source_rows):
        picked = lax.dot_general(
            token_map, source_rows, contract_first, preferred_element_type=jnp.float32
        ).astype(jnp.bfloat16)
        return picked.reshape(expert_count, capacity * source_rows.shape[1])

    recv_inputs, recv_grads, recv_gates = (
        lax.all_to_all(to_slots(saved_inputs), "expert", split_axis=0, concat_axis=0, tiled=True),
        lax.all_to_all(to_slots(output_grad), "expert", split_axis=0, concat_axis=0, tiled=True),
        lax.all_to_all(gate_slots, "expert", split_axis=0, concat_axis=0, tiled=True),
    )
    input_rows = recv_inputs.reshape(slot_count, model_width)
    grad_rows = recv_grads.reshape(slot_count, model_width)
    gain = recv_gates.reshape(slot_count, 1).astype(jnp.float32)
    gate_w = expert_gate[0]
    up_w = expert_up[0]
    down_w = expert_down[0]
    basis = proj_basis[0]
    rank_width = basis.shape[1]
    contract_last = (((1,), (1,)), ((), ()))
    pre_gate = jnp.dot(input_rows, gate_w, preferred_element_type=jnp.float32)
    pre_up = jnp.dot(input_rows, up_w, preferred_element_type=jnp.float32)
    grad_hidden = lax.dot_general(
        grad_rows, down_w, contract_last, preferred_element_type=jnp.float32
    )
    sigma = jax.nn.sigmoid(pre_gate)
    silu_val = pre_gate * sigma
    scaled = gain * grad_hidden
    grad_up = (scaled * silu_val).astype(jnp.bfloat16)
    grad_gate = (scaled * pre_up * sigma * (1.0 + pre_gate * (1.0 - sigma))).astype(jnp.bfloat16)
    hidden = (silu_val * pre_up).astype(jnp.bfloat16)
    part_rows = (
        lax.dot_general(grad_gate, gate_w, contract_last, preferred_element_type=jnp.float32)
        + lax.dot_general(grad_up, up_w, contract_last, preferred_element_type=jnp.float32)
    ).astype(jnp.bfloat16)
    coef_gate = jnp.dot(grad_gate, basis, preferred_element_type=jnp.float32).astype(jnp.bfloat16)
    coef_up = jnp.dot(grad_up, basis, preferred_element_type=jnp.float32).astype(jnp.bfloat16)
    coef_down = (gain * jnp.dot(hidden, basis, preferred_element_type=jnp.float32)).astype(
        jnp.bfloat16
    )
    coef_pair = jnp.concatenate([coef_gate, coef_up], axis=1)
    front = lax.dot_general(
        input_rows, coef_pair, contract_first, preferred_element_type=jnp.float32
    )
    rear = lax.dot_general(grad_rows, coef_down, contract_first, preferred_element_type=jnp.float32)
    summed_terms = lax.psum_scatter(
        jnp.concatenate([front, rear], axis=1).astype(jnp.bfloat16),
        "dp",
        scatter_dimension=0,
        tiled=True,
    ).astype(jnp.float32)
    projected = summed_terms.reshape(1, column_width, 3, rank_width)
    returned = lax.all_to_all(
        part_rows.reshape(expert_count, capacity * model_width),
        "expert",
        split_axis=0,
        concat_axis=0,
        tiled=True,
    )
    spread = jnp.dot(
        token_map, returned.reshape(slot_count, model_width), preferred_element_type=jnp.float32
    )
    token_grad = lax.psum_scatter(
        spread.astype(jnp.bfloat16), "dp", scatter_dimension=1, tiled=True
    )
    return (token_grad, projected)

MESH = pl.DeviceIdType.MESH
LANES = 128
TILE = 256
CONTRACT_LAST = (((1,), (1,)), ((), ()))


def column_chunks(half):
    tiles = half // TILE
    crossed = max(1, tiles // 7)
    straight = tiles - crossed
    sizes = [straight // 3 + (1 if i < straight % 3 else 0) for i in range(3)]
    chunks = []
    for side in range(2):
        start = side * half
        for size in [crossed] + sizes:
            chunks.append((start, size * TILE, start == side * half))
            start += size * TILE
    return chunks

PLAN = (
    ("ow", 0), ("ow", 1), ("ow", 2), ("sa", 0, 0), ("sa", 1, 0), ("za", 0, 1),
    ("fa", 1, True, 0), ("ow", 3), ("sa", 2, 0), ("fa", 0, True, 0), ("fx", 0), ("sa", 0, 1),
    ("za", 1, 1), ("sa", 3, 0), ("za", 3, 1), ("fy", 0), ("za", 2, 1), ("mm", 4, 0),
    ("sa", 1, 1), ("mm", 5, 0), ("fa", 0, True, 1), ("za", 0, 2), ("mm", 0, 0), ("mm", 2, 0),
    ("za", 1, 2), ("fa", 0, False, 1), ("fa", 1, False, 1), ("mm", 6, 0), ("mm", 7, 0),
    ("fx", 1), ("za", 3, 2), ("sa", 3, 1), ("mm", 1, 0), ("fa", 1, True, 1), ("co", 5, 0),
    ("fy", 1), ("sa", 0, 2), ("co", 1, 0), ("za", 2, 2), ("mm", 4, 1), ("mm", 0, 1),
    ("co", 2, 0), ("mm", 1, 1), ("sa", 1, 2), ("mm", 6, 1), ("fa", 1, False, 2), ("co", 0, 0),
    ("mm", 7, 1), ("fa", 0, False, 2), ("co", 6, 1), ("mm", 3, 1), ("mm", 2, 1), ("co", 0, 1),
    ("fa", 0, True, 2), ("sa", 3, 2), ("za", 0, 3), ("za", 1, 3), ("co", 1, 1), ("co", 7, 0),
    ("co", 4, 1), ("fx", 2), ("za", 3, 3), ("fa", 1, True, 2), ("co", 4, 0), ("co", 7, 1),
    ("sa", 0, 3), ("sd", 1, 0), ("co", 6, 0), ("fy", 2), ("mm", 6, 2), ("fa", 0, False, 3),
    ("mm", 4, 2), ("sa", 1, 3), ("mm", 1, 2), ("fa", 0, True, 3), ("za", 2, 3), ("mm", 3, 2),
    ("mm", 0, 2), ("fa", 1, False, 3), ("fx", 3), ("co", 0, 2), ("fa", 1, True, 3), ("co", 4, 2),
    ("sa", 3, 3), ("cf", 1), ("sd", 6, 1), ("co", 6, 2), ("fy", 3), ("co", 1, 2), ("mm", 0, 3),
    ("sd", 6, 2), ("mm", 6, 3), ("mm", 4, 3), ("co", 3, 2), ("co", 0, 3), ("mm", 7, 2),
    ("bz", 0, 1, True), ("co", 6, 3), ("co", 4, 3), ("sd", 1, 2), ("cf", 2), ("mm", 7, 3),
    ("bz", 4, 1, False), ("mm", 1, 3), ("co", 7, 2), ("bz", 4, 1, True), ("mm", 2, 2),
    ("sd", 7, 0), ("sd", 6, 3), ("co", 1, 3), ("sd", 3, 2), ("bz", 0, 1, False), ("sd", 5, 0),
    ("mm", 5, 2), ("co", 7, 3), ("mm", 3, 3), ("sd", 7, 1), ("pz", 6, 1), ("bz", 4, 2, False),
    ("co", 5, 2), ("sd", 1, 3), ("mm", 5, 3), ("mm", 2, 3), ("co", 3, 3), ("pz", 1, 1),
    ("co", 5, 3), ("pz", 6, 2), ("sd", 7, 3), ("mm", 5, 1), ("sd", 7, 2), ("co", 2, 1),
    ("co", 2, 3), ("co", 3, 1), ("pz", 7, 1), ("sd", 3, 3), ("sd", 1, 1), ("co", 2, 2),
    ("pz", 1, 2), ("cf", 0), ("bz", 0, 2, False), ("sd", 5, 3), ("sd", 5, 2), ("bz", 0, 2, True),
    ("pz", 3, 1), ("gw",), ("pz", 5, 1), ("co", 5, 1), ("pz", 7, 2), ("cf", 3), ("mm", 3, 0),
    ("sd", 2, 2), ("sd", 2, 3), ("bo", 0, True), ("sd", 3, 1), ("bz", 4, 2, True), ("pz", 3, 2),
    ("pz", 2, 1), ("bo", 4, False), ("co", 3, 0), ("sd", 2, 1), ("sd", 6, 0), ("sd", 5, 1),
    ("pz", 5, 2), ("fi", 7), ("bo", 4, True), ("fi", 1), ("bo", 0, False), ("rw", 7), ("fi", 6),
    ("pz", 2, 2), ("rw", 1), ("bs", 0), ("rw", 6), ("sd", 2, 0), ("sd", 3, 0), ("tc",),
    ("fi", 3), ("bs", 4), ("fi", 5), ("rw", 0), ("fi", 2), ("rw", 3), ("rw", 4), ("rw", 5),
    ("pj",), ("rw", 2),
)


def step_order(depth, layout, chunks):
    planar = range(len(layout))
    hops = range(1, depth - 1)
    steps = [("ow", p) for p in planar]
    for d in range(depth):
        steps += [("za", p, d) for p in planar if d]
        steps += [("sa", p, d) for p in planar if d == 0 or layout[p][0][0] != "b"]
        steps += [("fa", p, f, d) for p in range(2) for f in (False, True) if d or f]
        steps += [("fx", d), ("fy", d)]
    steps += [("gw",)] + [("cf", i) for i in range(depth)] + [("tc",), ("pj",)]
    for k, (_, _, z_first) in enumerate(chunks):
        steps += [("mm", k, i) for i in range(depth)] + [("co", k, i) for i in range(depth)]
        if z_first:
            steps += [("bz", k, hop, flipped) for flipped in (True, False) for hop in hops]
            steps += [("bo", k, True), ("bo", k, False), ("bs", k)]
        else:
            steps += [("sd", k, i) for i in reversed(range(depth))]
            steps += [("pz", k, hop) for hop in hops] + [("fi", k)]
        steps += [("rw", k)]
    return PLAN if sorted(map(str, PLAN)) == sorted(map(str, steps)) else steps


def gather_layout(width):
    tiles = width // LANES
    shares = (
        (("o", 0), 0, 10),
        (("o", 1), 0, 8),
        (("b", 0), 20, 8),
        (("a", 2), 16, 12),
    )
    unit = tiles // 28
    pieces = []
    for kind, start, size in shares:
        last = kind[0] != "o" and start + size == 28
        first = start * unit * LANES
        stop = width if last else first + size * unit * LANES
        pieces.append((kind, first, stop - first + (LANES if kind[1] == 2 else 0)))
    return pieces


def fused_kernel(
    depth, layout, chunks, plan, x_in, y_in, routes, gates, gate_in, up_in, down_in, basis_in,
    grad_out, proj_out,
    proj,
    x_all, y_all, gate_w, up_w, down_w, basis, pre_gate, pre_up, grad_gate, grad_up, hidden,
    coef, coef_half, far_coef, coef_t, part, from_core, from_side, from_z, from_zb, from_plane,
    recv_sem, up_sem, down_sem, side_sem, plane_sem, core_sem, local_sem, coef_sem,
    sum_core_sem, sum_side_sem, sum_z_sem, sum_plane_sem,
):
    dp = lax.axis_index("dp")
    me = lax.axis_index("expert")
    z, y, core = me // 4, (me // 2) % 2, me % 2
    rows, width = x_in.shape
    half = width // 2
    hidden_width = gate_w.shape[1]
    rank = basis.shape[1]
    plane_rows = 4 * rows
    core_device = (dp, z * 4 + y * 2 + 1 - core)
    side_device = (dp, z * 4 + (1 - y) * 2 + core)
    plane_device = (1 - dp, me)
    order = [
        sorted(range(depth), key=lambda q, p=p: (abs(q - p), q if 2 * p < depth else -q))
        for p in range(depth)
    ]
    seq = [
        sum(jnp.where(z == p, order[p][i], 0) for p in range(depth)) for i in range(depth)
    ]

    pieces = []
    for kind, start, size in layout:
        source, whole = ((x_in, x_all), (y_in, y_all), (None, y_all))[kind[1]]
        if kind[0] == "o":
            cols = pl.ds(pl.multiple_of(dp * size, LANES), size)
        else:
            cols = pl.ds(start, size)
        pieces.append((source, whole, cols))
    for kind, start, size in layout[:2]:
        source, whole = ((x_in, x_all), (y_in, y_all))[kind[1]]
        pieces.append((source, whole, pl.ds(pl.multiple_of((1 - dp) * size, LANES), size)))
    planar = range(len(layout))
    relayed = range(2)
    far = len(layout)
    y_first = [kind[0] == "b" for kind, _, _ in layout]

    def index(zz, yy, cc):
        return zz * 4 + yy * 2 + cc

    def item_rows(item):
        return pl.ds(pl.multiple_of(item * rows, rows), rows)

    def landed(piece, item):
        _, whole, cols = pieces[piece]
        return whole.at[item_rows(item), cols]

    def copy(piece, item, own, sem, device, recv_piece):
        start, _, cols = pieces[piece]
        src = start.at[:, cols] if own and start is not None else landed(piece, item)
        return pltpu.make_async_remote_copy(
            src_ref=src,
            dst_ref=landed(piece, item),
            send_sem=sem,
            recv_sem=recv_sem.at[recv_piece, item],
            device_id=device,
            device_id_type=MESH,
        )

    def up(piece, zz, yy, own=False):
        item = index(zz, yy, core)
        return copy(piece, item, own, up_sem.at[piece, item // 2], (dp, me + 4), piece)

    def down(piece, zz, yy, own=False):
        item = index(zz, yy, core)
        return copy(piece, item, own, down_sem.at[piece, item // 2], (dp, me - 4), piece)

    def side(piece, zz, own=False):
        return copy(piece, index(zz, y, core), own, side_sem.at[piece, zz], side_device, piece)

    def plane(piece, zz, yy):
        item = index(zz, yy, core)
        return copy(piece, item, False, plane_sem.at[piece, item // 2], plane_device, far + piece)

    def other(piece, zz, yy, own=False):
        item = index(zz, yy, core)
        return copy(piece, item, own, core_sem.at[piece, item // 2], core_device, piece)

    def arrive(piece, item):
        copy(piece, item, False, core_sem.at[0, 0], (dp, me), piece).wait_recv()

    own_loads = [
        pltpu.make_async_copy(a, b, local_sem.at[i])
        for i, (a, b) in enumerate((
            (y_in, y_all.at[item_rows(me), pl.ds(0, width)]), (x_in, x_all.at[item_rows(me), :]),
            (gate_in, gate_w), (up_in, up_w), (down_in, down_w), (basis_in, basis),
        ))
    ]
    for one in own_loads:
        one.start()

    lane = lax.broadcasted_iota(jnp.int32, (LANES, rows), 0)
    table = jnp.zeros((LANES, rows), jnp.float32)
    for k in range(routes.shape[0]):
        table = table + jnp.where(
            routes[k : k + 1, :] == lane, gates[k : k + 1, :].astype(jnp.float32), 0.0
        )
    y_all[item_rows(me), width : width + LANES] = table.T.astype(jnp.bfloat16)

    barrier = pltpu.get_barrier_semaphore()

    def greet(device):
        pl.semaphore_signal(barrier, inc=1, device_id=device, device_id_type=MESH)

    greet(plane_device)
    greet(side_device)
    greet(core_device)
    pl.when(z > 0)(lambda: greet((dp, me - 4)))
    pl.when(z < depth - 1)(lambda: greet((dp, me + 4)))
    pl.semaphore_wait(barrier, 3 + jnp.minimum(z, 1) + jnp.minimum(depth - 1 - z, 1))

    def spots(away):
        if away == 0:
            return [(z, None)]
        return [(z - away, z >= away), (z + away, z + away < depth)]

    def guarded(condition, act):
        act() if condition is None else pl.when(condition)(act)

    def rise(piece, zz, yy, own=False):
        pl.when(z < depth - 1)(lambda: up(piece, zz, yy, own).start())

    def fall(piece, zz, yy, own=False):
        pl.when(z > 0)(lambda: down(piece, zz, yy, own).start())

    def send_own(piece):
        if pieces[piece][0] is None:
            own_loads[0].wait()
        side(piece, z, True).start()
        rise(piece, z, y, True)
        fall(piece, z, y, True)
        other(piece, z, y, True).start()
        if piece in relayed:
            other(far + piece, z, y, True).start()

    def take_z(piece, away):
        for (zz, there), onward in zip(spots(away), (rise, fall)):
            def act(zz=zz, onward=onward):
                for yy in (y, 1 - y) if y_first[piece] else (y,):
                    arrive(piece, index(zz, yy, core))
                    if not y_first[piece]:
                        side(piece, zz).start()
                    onward(piece, zz, yy)
                    if piece in relayed:
                        plane(piece, zz, yy).start()
                    other(piece, zz, yy).start()

            guarded(there, act)

    def take_side(piece, away):
        for zz, there in spots(away):
            def act(zz=zz):
                arrive(piece, index(zz, 1 - y, core))
                if y_first[piece]:
                    rise(piece, zz, 1 - y)
                    fall(piece, zz, 1 - y)
                if piece in relayed:
                    plane(piece, zz, 1 - y).start()
                other(piece, zz, 1 - y).start()

            guarded(there, act)

    def take_far(piece, flipped, away):
        yy = 1 - y if flipped else y
        for zz, there in spots(away):
            def act(zz=zz):
                arrive(far + piece, index(zz, yy, core))
                other(far + piece, zz, yy).start()

            guarded(there, act)

    def take_core(kinds, away):
        numbers = [p for p, (kind, _, _) in enumerate(layout) if kind[1] in kinds]
        numbers += [far + p for p in numbers if p in relayed]
        for zz, there in spots(away):
            def act(zz=zz):
                for each in numbers:
                    arrive(each, index(zz, 0, 1 - core))
                    arrive(each, index(zz, 1, 1 - core))

            guarded(there, act)

    def rows_of(zz):
        return pl.ds(pl.multiple_of(zz * plane_rows, plane_rows), plane_rows)

    def coef_copy(i):
        return pltpu.make_async_remote_copy(
            src_ref=coef_half.at[rows_of(seq[i]), :],
            dst_ref=far_coef.at[rows_of(seq[i]), :],
            send_sem=coef_sem.at[0, i],
            recv_sem=coef_sem.at[1, i],
            device_id=plane_device,
            device_id_type=MESH,
        )

    def inner_forward(i):
        if i == 0:
            for one in own_loads[1:]:
                one.wait()
        take_core((0,), i)
        at = rows_of(seq[i])

        @pl.loop(0, hidden_width // TILE)
        def _(n):
            cols = pl.ds(pl.multiple_of(n * TILE, TILE), TILE)
            pre_gate[:, cols] = jnp.dot(
                x_all[at, :], gate_w[:, cols], preferred_element_type=jnp.float32
            )
            pre_up[:, cols] = jnp.dot(
                x_all[at, :], up_w[:, cols], preferred_element_type=jnp.float32
            )

    def inner_backward(i):
        take_core((1, 2), i)
        at = rows_of(seq[i])
        expert = lax.broadcasted_iota(jnp.int32, (plane_rows, LANES), 1)
        gain = jnp.sum(
            jnp.where(expert == me, y_all[at, width : width + LANES].astype(jnp.float32), 0.0),
            axis=1,
            keepdims=True,
        )

        @pl.loop(0, hidden_width // TILE)
        def _(n):
            cols = pl.ds(pl.multiple_of(n * TILE, TILE), TILE)
            grad_hidden = lax.dot_general(
                y_all[at, 0:width], down_w[cols, :], CONTRACT_LAST, preferred_element_type=jnp.float32
            )
            a = pre_gate[:, cols]
            u = pre_up[:, cols]
            sigma = jax.nn.sigmoid(a)
            silu = a * sigma
            scaled = gain * grad_hidden
            grad_up[at, cols] = (scaled * silu).astype(jnp.bfloat16)
            grad_gate[at, cols] = (scaled * u * sigma * (1.0 + a * (1.0 - sigma))).astype(
                jnp.bfloat16
            )
            hidden[:, cols] = (silu * u).astype(jnp.bfloat16)

        low = jnp.dot(grad_gate[at, :], basis[...], preferred_element_type=jnp.float32)
        mid = jnp.dot(grad_up[at, :], basis[...], preferred_element_type=jnp.float32)
        top = gain * jnp.dot(hidden[...], basis[...], preferred_element_type=jnp.float32)
        for j, value in enumerate((low, mid, top)):
            coef[at, j * rank : (j + 1) * rank] = value
            coef_half[at, j * rank : (j + 1) * rank] = value.astype(jnp.bfloat16)

    def send_coef(i):
        coef_copy(i).start()

    def gather_sent():
        for piece in planar:
            for zz in range(depth):
                if not y_first[piece]:
                    side(piece, zz).wait_send()
                for yy in (y, 1 - y) if y_first[piece] else (y,):
                    pl.when((zz <= z) & (z < depth - 1))(
                        lambda p=piece, q=zz, yy=yy: up(p, q, yy).wait_send()
                    )
                    pl.when((zz >= z) & (z > 0))(
                        lambda p=piece, q=zz, yy=yy: down(p, q, yy).wait_send()
                    )
            if y_first[piece]:
                side(piece, z).wait_send()
        for piece in relayed:
            for pair in range(2 * depth):
                pl.when(pair != me // 2)(
                    lambda p=piece, q=pair: plane(p, q // 2, q % 2).wait_send()
                )
        for piece in range(len(pieces)):
            for pair in range(2 * depth):
                other(piece, pair // 2, pair % 2).wait_send()

    def remote(src, dst, send, recv, device):
        return pltpu.make_async_remote_copy(
            src_ref=src, dst_ref=dst, send_sem=send, recv_sem=recv,
            device_id=device, device_id_type=MESH,
        )

    crossed = [k for k, chunk in enumerate(chunks) if chunk[2]]

    def cols_of(k):
        return pl.ds(chunks[k][0], chunks[k][1])

    def sum_core_copy(k, i):
        pair = pl.ds(seq[i] * 2, 2)
        return remote(
            part.at[pair, 1 - core, :, cols_of(k)], from_core.at[pair, :, cols_of(k)],
            sum_core_sem.at[0, k, i], sum_core_sem.at[1, k, i], core_device,
        )

    def sum_side_copy(k, zz):
        return remote(
            part.at[zz * 2 + 1 - y, core, :, cols_of(k)], from_side.at[zz, :, cols_of(k)],
            sum_side_sem.at[0, k, zz], sum_side_sem.at[1, k, zz], side_device,
        )

    def sum_z_copy(k, zz, upward, flipped=False):
        way = 0 if upward else 1
        if flipped:
            number = crossed.index(k)
            landing = from_zb.at[way, zz, :, pl.ds(number * chunks[k][1], chunks[k][1])]
            number += len(chunks)
        else:
            number = k
            landing = from_z.at[way, zz, :, cols_of(k)]
        slot = zz * 2 + (1 - y if flipped else y)
        return remote(
            part.at[slot, core, :, cols_of(k)], landing,
            sum_z_sem.at[0, way, number, zz], sum_z_sem.at[1, way, number, zz],
            (dp, me + 4 if upward else me - 4),
        )

    def sum_plane_copy(k):
        start, size, _ = chunks[k]
        return remote(
            part.at[z * 2 + y, core, :, cols_of(k)], from_plane.at[:, pl.ds(start % half, size)],
            sum_plane_sem.at[0, k], sum_plane_sem.at[1, k], plane_device,
        )

    def add_into(slot, k, term):
        total = part[slot, core, :, cols_of(k)].astype(jnp.float32) + term.astype(jnp.float32)
        part[slot, core, :, cols_of(k)] = total.astype(jnp.bfloat16)

    def multiply(k, i):
        start, size, _ = chunks[k]
        at = rows_of(seq[i])

        @pl.loop(0, size // TILE)
        def _(n):
            cols = pl.ds(pl.multiple_of(start + n * TILE, TILE), TILE)
            rows_out = lax.dot_general(
                grad_gate[at, :], gate_w[cols, :], CONTRACT_LAST,
                preferred_element_type=jnp.float32,
            ) + lax.dot_general(
                grad_up[at, :], up_w[cols, :], CONTRACT_LAST,
                preferred_element_type=jnp.float32,
            )
            part[pl.ds(seq[i] * 2, 2), :, :, cols] = rows_out.astype(jnp.bfloat16).reshape(
                2, 2, rows, TILE
            )

        sum_core_copy(k, i).start()

    def over_cores(k, i):
        zz = seq[i]
        sum_core_copy(k, i).wait_recv()
        slot = zz * 2 + 1 - y
        add_into(slot, k, from_core[slot, :, cols_of(k)])
        if not chunks[k][2]:
            sum_side_copy(k, zz).start()
        slot = zz * 2 + y
        add_into(slot, k, from_core[slot, :, cols_of(k)])
        if chunks[k][2]:
            for flipped in (True, False):
                pl.when((z == 0) & (zz > 0))(
                    lambda f=flipped: sum_z_copy(k, zz, True, f).start()
                )
                pl.when((z == depth - 1) & (zz < z))(
                    lambda f=flipped: sum_z_copy(k, zz, False, f).start()
                )

    def z_term(k, zz, upward, flipped):
        sum_z_copy(k, zz, upward, flipped).wait_recv()
        if flipped:
            size = chunks[k][1]
            at = pl.ds(crossed.index(k) * size, size)
            term = from_zb[0 if upward else 1, zz, :, at]
        else:
            term = from_z[0 if upward else 1, zz, :, cols_of(k)]
        add_into(zz * 2 + (1 - y if flipped else y), k, term)

    def pass_on(k, hop, flipped=False):
        def climb():
            for zz in reversed(range(hop + 1, depth)):
                z_term(k, zz, True, flipped)
                sum_z_copy(k, zz, True, flipped).start()

        def sink():
            for zz in range(depth - 1 - hop):
                z_term(k, zz, False, flipped)
                sum_z_copy(k, zz, False, flipped).start()

        pl.when(z == hop)(climb)
        pl.when(z == depth - 1 - hop)(sink)

    def own_plane(k, flipped=False):
        pl.when(z > 0)(lambda: z_term(k, z, True, flipped))
        pl.when(z < depth - 1)(lambda: z_term(k, z, False, flipped))

    def over_side(k, i):
        zz = seq[i]
        sum_side_copy(k, zz).wait_recv()
        add_into(zz * 2 + y, k, from_side[zz, :, cols_of(k)])
        pl.when((z == 0) & (zz > 0))(lambda: sum_z_copy(k, zz, True).start())
        pl.when((z == depth - 1) & (zz < z))(lambda: sum_z_copy(k, zz, False).start())

    def leave(k):
        pl.when(dp != chunks[k][0] // half)(lambda: sum_plane_copy(k).start())

    def finish(k):
        own_plane(k)
        leave(k)

    def crossed_own(k, flipped):
        own_plane(k, flipped)
        if flipped:
            sum_side_copy(k, z).start()

    def crossed_side(k):
        sum_side_copy(k, z).wait_recv()
        add_into(z * 2 + y, k, from_side[z, :, cols_of(k)])
        leave(k)

    def turn_coef():
        for i in range(depth):
            coef_copy(i).wait_recv()
        coef_t[...] = (coef[...] + far_coef[...].astype(jnp.float32)).T.astype(jnp.bfloat16)

    def project():
        @pl.loop(0, half // TILE)
        def _(n):
            cols = pl.ds(pl.multiple_of(dp * half + n * TILE, TILE), TILE)
            at = pl.ds(pl.multiple_of(n * TILE, TILE), TILE)
            front = jnp.dot(
                coef_t[0 : 2 * rank, :], x_all[:, cols], preferred_element_type=jnp.float32
            ).T
            proj[0, at, :] = front[:, 0:rank]
            proj[1, at, :] = front[:, rank : 2 * rank]
            proj[2, at, :] = jnp.dot(
                coef_t[2 * rank : 3 * rank, :], y_all[:, cols], preferred_element_type=jnp.float32
            ).T

    def sums_sent(k):
        start, _, z_first = chunks[k]
        pl.when(dp != start // half)(lambda: sum_plane_copy(k).wait_send())
        for i in range(depth):
            sum_core_copy(k, i).wait_send()
        if z_first:
            sum_side_copy(k, z).wait_send()
        for zz in range(depth):
            if not z_first:
                sum_side_copy(k, zz).wait_send()
            for flipped in (False, True) if z_first else (False,):
                pl.when(zz > z)(lambda zz=zz, f=flipped: sum_z_copy(k, zz, True, f).wait_send())
                pl.when(zz < z)(lambda zz=zz, f=flipped: sum_z_copy(k, zz, False, f).wait_send())

    proj_copy = pltpu.make_async_copy(proj, proj_out, local_sem.at[6])

    def give_projected():
        project()
        proj_copy.start()

    stages = {
        "ow": send_own, "za": take_z, "sa": take_side, "fa": take_far, "fx": inner_forward,
        "fy": inner_backward, "cf": send_coef, "gw": gather_sent,
        "mm": multiply, "co": over_cores, "sd": over_side, "pz": pass_on, "fi": finish,
        "bz": pass_on, "bo": crossed_own, "bs": crossed_side, "tc": turn_coef, "pj": give_projected, "rw": sums_sent,
    }
    for stage, *at in plan:
        stages[stage](*at)

    for k, (start, size, _) in enumerate(chunks):
        def take_plane(k=k, start=start, size=size):
            sum_plane_copy(k).wait_recv()
            at = pl.ds(start % half, size)
            total = part[z * 2 + y, core, :, cols_of(k)].astype(jnp.float32) + from_plane[
                :, at
            ].astype(jnp.float32)
            grad_out[:, at] = total.astype(jnp.bfloat16)

        pl.when(dp == start // half)(take_plane)

    for i in range(depth):
        coef_copy(i).wait_send()
    proj_copy.wait()


def dense_form(
    saved_inputs, output_grad, routes, route_gates, expert_gate, expert_up, expert_down, proj_basis
):
    expert_count = lax.axis_size("expert")
    group_count = lax.axis_size("dp")
    rows, width = saved_inputs.shape
    all_rows = rows * expert_count
    hidden_width = expert_gate.shape[2]
    rank = proj_basis.shape[2]
    depth = expert_count // 4
    half = width // group_count
    layout = gather_layout(width)
    chunks = column_chunks(half)
    crossed_width = sum(size for _, size, z_first in chunks if z_first)
    dma = pltpu.SemaphoreType.DMA
    bf16, f32 = jnp.bfloat16, jnp.float32
    whole = pl.BlockSpec(memory_space=pl.ANY)
    held = pl.BlockSpec(memory_space=pltpu.VMEM)
    token_grad, terms = pl.pallas_call(
        functools.partial(
            fused_kernel, depth, layout, chunks, step_order(depth, layout, chunks)
        ),
        out_shape=[
            jax.ShapeDtypeStruct((rows, half), bf16),
            jax.ShapeDtypeStruct((3, half, rank), f32),
        ],
        in_specs=[whole, whole, held, held, whole, whole, whole, whole],
        out_specs=[held, whole],
        scratch_shapes=[
            pltpu.VMEM((3, half, rank), f32),
            pltpu.VMEM((all_rows, width), bf16),
            pltpu.VMEM((all_rows, width + LANES), bf16),
            pltpu.VMEM((width, hidden_width), bf16),
            pltpu.VMEM((width, hidden_width), bf16),
            pltpu.VMEM((hidden_width, width), bf16),
            pltpu.VMEM((hidden_width, rank), bf16),
            pltpu.VMEM((4 * rows, hidden_width), f32),
            pltpu.VMEM((4 * rows, hidden_width), f32),
            pltpu.VMEM((all_rows, hidden_width), bf16),
            pltpu.VMEM((all_rows, hidden_width), bf16),
            pltpu.VMEM((4 * rows, hidden_width), bf16),
            pltpu.VMEM((all_rows, 3 * rank), f32),
            pltpu.VMEM((all_rows, 3 * rank), bf16),
            pltpu.VMEM((all_rows, 3 * rank), bf16),
            pltpu.VMEM((3 * rank, all_rows), bf16),
            pltpu.VMEM((2 * depth, 2, rows, width), bf16),
            pltpu.VMEM((2 * depth, rows, width), bf16),
            pltpu.VMEM((depth, rows, width), bf16),
            pltpu.VMEM((2, depth, rows, width), bf16),
            pltpu.VMEM((2, depth, rows, crossed_width), bf16),
            pltpu.VMEM((rows, half), bf16),
            dma((len(layout) + 2, expert_count)),
            dma((len(layout), 2 * depth)),
            dma((len(layout), 2 * depth)),
            dma((len(layout), depth)),
            dma((2, 2 * depth)),
            dma((len(layout) + 2, 2 * depth)),
            dma((7,)),
            dma((2, depth)),
            dma((2, len(chunks), depth)),
            dma((2, len(chunks), depth)),
            dma((2, 2, len(chunks) + 2, depth)),
            dma((2, len(chunks))),
        ],
        compiler_params=pltpu.CompilerParams(
            collective_id=0, has_side_effects=True, vmem_limit_bytes=60 * 1024 * 1024
        ),
    )(
        saved_inputs, output_grad, routes.T, route_gates.T,
        expert_gate[0], expert_up[0], expert_down[0], proj_basis[0],
    )
    return (token_grad, terms.transpose(1, 0, 2)[None])


def on_device(*arrays):
    if lax.axis_size("expert") <= 2 * arrays[2].shape[1]:
        return dense_form(*arrays)
    return slot_form(*arrays)


def solution(mesh):
    placed = (
        P("expert", None),
        P("expert", None),
        P("expert", None),
        P("expert", None),
        P("expert", None, "dp"),
        P("expert", None, "dp"),
        P("expert", "dp", None),
        P("expert", "dp", None),
    )
    return jax.shard_map(
        on_device,
        mesh=mesh,
        in_specs=placed,
        out_specs=(P("expert", "dp"), P("expert", "dp", None, None)),
        check_vma=False,
    )
```

```python
import functools

import jax
import jax.numpy as jnp
from jax import lax
from jax.experimental import pallas as pl
from jax.experimental.pallas import tpu as pltpu
from jax.sharding import PartitionSpec as P


def slot_form(
    saved_inputs, output_grad, routes, route_gates, expert_gate, expert_up, expert_down, proj_basis
):
    token_count, model_width = saved_inputs.shape
    top_count = routes.shape[1]
    expert_count = lax.axis_size("expert")
    group_count = lax.axis_size("dp")
    capacity = token_count * top_count * 9 // (8 * expert_count)
    slot_count = expert_count * capacity
    column_width = model_width // group_count
    route_count = token_count * top_count
    flat_routes = routes.reshape(-1)
    position = jnp.arange(route_count, dtype=jnp.int32)
    earlier = jnp.sum(
        (
            (flat_routes[:, None] == flat_routes[None, :])
            & (position[None, :] < position[:, None])
        ).astype(jnp.int32),
        axis=1,
    )
    target_slot = flat_routes * capacity + earlier
    slot_owner = (
        jnp.full((slot_count,), route_count, jnp.int32)
        .at[target_slot]
        .set(jnp.arange(route_count, dtype=jnp.int32))
    )
    filled = slot_owner < route_count
    safe_route = jnp.minimum(slot_owner, route_count - 1)
    source_token = safe_route // top_count
    zero_half = jnp.zeros((), jnp.bfloat16)
    gate_slots = jnp.where(filled, route_gates.reshape(-1)[safe_route], zero_half).reshape(
        expert_count, capacity
    )
    token_map = (
        (source_token[None, :] == jnp.arange(token_count, dtype=jnp.int32)[:, None])
        & filled[None, :]
    ).astype(jnp.bfloat16)
    contract_first = (((0,), (0,)), ((), ()))

    def to_slots(source_rows):
        picked = lax.dot_general(
            token_map, source_rows, contract_first, preferred_element_type=jnp.float32
        ).astype(jnp.bfloat16)
        return picked.reshape(expert_count, capacity * source_rows.shape[1])

    recv_inputs, recv_grads, recv_gates = (
        lax.all_to_all(to_slots(saved_inputs), "expert", split_axis=0, concat_axis=0, tiled=True),
        lax.all_to_all(to_slots(output_grad), "expert", split_axis=0, concat_axis=0, tiled=True),
        lax.all_to_all(gate_slots, "expert", split_axis=0, concat_axis=0, tiled=True),
    )
    input_rows = recv_inputs.reshape(slot_count, model_width)
    grad_rows = recv_grads.reshape(slot_count, model_width)
    gain = recv_gates.reshape(slot_count, 1).astype(jnp.float32)
    gate_w = expert_gate[0]
    up_w = expert_up[0]
    down_w = expert_down[0]
    basis = proj_basis[0]
    rank_width = basis.shape[1]
    contract_last = (((1,), (1,)), ((), ()))
    pre_gate = jnp.dot(input_rows, gate_w, preferred_element_type=jnp.float32)
    pre_up = jnp.dot(input_rows, up_w, preferred_element_type=jnp.float32)
    grad_hidden = lax.dot_general(
        grad_rows, down_w, contract_last, preferred_element_type=jnp.float32
    )
    sigma = jax.nn.sigmoid(pre_gate)
    silu_val = pre_gate * sigma
    scaled = gain * grad_hidden
    grad_up = (scaled * silu_val).astype(jnp.bfloat16)
    grad_gate = (scaled * pre_up * sigma * (1.0 + pre_gate * (1.0 - sigma))).astype(jnp.bfloat16)
    hidden = (silu_val * pre_up).astype(jnp.bfloat16)
    part_rows = (
        lax.dot_general(grad_gate, gate_w, contract_last, preferred_element_type=jnp.float32)
        + lax.dot_general(grad_up, up_w, contract_last, preferred_element_type=jnp.float32)
    ).astype(jnp.bfloat16)
    coef_gate = jnp.dot(grad_gate, basis, preferred_element_type=jnp.float32).astype(jnp.bfloat16)
    coef_up = jnp.dot(grad_up, basis, preferred_element_type=jnp.float32).astype(jnp.bfloat16)
    coef_down = (gain * jnp.dot(hidden, basis, preferred_element_type=jnp.float32)).astype(
        jnp.bfloat16
    )
    coef_pair = jnp.concatenate([coef_gate, coef_up], axis=1)
    front = lax.dot_general(
        input_rows, coef_pair, contract_first, preferred_element_type=jnp.float32
    )
    rear = lax.dot_general(grad_rows, coef_down, contract_first, preferred_element_type=jnp.float32)
    summed_terms = lax.psum_scatter(
        jnp.concatenate([front, rear], axis=1).astype(jnp.bfloat16),
        "dp",
        scatter_dimension=0,
        tiled=True,
    ).astype(jnp.float32)
    projected = summed_terms.reshape(1, column_width, 3, rank_width)
    returned = lax.all_to_all(
        part_rows.reshape(expert_count, capacity * model_width),
        "expert",
        split_axis=0,
        concat_axis=0,
        tiled=True,
    )
    spread = jnp.dot(
        token_map, returned.reshape(slot_count, model_width), preferred_element_type=jnp.float32
    )
    token_grad = lax.psum_scatter(
        spread.astype(jnp.bfloat16), "dp", scatter_dimension=1, tiled=True
    )
    return (token_grad, projected)

MESH = pl.DeviceIdType.MESH
LANES = 128
TILE = 256
CONTRACT_LAST = (((1,), (1,)), ((), ()))


def column_chunks(half):
    tiles = half // TILE
    crossed = max(1, tiles // 7)
    straight = tiles - crossed
    sizes = [straight // 3 + (1 if i < straight % 3 else 0) for i in range(3)]
    chunks = []
    for side in range(2):
        start = side * half
        for size in [crossed] + sizes:
            chunks.append((start, size * TILE, start == side * half))
            start += size * TILE
    return chunks

PLAN = (
    ("ow", 0), ("ow", 1), ("sa", 0, 0), ("ow", 2), ("ow", 3), ("sa", 1, 0), ("sa", 2, 0),
    ("za", 0, 1), ("fa", 0, True, 0), ("za", 1, 1), ("fx", 0), ("sa", 3, 0), ("fa", 1, True, 0),
    ("za", 3, 1), ("fy", 0), ("mm", 7, 0), ("mm", 6, 0), ("mm", 0, 0), ("sa", 0, 1),
    ("mm", 4, 0), ("mm", 3, 0), ("za", 2, 1), ("mm", 5, 0), ("sa", 1, 1), ("mm", 2, 0),
    ("za", 0, 2), ("mm", 1, 0), ("fa", 0, False, 1), ("za", 1, 2), ("fa", 1, False, 1),
    ("fa", 0, True, 1), ("co", 4, 0), ("fx", 1), ("za", 3, 2), ("sa", 3, 1), ("co", 6, 0),
    ("fa", 1, True, 1), ("fy", 1), ("mm", 1, 1), ("mm", 4, 1), ("sa", 0, 2), ("co", 0, 0),
    ("mm", 7, 1), ("co", 2, 0), ("mm", 2, 1), ("za", 2, 2), ("sa", 1, 2), ("mm", 5, 1),
    ("mm", 3, 1), ("mm", 0, 1), ("co", 7, 1), ("za", 0, 3), ("fa", 0, False, 2), ("mm", 6, 1),
    ("fa", 1, False, 2), ("co", 4, 1), ("co", 2, 1), ("co", 3, 0), ("fa", 0, True, 2),
    ("sa", 3, 2), ("co", 1, 1), ("za", 1, 3), ("co", 6, 1), ("fx", 2), ("fa", 1, True, 2),
    ("za", 3, 3), ("co", 5, 1), ("co", 0, 1), ("co", 7, 0), ("sa", 0, 3), ("sd", 7, 1),
    ("fy", 2), ("mm", 4, 2), ("mm", 0, 2), ("mm", 3, 2), ("mm", 5, 2), ("mm", 2, 2),
    ("fa", 0, False, 3), ("fa", 1, False, 3), ("fa", 0, True, 3), ("za", 2, 3), ("sa", 1, 3),
    ("sd", 2, 1), ("sd", 1, 1), ("mm", 1, 2), ("sd", 6, 1), ("cf", 0), ("co", 4, 2),
    ("mm", 7, 2), ("fx", 3), ("co", 1, 2), ("fa", 1, True, 3), ("sa", 3, 3), ("co", 5, 2),
    ("co", 3, 2), ("co", 0, 2), ("fy", 3), ("mm", 7, 3), ("sd", 1, 2), ("cf", 3), ("mm", 4, 3),
    ("mm", 3, 3), ("co", 7, 3), ("mm", 1, 3), ("co", 4, 3), ("bz", 4, 1, True), ("co", 3, 3),
    ("mm", 6, 2), ("sd", 3, 2), ("cf", 1), ("co", 1, 3), ("bz", 4, 1, False), ("mm", 0, 3),
    ("mm", 6, 3), ("mm", 2, 3), ("co", 0, 3), ("co", 7, 2), ("bz", 0, 1, True), ("mm", 5, 3),
    ("bz", 0, 1, False), ("co", 3, 1), ("sd", 3, 3), ("pz", 3, 1), ("co", 5, 3),
    ("bz", 4, 2, False), ("sd", 1, 3), ("sd", 5, 2), ("co", 6, 3), ("co", 6, 2), ("pz", 1, 1),
    ("cf", 2), ("co", 1, 0), ("sd", 7, 2), ("bz", 4, 2, True), ("bz", 0, 2, True), ("gw",),
    ("sd", 5, 3), ("pz", 5, 1), ("co", 2, 3), ("sd", 7, 3), ("pz", 7, 1), ("sd", 6, 3),
    ("co", 5, 0), ("sd", 3, 1), ("pz", 3, 2), ("tc",), ("bo", 4, True), ("pz", 1, 2),
    ("bz", 0, 2, False), ("co", 2, 2), ("sd", 6, 2), ("sd", 5, 1), ("bo", 0, True), ("pz", 5, 2),
    ("pz", 6, 1), ("pj",), ("pz", 7, 2), ("sd", 2, 3), ("sd", 2, 2), ("pz", 2, 1),
    ("bo", 0, False), ("bo", 4, False), ("pz", 6, 2), ("sd", 1, 0), ("fi", 1), ("sd", 3, 0),
    ("bs", 4), ("fi", 3), ("sd", 7, 0), ("fi", 7), ("bs", 0), ("pz", 2, 2), ("rw", 1),
    ("sd", 6, 0), ("sd", 5, 0), ("fi", 6), ("fi", 5), ("rw", 5), ("rw", 4), ("sd", 2, 0),
    ("fi", 2), ("rw", 2), ("rw", 6), ("rw", 7), ("rw", 3), ("rw", 0),
)


def step_order(depth, layout, chunks):
    planar = range(len(layout))
    hops = range(1, depth - 1)
    steps = [("ow", p) for p in planar]
    for d in range(depth):
        steps += [("za", p, d) for p in planar if d]
        steps += [("sa", p, d) for p in planar if d == 0 or layout[p][0][0] != "b"]
        steps += [("fa", p, f, d) for p in range(2) for f in (False, True) if d or f]
        steps += [("fx", d), ("fy", d)]
    steps += [("gw",)] + [("cf", i) for i in range(depth)] + [("tc",), ("pj",)]
    for k, (_, _, z_first) in enumerate(chunks):
        steps += [("mm", k, i) for i in range(depth)] + [("co", k, i) for i in range(depth)]
        if z_first:
            steps += [("bz", k, hop, flipped) for flipped in (True, False) for hop in hops]
            steps += [("bo", k, True), ("bo", k, False), ("bs", k)]
        else:
            steps += [("sd", k, i) for i in reversed(range(depth))]
            steps += [("pz", k, hop) for hop in hops] + [("fi", k)]
        steps += [("rw", k)]
    return PLAN if sorted(map(str, PLAN)) == sorted(map(str, steps)) else steps


def gather_layout(width):
    tiles = width // LANES
    shares = (
        (("o", 0), 0, 10),
        (("o", 1), 0, 8),
        (("b", 0), 20, 8),
        (("a", 2), 16, 12),
    )
    unit = tiles // 28
    pieces = []
    for kind, start, size in shares:
        last = kind[0] != "o" and start + size == 28
        first = start * unit * LANES
        stop = width if last else first + size * unit * LANES
        pieces.append((kind, first, stop - first + (LANES if kind[1] == 2 else 0)))
    return pieces


def fused_kernel(
    depth, layout, chunks, plan, x_in, y_in, routes, gates, gate_in, up_in, down_in, basis_in,
    grad_out, proj_out,
    proj,
    x_all, y_all, gate_w, up_w, down_w, basis, pre_gate, pre_up, grad_gate, grad_up, hidden,
    coef, coef_half, far_coef, coef_t, part, from_core, from_side, from_z, from_zb, from_plane,
    recv_sem, up_sem, down_sem, side_sem, plane_sem, core_sem, local_sem, coef_sem,
    sum_core_sem, sum_side_sem, sum_z_sem, sum_plane_sem,
):
    dp = lax.axis_index("dp")
    me = lax.axis_index("expert")
    z, y, core = me // 4, (me // 2) % 2, me % 2
    rows, width = x_in.shape
    half = width // 2
    hidden_width = gate_w.shape[1]
    rank = basis.shape[1]
    plane_rows = 4 * rows
    core_device = (dp, z * 4 + y * 2 + 1 - core)
    side_device = (dp, z * 4 + (1 - y) * 2 + core)
    plane_device = (1 - dp, me)
    order = [
        sorted(range(depth), key=lambda q, p=p: (abs(q - p), q if 2 * p < depth else -q))
        for p in range(depth)
    ]
    seq = [
        sum(jnp.where(z == p, order[p][i], 0) for p in range(depth)) for i in range(depth)
    ]

    pieces = []
    for kind, start, size in layout:
        source, whole = ((x_in, x_all), (y_in, y_all), (None, y_all))[kind[1]]
        if kind[0] == "o":
            cols = pl.ds(pl.multiple_of(dp * size, LANES), size)
        else:
            cols = pl.ds(start, size)
        pieces.append((source, whole, cols))
    for kind, start, size in layout[:2]:
        source, whole = ((x_in, x_all), (y_in, y_all))[kind[1]]
        pieces.append((source, whole, pl.ds(pl.multiple_of((1 - dp) * size, LANES), size)))
    planar = range(len(layout))
    relayed = range(2)
    far = len(layout)
    y_first = [kind[0] == "b" for kind, _, _ in layout]

    def index(zz, yy, cc):
        return zz * 4 + yy * 2 + cc

    def item_rows(item):
        return pl.ds(pl.multiple_of(item * rows, rows), rows)

    def landed(piece, item):
        _, whole, cols = pieces[piece]
        return whole.at[item_rows(item), cols]

    def copy(piece, item, own, sem, device, recv_piece):
        start, _, cols = pieces[piece]
        src = start.at[:, cols] if own and start is not None else landed(piece, item)
        return pltpu.make_async_remote_copy(
            src_ref=src,
            dst_ref=landed(piece, item),
            send_sem=sem,
            recv_sem=recv_sem.at[recv_piece, item],
            device_id=device,
            device_id_type=MESH,
        )

    def up(piece, zz, yy, own=False):
        item = index(zz, yy, core)
        return copy(piece, item, own, up_sem.at[piece, item // 2], (dp, me + 4), piece)

    def down(piece, zz, yy, own=False):
        item = index(zz, yy, core)
        return copy(piece, item, own, down_sem.at[piece, item // 2], (dp, me - 4), piece)

    def side(piece, zz, own=False):
        return copy(piece, index(zz, y, core), own, side_sem.at[piece, zz], side_device, piece)

    def plane(piece, zz, yy):
        item = index(zz, yy, core)
        return copy(piece, item, False, plane_sem.at[piece, item // 2], plane_device, far + piece)

    def other(piece, zz, yy, own=False):
        item = index(zz, yy, core)
        return copy(piece, item, own, core_sem.at[piece, item // 2], core_device, piece)

    def arrive(piece, item):
        copy(piece, item, False, core_sem.at[0, 0], (dp, me), piece).wait_recv()

    own_loads = [
        pltpu.make_async_copy(a, b, local_sem.at[i])
        for i, (a, b) in enumerate((
            (y_in, y_all.at[item_rows(me), pl.ds(0, width)]), (x_in, x_all.at[item_rows(me), :]),
            (gate_in, gate_w), (up_in, up_w), (down_in, down_w), (basis_in, basis),
        ))
    ]
    for one in own_loads:
        one.start()

    lane = lax.broadcasted_iota(jnp.int32, (LANES, rows), 0)
    table = jnp.zeros((LANES, rows), jnp.float32)
    for k in range(routes.shape[0]):
        table = table + jnp.where(
            routes[k : k + 1, :] == lane, gates[k : k + 1, :].astype(jnp.float32), 0.0
        )
    y_all[item_rows(me), width : width + LANES] = table.T.astype(jnp.bfloat16)

    barrier = pltpu.get_barrier_semaphore()

    def greet(device):
        pl.semaphore_signal(barrier, inc=1, device_id=device, device_id_type=MESH)

    greet(plane_device)
    greet(side_device)
    greet(core_device)
    pl.when(z > 0)(lambda: greet((dp, me - 4)))
    pl.when(z < depth - 1)(lambda: greet((dp, me + 4)))
    pl.semaphore_wait(barrier, 3 + jnp.minimum(z, 1) + jnp.minimum(depth - 1 - z, 1))

    def spots(away):
        if away == 0:
            return [(z, None)]
        return [(z - away, z >= away), (z + away, z + away < depth)]

    def guarded(condition, act):
        act() if condition is None else pl.when(condition)(act)

    def rise(piece, zz, yy, own=False):
        pl.when(z < depth - 1)(lambda: up(piece, zz, yy, own).start())

    def fall(piece, zz, yy, own=False):
        pl.when(z > 0)(lambda: down(piece, zz, yy, own).start())

    def send_own(piece):
        if pieces[piece][0] is None:
            own_loads[0].wait()
        side(piece, z, True).start()
        rise(piece, z, y, True)
        fall(piece, z, y, True)
        other(piece, z, y, True).start()
        if piece in relayed:
            other(far + piece, z, y, True).start()

    def take_z(piece, away):
        for (zz, there), onward in zip(spots(away), (rise, fall)):
            def act(zz=zz, onward=onward):
                for yy in (y, 1 - y) if y_first[piece] else (y,):
                    arrive(piece, index(zz, yy, core))
                    if not y_first[piece]:
                        side(piece, zz).start()
                    onward(piece, zz, yy)
                    if piece in relayed:
                        plane(piece, zz, yy).start()
                    other(piece, zz, yy).start()

            guarded(there, act)

    def take_side(piece, away):
        for zz, there in spots(away):
            def act(zz=zz):
                arrive(piece, index(zz, 1 - y, core))
                if y_first[piece]:
                    rise(piece, zz, 1 - y)
                    fall(piece, zz, 1 - y)
                if piece in relayed:
                    plane(piece, zz, 1 - y).start()
                other(piece, zz, 1 - y).start()

            guarded(there, act)

    def take_far(piece, flipped, away):
        yy = 1 - y if flipped else y
        for zz, there in spots(away):
            def act(zz=zz):
                arrive(far + piece, index(zz, yy, core))
                other(far + piece, zz, yy).start()

            guarded(there, act)

    def take_core(kinds, away):
        numbers = [p for p, (kind, _, _) in enumerate(layout) if kind[1] in kinds]
        numbers += [far + p for p in numbers if p in relayed]
        for zz, there in spots(away):
            def act(zz=zz):
                for each in numbers:
                    arrive(each, index(zz, 0, 1 - core))
                    arrive(each, index(zz, 1, 1 - core))

            guarded(there, act)

    def rows_of(zz):
        return pl.ds(pl.multiple_of(zz * plane_rows, plane_rows), plane_rows)

    def coef_copy(i):
        return pltpu.make_async_remote_copy(
            src_ref=coef_half.at[rows_of(seq[i]), :],
            dst_ref=far_coef.at[rows_of(seq[i]), :],
            send_sem=coef_sem.at[0, i],
            recv_sem=coef_sem.at[1, i],
            device_id=plane_device,
            device_id_type=MESH,
        )

    def inner_forward(i):
        if i == 0:
            for one in own_loads[1:]:
                one.wait()
        take_core((0,), i)
        at = rows_of(seq[i])

        @pl.loop(0, hidden_width // TILE)
        def _(n):
            cols = pl.ds(pl.multiple_of(n * TILE, TILE), TILE)
            pre_gate[:, cols] = jnp.dot(
                x_all[at, :], gate_w[:, cols], preferred_element_type=jnp.float32
            )
            pre_up[:, cols] = jnp.dot(
                x_all[at, :], up_w[:, cols], preferred_element_type=jnp.float32
            )

    def inner_backward(i):
        take_core((1, 2), i)
        at = rows_of(seq[i])
        expert = lax.broadcasted_iota(jnp.int32, (plane_rows, LANES), 1)
        gain = jnp.sum(
            jnp.where(expert == me, y_all[at, width : width + LANES].astype(jnp.float32), 0.0),
            axis=1,
            keepdims=True,
        )

        @pl.loop(0, hidden_width // TILE)
        def _(n):
            cols = pl.ds(pl.multiple_of(n * TILE, TILE), TILE)
            grad_hidden = lax.dot_general(
                y_all[at, 0:width], down_w[cols, :], CONTRACT_LAST, preferred_element_type=jnp.float32
            )
            a = pre_gate[:, cols]
            u = pre_up[:, cols]
            sigma = jax.nn.sigmoid(a)
            silu = a * sigma
            scaled = gain * grad_hidden
            grad_up[at, cols] = (scaled * silu).astype(jnp.bfloat16)
            grad_gate[at, cols] = (scaled * u * sigma * (1.0 + a * (1.0 - sigma))).astype(
                jnp.bfloat16
            )
            hidden[:, cols] = (silu * u).astype(jnp.bfloat16)

        low = jnp.dot(grad_gate[at, :], basis[...], preferred_element_type=jnp.float32)
        mid = jnp.dot(grad_up[at, :], basis[...], preferred_element_type=jnp.float32)
        top = gain * jnp.dot(hidden[...], basis[...], preferred_element_type=jnp.float32)
        for j, value in enumerate((low, mid, top)):
            coef[at, j * rank : (j + 1) * rank] = value
            coef_half[at, j * rank : (j + 1) * rank] = value.astype(jnp.bfloat16)

    def send_coef(i):
        coef_copy(i).start()

    def gather_sent():
        for piece in planar:
            for zz in range(depth):
                if not y_first[piece]:
                    side(piece, zz).wait_send()
                for yy in (y, 1 - y) if y_first[piece] else (y,):
                    pl.when((zz <= z) & (z < depth - 1))(
                        lambda p=piece, q=zz, yy=yy: up(p, q, yy).wait_send()
                    )
                    pl.when((zz >= z) & (z > 0))(
                        lambda p=piece, q=zz, yy=yy: down(p, q, yy).wait_send()
                    )
            if y_first[piece]:
                side(piece, z).wait_send()
        for piece in relayed:
            for pair in range(2 * depth):
                pl.when(pair != me // 2)(
                    lambda p=piece, q=pair: plane(p, q // 2, q % 2).wait_send()
                )
        for piece in range(len(pieces)):
            for pair in range(2 * depth):
                other(piece, pair // 2, pair % 2).wait_send()

    def remote(src, dst, send, recv, device):
        return pltpu.make_async_remote_copy(
            src_ref=src, dst_ref=dst, send_sem=send, recv_sem=recv,
            device_id=device, device_id_type=MESH,
        )

    crossed = [k for k, chunk in enumerate(chunks) if chunk[2]]

    def cols_of(k):
        return pl.ds(chunks[k][0], chunks[k][1])

    def sum_core_copy(k, i):
        pair = pl.ds(seq[i] * 2, 2)
        return remote(
            part.at[pair, 1 - core, :, cols_of(k)], from_core.at[pair, :, cols_of(k)],
            sum_core_sem.at[0, k, i], sum_core_sem.at[1, k, i], core_device,
        )

    def sum_side_copy(k, zz):
        return remote(
            part.at[zz * 2 + 1 - y, core, :, cols_of(k)], from_side.at[zz, :, cols_of(k)],
            sum_side_sem.at[0, k, zz], sum_side_sem.at[1, k, zz], side_device,
        )

    def sum_z_copy(k, zz, upward, flipped=False):
        way = 0 if upward else 1
        if flipped:
            number = crossed.index(k)
            landing = from_zb.at[way, zz, :, pl.ds(number * chunks[k][1], chunks[k][1])]
            number += len(chunks)
        else:
            number = k
            landing = from_z.at[way, zz, :, cols_of(k)]
        slot = zz * 2 + (1 - y if flipped else y)
        return remote(
            part.at[slot, core, :, cols_of(k)], landing,
            sum_z_sem.at[0, way, number, zz], sum_z_sem.at[1, way, number, zz],
            (dp, me + 4 if upward else me - 4),
        )

    def sum_plane_copy(k):
        start, size, _ = chunks[k]
        return remote(
            part.at[z * 2 + y, core, :, cols_of(k)], from_plane.at[:, pl.ds(start % half, size)],
            sum_plane_sem.at[0, k], sum_plane_sem.at[1, k], plane_device,
        )

    def add_into(slot, k, term):
        total = part[slot, core, :, cols_of(k)].astype(jnp.float32) + term.astype(jnp.float32)
        part[slot, core, :, cols_of(k)] = total.astype(jnp.bfloat16)

    def multiply(k, i):
        start, size, _ = chunks[k]
        at = rows_of(seq[i])

        @pl.loop(0, size // TILE)
        def _(n):
            cols = pl.ds(pl.multiple_of(start + n * TILE, TILE), TILE)
            rows_out = lax.dot_general(
                grad_gate[at, :], gate_w[cols, :], CONTRACT_LAST,
                preferred_element_type=jnp.float32,
            ) + lax.dot_general(
                grad_up[at, :], up_w[cols, :], CONTRACT_LAST,
                preferred_element_type=jnp.float32,
            )
            part[pl.ds(seq[i] * 2, 2), :, :, cols] = rows_out.astype(jnp.bfloat16).reshape(
                2, 2, rows, TILE
            )

        sum_core_copy(k, i).start()

    def over_cores(k, i):
        zz = seq[i]
        sum_core_copy(k, i).wait_recv()
        slot = zz * 2 + 1 - y
        add_into(slot, k, from_core[slot, :, cols_of(k)])
        if not chunks[k][2]:
            sum_side_copy(k, zz).start()
        slot = zz * 2 + y
        add_into(slot, k, from_core[slot, :, cols_of(k)])
        if chunks[k][2]:
            for flipped in (True, False):
                pl.when((z == 0) & (zz > 0))(
                    lambda f=flipped: sum_z_copy(k, zz, True, f).start()
                )
                pl.when((z == depth - 1) & (zz < z))(
                    lambda f=flipped: sum_z_copy(k, zz, False, f).start()
                )

    def z_term(k, zz, upward, flipped):
        sum_z_copy(k, zz, upward, flipped).wait_recv()
        if flipped:
            size = chunks[k][1]
            at = pl.ds(crossed.index(k) * size, size)
            term = from_zb[0 if upward else 1, zz, :, at]
        else:
            term = from_z[0 if upward else 1, zz, :, cols_of(k)]
        add_into(zz * 2 + (1 - y if flipped else y), k, term)

    def pass_on(k, hop, flipped=False):
        def climb():
            for zz in reversed(range(hop + 1, depth)):
                z_term(k, zz, True, flipped)
                sum_z_copy(k, zz, True, flipped).start()

        def sink():
            for zz in range(depth - 1 - hop):
                z_term(k, zz, False, flipped)
                sum_z_copy(k, zz, False, flipped).start()

        pl.when(z == hop)(climb)
        pl.when(z == depth - 1 - hop)(sink)

    def own_plane(k, flipped=False):
        pl.when(z > 0)(lambda: z_term(k, z, True, flipped))
        pl.when(z < depth - 1)(lambda: z_term(k, z, False, flipped))

    def over_side(k, i):
        zz = seq[i]
        sum_side_copy(k, zz).wait_recv()
        add_into(zz * 2 + y, k, from_side[zz, :, cols_of(k)])
        pl.when((z == 0) & (zz > 0))(lambda: sum_z_copy(k, zz, True).start())
        pl.when((z == depth - 1) & (zz < z))(lambda: sum_z_copy(k, zz, False).start())

    def leave(k):
        pl.when(dp != chunks[k][0] // half)(lambda: sum_plane_copy(k).start())

    def finish(k):
        own_plane(k)
        leave(k)

    def crossed_own(k, flipped):
        own_plane(k, flipped)
        if flipped:
            sum_side_copy(k, z).start()

    def crossed_side(k):
        sum_side_copy(k, z).wait_recv()
        add_into(z * 2 + y, k, from_side[z, :, cols_of(k)])
        leave(k)

    def turn_coef():
        for i in range(depth):
            coef_copy(i).wait_recv()
        coef_t[...] = (coef[...] + far_coef[...].astype(jnp.float32)).T.astype(jnp.bfloat16)

    def project():
        @pl.loop(0, half // TILE)
        def _(n):
            cols = pl.ds(pl.multiple_of(dp * half + n * TILE, TILE), TILE)
            at = pl.ds(pl.multiple_of(n * TILE, TILE), TILE)
            front = jnp.dot(
                coef_t[0 : 2 * rank, :], x_all[:, cols], preferred_element_type=jnp.float32
            ).T.astype(jnp.bfloat16)
            proj[0, at, :] = front[:, 0:rank]
            proj[1, at, :] = front[:, rank : 2 * rank]
            proj[2, at, :] = jnp.dot(
                coef_t[2 * rank : 3 * rank, :], y_all[:, cols], preferred_element_type=jnp.float32
            ).T.astype(jnp.bfloat16)

    def sums_sent(k):
        start, _, z_first = chunks[k]
        pl.when(dp != start // half)(lambda: sum_plane_copy(k).wait_send())
        for i in range(depth):
            sum_core_copy(k, i).wait_send()
        if z_first:
            sum_side_copy(k, z).wait_send()
        for zz in range(depth):
            if not z_first:
                sum_side_copy(k, zz).wait_send()
            for flipped in (False, True) if z_first else (False,):
                pl.when(zz > z)(lambda zz=zz, f=flipped: sum_z_copy(k, zz, True, f).wait_send())
                pl.when(zz < z)(lambda zz=zz, f=flipped: sum_z_copy(k, zz, False, f).wait_send())

    proj_copy = pltpu.make_async_copy(proj, proj_out, local_sem.at[6])

    def give_projected():
        project()
        proj_copy.start()

    stages = {
        "ow": send_own, "za": take_z, "sa": take_side, "fa": take_far, "fx": inner_forward,
        "fy": inner_backward, "cf": send_coef, "gw": gather_sent,
        "mm": multiply, "co": over_cores, "sd": over_side, "pz": pass_on, "fi": finish,
        "bz": pass_on, "bo": crossed_own, "bs": crossed_side, "tc": turn_coef, "pj": give_projected, "rw": sums_sent,
    }
    for stage, *at in plan:
        stages[stage](*at)

    for k, (start, size, _) in enumerate(chunks):
        def take_plane(k=k, start=start, size=size):
            sum_plane_copy(k).wait_recv()
            at = pl.ds(start % half, size)
            total = part[z * 2 + y, core, :, cols_of(k)].astype(jnp.float32) + from_plane[
                :, at
            ].astype(jnp.float32)
            grad_out[:, at] = total.astype(jnp.bfloat16)

        pl.when(dp == start // half)(take_plane)

    for i in range(depth):
        coef_copy(i).wait_send()
    proj_copy.wait()


def dense_form(
    saved_inputs, output_grad, routes, route_gates, expert_gate, expert_up, expert_down, proj_basis
):
    expert_count = lax.axis_size("expert")
    group_count = lax.axis_size("dp")
    rows, width = saved_inputs.shape
    all_rows = rows * expert_count
    hidden_width = expert_gate.shape[2]
    rank = proj_basis.shape[2]
    depth = expert_count // 4
    half = width // group_count
    layout = gather_layout(width)
    chunks = column_chunks(half)
    crossed_width = sum(size for _, size, z_first in chunks if z_first)
    dma = pltpu.SemaphoreType.DMA
    bf16, f32 = jnp.bfloat16, jnp.float32
    whole = pl.BlockSpec(memory_space=pl.ANY)
    held = pl.BlockSpec(memory_space=pltpu.VMEM)
    token_grad, terms = pl.pallas_call(
        functools.partial(
            fused_kernel, depth, layout, chunks, step_order(depth, layout, chunks)
        ),
        out_shape=[
            jax.ShapeDtypeStruct((rows, half), bf16),
            jax.ShapeDtypeStruct((3, half, rank), bf16),
        ],
        in_specs=[whole, whole, held, held, whole, whole, whole, whole],
        out_specs=[held, whole],
        scratch_shapes=[
            pltpu.VMEM((3, half, rank), bf16),
            pltpu.VMEM((all_rows, width), bf16),
            pltpu.VMEM((all_rows, width + LANES), bf16),
            pltpu.VMEM((width, hidden_width), bf16),
            pltpu.VMEM((width, hidden_width), bf16),
            pltpu.VMEM((hidden_width, width), bf16),
            pltpu.VMEM((hidden_width, rank), bf16),
            pltpu.VMEM((4 * rows, hidden_width), f32),
            pltpu.VMEM((4 * rows, hidden_width), f32),
            pltpu.VMEM((all_rows, hidden_width), bf16),
            pltpu.VMEM((all_rows, hidden_width), bf16),
            pltpu.VMEM((4 * rows, hidden_width), bf16),
            pltpu.VMEM((all_rows, 3 * rank), f32),
            pltpu.VMEM((all_rows, 3 * rank), bf16),
            pltpu.VMEM((all_rows, 3 * rank), bf16),
            pltpu.VMEM((3 * rank, all_rows), bf16),
            pltpu.VMEM((2 * depth, 2, rows, width), bf16),
            pltpu.VMEM((2 * depth, rows, width), bf16),
            pltpu.VMEM((depth, rows, width), bf16),
            pltpu.VMEM((2, depth, rows, width), bf16),
            pltpu.VMEM((2, depth, rows, crossed_width), bf16),
            pltpu.VMEM((rows, half), bf16),
            dma((len(layout) + 2, expert_count)),
            dma((len(layout), 2 * depth)),
            dma((len(layout), 2 * depth)),
            dma((len(layout), depth)),
            dma((2, 2 * depth)),
            dma((len(layout) + 2, 2 * depth)),
            dma((7,)),
            dma((2, depth)),
            dma((2, len(chunks), depth)),
            dma((2, len(chunks), depth)),
            dma((2, 2, len(chunks) + 2, depth)),
            dma((2, len(chunks))),
        ],
        compiler_params=pltpu.CompilerParams(
            collective_id=0, has_side_effects=True, vmem_limit_bytes=60 * 1024 * 1024
        ),
    )(
        saved_inputs, output_grad, routes.T, route_gates.T,
        expert_gate[0], expert_up[0], expert_down[0], proj_basis[0],
    )
    return (token_grad, terms.astype(f32).transpose(1, 0, 2)[None])


def on_device(*arrays):
    if lax.axis_size("expert") <= 2 * arrays[2].shape[1]:
        return dense_form(*arrays)
    return slot_form(*arrays)


def solution(mesh):
    placed = (
        P("expert", None),
        P("expert", None),
        P("expert", None),
        P("expert", None),
        P("expert", None, "dp"),
        P("expert", None, "dp"),
        P("expert", "dp", None),
        P("expert", "dp", None),
    )
    return jax.shard_map(
        on_device,
        mesh=mesh,
        in_specs=placed,
        out_specs=(P("expert", "dp"), P("expert", "dp", None, None)),
        check_vma=False,
    )
```

```python
import functools

import jax
import jax.numpy as jnp
from jax import lax
from jax.experimental import pallas as pl
from jax.experimental.pallas import tpu as pltpu
from jax.sharding import PartitionSpec as P


def slot_form(
    saved_inputs, output_grad, routes, route_gates, expert_gate, expert_up, expert_down, proj_basis
):
    token_count, model_width = saved_inputs.shape
    top_count = routes.shape[1]
    expert_count = lax.axis_size("expert")
    group_count = lax.axis_size("dp")
    capacity = token_count * top_count * 9 // (8 * expert_count)
    slot_count = expert_count * capacity
    column_width = model_width // group_count
    route_count = token_count * top_count
    flat_routes = routes.reshape(-1)
    position = jnp.arange(route_count, dtype=jnp.int32)
    earlier = jnp.sum(
        (
            (flat_routes[:, None] == flat_routes[None, :])
            & (position[None, :] < position[:, None])
        ).astype(jnp.int32),
        axis=1,
    )
    target_slot = flat_routes * capacity + earlier
    slot_owner = (
        jnp.full((slot_count,), route_count, jnp.int32)
        .at[target_slot]
        .set(jnp.arange(route_count, dtype=jnp.int32))
    )
    filled = slot_owner < route_count
    safe_route = jnp.minimum(slot_owner, route_count - 1)
    source_token = safe_route // top_count
    zero_half = jnp.zeros((), jnp.bfloat16)
    gate_slots = jnp.where(filled, route_gates.reshape(-1)[safe_route], zero_half).reshape(
        expert_count, capacity
    )
    token_map = (
        (source_token[None, :] == jnp.arange(token_count, dtype=jnp.int32)[:, None])
        & filled[None, :]
    ).astype(jnp.bfloat16)
    contract_first = (((0,), (0,)), ((), ()))

    def to_slots(source_rows):
        picked = lax.dot_general(
            token_map, source_rows, contract_first, preferred_element_type=jnp.float32
        ).astype(jnp.bfloat16)
        return picked.reshape(expert_count, capacity * source_rows.shape[1])

    recv_inputs, recv_grads, recv_gates = (
        lax.all_to_all(to_slots(saved_inputs), "expert", split_axis=0, concat_axis=0, tiled=True),
        lax.all_to_all(to_slots(output_grad), "expert", split_axis=0, concat_axis=0, tiled=True),
        lax.all_to_all(gate_slots, "expert", split_axis=0, concat_axis=0, tiled=True),
    )
    input_rows = recv_inputs.reshape(slot_count, model_width)
    grad_rows = recv_grads.reshape(slot_count, model_width)
    gain = recv_gates.reshape(slot_count, 1).astype(jnp.float32)
    gate_w = expert_gate[0]
    up_w = expert_up[0]
    down_w = expert_down[0]
    basis = proj_basis[0]
    rank_width = basis.shape[1]
    contract_last = (((1,), (1,)), ((), ()))
    pre_gate = jnp.dot(input_rows, gate_w, preferred_element_type=jnp.float32)
    pre_up = jnp.dot(input_rows, up_w, preferred_element_type=jnp.float32)
    grad_hidden = lax.dot_general(
        grad_rows, down_w, contract_last, preferred_element_type=jnp.float32
    )
    sigma = jax.nn.sigmoid(pre_gate)
    silu_val = pre_gate * sigma
    scaled = gain * grad_hidden
    grad_up = (scaled * silu_val).astype(jnp.bfloat16)
    grad_gate = (scaled * pre_up * sigma * (1.0 + pre_gate * (1.0 - sigma))).astype(jnp.bfloat16)
    hidden = (silu_val * pre_up).astype(jnp.bfloat16)
    part_rows = (
        lax.dot_general(grad_gate, gate_w, contract_last, preferred_element_type=jnp.float32)
        + lax.dot_general(grad_up, up_w, contract_last, preferred_element_type=jnp.float32)
    ).astype(jnp.bfloat16)
    coef_gate = jnp.dot(grad_gate, basis, preferred_element_type=jnp.float32).astype(jnp.bfloat16)
    coef_up = jnp.dot(grad_up, basis, preferred_element_type=jnp.float32).astype(jnp.bfloat16)
    coef_down = (gain * jnp.dot(hidden, basis, preferred_element_type=jnp.float32)).astype(
        jnp.bfloat16
    )
    coef_pair = jnp.concatenate([coef_gate, coef_up], axis=1)
    front = lax.dot_general(
        input_rows, coef_pair, contract_first, preferred_element_type=jnp.float32
    )
    rear = lax.dot_general(grad_rows, coef_down, contract_first, preferred_element_type=jnp.float32)
    summed_terms = lax.psum_scatter(
        jnp.concatenate([front, rear], axis=1).astype(jnp.bfloat16),
        "dp",
        scatter_dimension=0,
        tiled=True,
    ).astype(jnp.float32)
    projected = summed_terms.reshape(1, column_width, 3, rank_width)
    returned = lax.all_to_all(
        part_rows.reshape(expert_count, capacity * model_width),
        "expert",
        split_axis=0,
        concat_axis=0,
        tiled=True,
    )
    spread = jnp.dot(
        token_map, returned.reshape(slot_count, model_width), preferred_element_type=jnp.float32
    )
    token_grad = lax.psum_scatter(
        spread.astype(jnp.bfloat16), "dp", scatter_dimension=1, tiled=True
    )
    return (token_grad, projected)

MESH = pl.DeviceIdType.MESH
LANES = 128
TILE = 256
CONTRACT_LAST = (((1,), (1,)), ((), ()))


def column_chunks(half):
    tiles = half // TILE
    crossed = max(1, tiles // 7)
    straight = tiles - crossed
    sizes = [straight // 3 + (1 if i < straight % 3 else 0) for i in range(3)]
    chunks = []
    for side in range(2):
        start = side * half
        for size in [crossed] + sizes:
            chunks.append((start, size * TILE, start == side * half))
            start += size * TILE
    return chunks

PLAN = (
    ("ow", 0), ("ow", 1), ("ow", 2), ("sa", 0, 0), ("sa", 1, 0), ("ow", 3), ("sa", 2, 0),
    ("za", 0, 1), ("za", 1, 1), ("fa", 0, True, 0), ("fx", 0), ("sa", 3, 0), ("fa", 1, True, 0),
    ("fy", 0), ("za", 3, 1), ("mm", 4, 0), ("sa", 0, 1), ("mm", 1, 0), ("za", 2, 1),
    ("mm", 3, 0), ("fa", 0, False, 1), ("mm", 6, 0), ("sa", 1, 1), ("za", 0, 2), ("mm", 7, 0),
    ("mm", 0, 0), ("fa", 1, False, 1), ("za", 1, 2), ("mm", 5, 0), ("fa", 0, True, 1),
    ("mm", 2, 0), ("fx", 1), ("za", 3, 2), ("sa", 3, 1), ("co", 0, 0), ("co", 6, 0),
    ("co", 2, 0), ("fa", 1, True, 1), ("fy", 1), ("mm", 6, 1), ("mm", 0, 1), ("fa", 0, False, 2),
    ("sa", 0, 2), ("mm", 4, 1), ("mm", 1, 1), ("za", 2, 2), ("sa", 1, 2), ("mm", 7, 1),
    ("mm", 3, 1), ("co", 4, 1), ("mm", 5, 1), ("za", 0, 3), ("co", 7, 1), ("mm", 2, 1),
    ("co", 6, 1), ("co", 4, 0), ("co", 1, 1), ("co", 0, 1), ("za", 1, 3), ("fa", 0, True, 2),
    ("sa", 3, 2), ("co", 2, 1), ("fa", 1, False, 2), ("co", 3, 0), ("fx", 2), ("sa", 0, 3),
    ("fa", 1, True, 2), ("za", 3, 3), ("co", 5, 1), ("fa", 0, False, 3), ("co", 5, 0),
    ("co", 1, 0), ("fy", 2), ("mm", 1, 2), ("mm", 4, 2), ("mm", 2, 2), ("sa", 1, 3), ("cf", 0),
    ("mm", 5, 2), ("fa", 1, False, 3), ("za", 2, 3), ("sd", 7, 1), ("mm", 7, 2), ("cf", 2),
    ("mm", 3, 2), ("sd", 1, 1), ("fa", 0, True, 3), ("mm", 0, 2), ("co", 5, 2), ("fx", 3),
    ("co", 4, 2), ("co", 3, 2), ("fa", 1, True, 3), ("sa", 3, 3), ("co", 0, 2), ("sd", 2, 1),
    ("co", 1, 2), ("sd", 6, 1), ("fy", 3), ("mm", 0, 3), ("mm", 4, 3), ("mm", 3, 3), ("cf", 3),
    ("co", 0, 3), ("bz", 0, 1, False), ("mm", 2, 3), ("sd", 5, 2), ("mm", 7, 3),
    ("bz", 0, 1, True), ("mm", 6, 3), ("co", 3, 3), ("mm", 1, 3), ("sd", 3, 2), ("co", 7, 3),
    ("co", 4, 3), ("bz", 4, 1, True), ("mm", 5, 3), ("mm", 6, 2), ("co", 1, 3),
    ("bz", 4, 1, False), ("co", 6, 3), ("sd", 3, 3), ("pz", 3, 1), ("cf", 1), ("co", 5, 3),
    ("co", 6, 2), ("bz", 4, 2, True), ("co", 7, 2), ("sd", 1, 2), ("co", 3, 1), ("sd", 1, 3),
    ("sd", 7, 3), ("pz", 1, 1), ("bz", 0, 2, True), ("gw",), ("sd", 5, 3), ("pz", 5, 1),
    ("bz", 4, 2, False), ("sd", 6, 3), ("tc",), ("co", 7, 0), ("bo", 4, True), ("co", 2, 2),
    ("sd", 6, 2), ("pz", 6, 1), ("sd", 7, 2), ("pz", 7, 1), ("pz", 1, 2), ("sd", 5, 1),
    ("pz", 5, 2), ("sd", 3, 1), ("pz", 3, 2), ("co", 2, 3), ("pj",), ("bz", 0, 2, False),
    ("pz", 7, 2), ("sd", 2, 2), ("sd", 2, 3), ("pz", 2, 1), ("bo", 0, True), ("pz", 6, 2),
    ("bo", 4, False), ("sd", 3, 0), ("bs", 4), ("fi", 3), ("sd", 1, 0), ("fi", 1), ("sd", 7, 0),
    ("fi", 7), ("bo", 0, False), ("pz", 2, 2), ("rw", 4), ("bs", 0), ("rw", 0), ("sd", 6, 0),
    ("fi", 6), ("rw", 6), ("sd", 5, 0), ("sd", 2, 0), ("fi", 2), ("fi", 5), ("rw", 5), ("rw", 3),
    ("rw", 7), ("rw", 1), ("rw", 2),
)


def step_order(depth, layout, chunks):
    planar = range(len(layout))
    hops = range(1, depth - 1)
    steps = [("ow", p) for p in planar]
    for d in range(depth):
        steps += [("za", p, d) for p in planar if d]
        steps += [("sa", p, d) for p in planar if d == 0 or layout[p][0][0] != "b"]
        steps += [("fa", p, f, d) for p in range(2) for f in (False, True) if d or f]
        steps += [("fx", d), ("fy", d)]
    steps += [("gw",)] + [("cf", i) for i in range(depth)] + [("tc",), ("pj",)]
    for k, (_, _, z_first) in enumerate(chunks):
        steps += [("mm", k, i) for i in range(depth)] + [("co", k, i) for i in range(depth)]
        if z_first:
            steps += [("bz", k, hop, flipped) for flipped in (True, False) for hop in hops]
            steps += [("bo", k, True), ("bo", k, False), ("bs", k)]
        else:
            steps += [("sd", k, i) for i in reversed(range(depth))]
            steps += [("pz", k, hop) for hop in hops] + [("fi", k)]
        steps += [("rw", k)]
    return PLAN if sorted(map(str, PLAN)) == sorted(map(str, steps)) else steps


def gather_layout(width):
    tiles = width // LANES
    shares = (
        (("o", 0), 0, 10),
        (("o", 1), 0, 8),
        (("b", 0), 20, 8),
        (("a", 2), 16, 12),
    )
    unit = tiles // 28
    pieces = []
    for kind, start, size in shares:
        last = kind[0] != "o" and start + size == 28
        first = start * unit * LANES
        stop = width if last else first + size * unit * LANES
        pieces.append((kind, first, stop - first + (LANES if kind[1] == 2 else 0)))
    return pieces


def fused_kernel(
    depth, layout, chunks, plan, x_in, y_in, routes, gates, gate_in, up_in, down_in, basis_in,
    grad_out, proj_out,
    proj,
    x_all, y_all, gate_w, up_w, down_w, basis, pre_gate, pre_up, grad_gate, grad_up, hidden,
    coef, coef_half, far_coef, coef_t, part, from_core, from_side, from_z, from_zb, from_plane,
    recv_sem, up_sem, down_sem, side_sem, plane_sem, core_sem, local_sem, coef_sem,
    sum_core_sem, sum_side_sem, sum_z_sem, sum_plane_sem,
):
    dp = lax.axis_index("dp")
    me = lax.axis_index("expert")
    z, y, core = me // 4, (me // 2) % 2, me % 2
    rows, width = x_in.shape
    half = width // 2
    hidden_width = gate_w.shape[1]
    rank = basis.shape[1]
    plane_rows = 4 * rows
    core_device = (dp, z * 4 + y * 2 + 1 - core)
    side_device = (dp, z * 4 + (1 - y) * 2 + core)
    plane_device = (1 - dp, me)
    order = [
        sorted(range(depth), key=lambda q, p=p: (abs(q - p), q if 2 * p < depth else -q))
        for p in range(depth)
    ]
    seq = [
        sum(jnp.where(z == p, order[p][i], 0) for p in range(depth)) for i in range(depth)
    ]

    pieces = []
    for kind, start, size in layout:
        source, whole = ((x_in, x_all), (y_in, y_all), (None, y_all))[kind[1]]
        if kind[0] == "o":
            cols = pl.ds(pl.multiple_of(dp * size, LANES), size)
        else:
            cols = pl.ds(start, size)
        pieces.append((source, whole, cols))
    for kind, start, size in layout[:2]:
        source, whole = ((x_in, x_all), (y_in, y_all))[kind[1]]
        pieces.append((source, whole, pl.ds(pl.multiple_of((1 - dp) * size, LANES), size)))
    planar = range(len(layout))
    relayed = range(2)
    far = len(layout)
    y_first = [kind[0] == "b" for kind, _, _ in layout]

    def index(zz, yy, cc):
        return zz * 4 + yy * 2 + cc

    def item_rows(item):
        return pl.ds(pl.multiple_of(item * rows, rows), rows)

    def landed(piece, item):
        _, whole, cols = pieces[piece]
        return whole.at[item_rows(item), cols]

    def copy(piece, item, own, sem, device, recv_piece):
        start, _, cols = pieces[piece]
        src = start.at[:, cols] if own and start is not None else landed(piece, item)
        return pltpu.make_async_remote_copy(
            src_ref=src,
            dst_ref=landed(piece, item),
            send_sem=sem,
            recv_sem=recv_sem.at[recv_piece, item],
            device_id=device,
            device_id_type=MESH,
        )

    def up(piece, zz, yy, own=False):
        item = index(zz, yy, core)
        return copy(piece, item, own, up_sem.at[piece, item // 2], (dp, me + 4), piece)

    def down(piece, zz, yy, own=False):
        item = index(zz, yy, core)
        return copy(piece, item, own, down_sem.at[piece, item // 2], (dp, me - 4), piece)

    def side(piece, zz, own=False):
        return copy(piece, index(zz, y, core), own, side_sem.at[piece, zz], side_device, piece)

    def plane(piece, zz, yy):
        item = index(zz, yy, core)
        return copy(piece, item, False, plane_sem.at[piece, item // 2], plane_device, far + piece)

    def other(piece, zz, yy, own=False):
        item = index(zz, yy, core)
        return copy(piece, item, own, core_sem.at[piece, item // 2], core_device, piece)

    def arrive(piece, item):
        copy(piece, item, False, core_sem.at[0, 0], (dp, me), piece).wait_recv()

    own_loads = [
        pltpu.make_async_copy(a, b, local_sem.at[i])
        for i, (a, b) in enumerate((
            (y_in, y_all.at[item_rows(me), pl.ds(0, width)]), (x_in, x_all.at[item_rows(me), :]),
            (gate_in, gate_w), (up_in, up_w), (down_in, down_w), (basis_in, basis),
        ))
    ]
    for one in own_loads:
        one.start()

    lane = lax.broadcasted_iota(jnp.int32, (LANES, rows), 0)
    table = jnp.zeros((LANES, rows), jnp.float32)
    for k in range(routes.shape[0]):
        table = table + jnp.where(
            routes[k : k + 1, :] == lane, gates[k : k + 1, :].astype(jnp.float32), 0.0
        )
    y_all[item_rows(me), width : width + LANES] = table.T.astype(jnp.bfloat16)

    barrier = pltpu.get_barrier_semaphore()

    def greet(device):
        pl.semaphore_signal(barrier, inc=1, device_id=device, device_id_type=MESH)

    greet(plane_device)
    greet(side_device)
    greet(core_device)
    pl.when(z > 0)(lambda: greet((dp, me - 4)))
    pl.when(z < depth - 1)(lambda: greet((dp, me + 4)))
    pl.semaphore_wait(barrier, 3 + jnp.minimum(z, 1) + jnp.minimum(depth - 1 - z, 1))

    def spots(away):
        if away == 0:
            return [(z, None)]
        return [(z - away, z >= away), (z + away, z + away < depth)]

    def guarded(condition, act):
        act() if condition is None else pl.when(condition)(act)

    def rise(piece, zz, yy, own=False):
        pl.when(z < depth - 1)(lambda: up(piece, zz, yy, own).start())

    def fall(piece, zz, yy, own=False):
        pl.when(z > 0)(lambda: down(piece, zz, yy, own).start())

    def send_own(piece):
        if pieces[piece][0] is None:
            own_loads[0].wait()
        side(piece, z, True).start()
        rise(piece, z, y, True)
        fall(piece, z, y, True)
        other(piece, z, y, True).start()
        if piece in relayed:
            other(far + piece, z, y, True).start()

    def take_z(piece, away):
        for (zz, there), onward in zip(spots(away), (rise, fall)):
            def act(zz=zz, onward=onward):
                for yy in (y, 1 - y) if y_first[piece] else (y,):
                    arrive(piece, index(zz, yy, core))
                    if not y_first[piece]:
                        side(piece, zz).start()
                    onward(piece, zz, yy)
                    if piece in relayed:
                        plane(piece, zz, yy).start()
                    other(piece, zz, yy).start()

            guarded(there, act)

    def take_side(piece, away):
        for zz, there in spots(away):
            def act(zz=zz):
                arrive(piece, index(zz, 1 - y, core))
                if y_first[piece]:
                    rise(piece, zz, 1 - y)
                    fall(piece, zz, 1 - y)
                if piece in relayed:
                    plane(piece, zz, 1 - y).start()
                other(piece, zz, 1 - y).start()

            guarded(there, act)

    def take_far(piece, flipped, away):
        yy = 1 - y if flipped else y
        for zz, there in spots(away):
            def act(zz=zz):
                arrive(far + piece, index(zz, yy, core))
                other(far + piece, zz, yy).start()

            guarded(there, act)

    def take_core(kinds, away):
        numbers = [p for p, (kind, _, _) in enumerate(layout) if kind[1] in kinds]
        numbers += [far + p for p in numbers if p in relayed]
        for zz, there in spots(away):
            def act(zz=zz):
                for each in numbers:
                    arrive(each, index(zz, 0, 1 - core))
                    arrive(each, index(zz, 1, 1 - core))

            guarded(there, act)

    def rows_of(zz):
        return pl.ds(pl.multiple_of(zz * plane_rows, plane_rows), plane_rows)

    def coef_copy(i):
        return pltpu.make_async_remote_copy(
            src_ref=coef_half.at[rows_of(seq[i]), :],
            dst_ref=far_coef.at[rows_of(seq[i]), :],
            send_sem=coef_sem.at[0, i],
            recv_sem=coef_sem.at[1, i],
            device_id=plane_device,
            device_id_type=MESH,
        )

    def inner_forward(i):
        if i == 0:
            for one in own_loads[1:]:
                one.wait()
        take_core((0,), i)
        at = rows_of(seq[i])

        @pl.loop(0, hidden_width // TILE)
        def _(n):
            cols = pl.ds(pl.multiple_of(n * TILE, TILE), TILE)
            pre_gate[:, cols] = jnp.dot(
                x_all[at, :], gate_w[:, cols], preferred_element_type=jnp.float32
            )
            pre_up[:, cols] = jnp.dot(
                x_all[at, :], up_w[:, cols], preferred_element_type=jnp.float32
            )

    def inner_backward(i):
        take_core((1, 2), i)
        at = rows_of(seq[i])
        expert = lax.broadcasted_iota(jnp.int32, (plane_rows, LANES), 1)
        gain = jnp.sum(
            jnp.where(expert == me, y_all[at, width : width + LANES].astype(jnp.float32), 0.0),
            axis=1,
            keepdims=True,
        )

        @pl.loop(0, hidden_width // TILE)
        def _(n):
            cols = pl.ds(pl.multiple_of(n * TILE, TILE), TILE)
            grad_hidden = lax.dot_general(
                y_all[at, 0:width], down_w[cols, :], CONTRACT_LAST, preferred_element_type=jnp.float32
            )
            a = pre_gate[:, cols]
            u = pre_up[:, cols]
            sigma = jax.nn.sigmoid(a)
            silu = a * sigma
            scaled = gain * grad_hidden
            grad_up[at, cols] = (scaled * silu).astype(jnp.bfloat16)
            grad_gate[at, cols] = (scaled * u * sigma * (1.0 + a * (1.0 - sigma))).astype(
                jnp.bfloat16
            )
            hidden[:, cols] = (silu * u).astype(jnp.bfloat16)

        low = jnp.dot(grad_gate[at, :], basis[...], preferred_element_type=jnp.float32)
        mid = jnp.dot(grad_up[at, :], basis[...], preferred_element_type=jnp.float32)
        top = gain * jnp.dot(hidden[...], basis[...], preferred_element_type=jnp.float32)
        for j, value in enumerate((low, mid, top)):
            coef[at, j * rank : (j + 1) * rank] = value
            coef_half[at, j * rank : (j + 1) * rank] = value.astype(jnp.bfloat16)

    def send_coef(i):
        coef_copy(i).start()

    def gather_sent():
        for piece in planar:
            for zz in range(depth):
                if not y_first[piece]:
                    side(piece, zz).wait_send()
                for yy in (y, 1 - y) if y_first[piece] else (y,):
                    pl.when((zz <= z) & (z < depth - 1))(
                        lambda p=piece, q=zz, yy=yy: up(p, q, yy).wait_send()
                    )
                    pl.when((zz >= z) & (z > 0))(
                        lambda p=piece, q=zz, yy=yy: down(p, q, yy).wait_send()
                    )
            if y_first[piece]:
                side(piece, z).wait_send()
        for piece in relayed:
            for pair in range(2 * depth):
                pl.when(pair != me // 2)(
                    lambda p=piece, q=pair: plane(p, q // 2, q % 2).wait_send()
                )
        for piece in range(len(pieces)):
            for pair in range(2 * depth):
                other(piece, pair // 2, pair % 2).wait_send()

    def remote(src, dst, send, recv, device):
        return pltpu.make_async_remote_copy(
            src_ref=src, dst_ref=dst, send_sem=send, recv_sem=recv,
            device_id=device, device_id_type=MESH,
        )

    crossed = [k for k, chunk in enumerate(chunks) if chunk[2]]

    def cols_of(k):
        return pl.ds(chunks[k][0], chunks[k][1])

    def sum_core_copy(k, i):
        pair = pl.ds(seq[i] * 2, 2)
        return remote(
            part.at[pair, 1 - core, :, cols_of(k)], from_core.at[pair, :, cols_of(k)],
            sum_core_sem.at[0, k, i], sum_core_sem.at[1, k, i], core_device,
        )

    def sum_side_copy(k, zz):
        return remote(
            part.at[zz * 2 + 1 - y, core, :, cols_of(k)], from_side.at[zz, :, cols_of(k)],
            sum_side_sem.at[0, k, zz], sum_side_sem.at[1, k, zz], side_device,
        )

    def sum_z_copy(k, zz, upward, flipped=False):
        way = 0 if upward else 1
        if flipped:
            number = crossed.index(k)
            landing = from_zb.at[way, zz, :, pl.ds(number * chunks[k][1], chunks[k][1])]
            number += len(chunks)
        else:
            number = k
            landing = from_z.at[way, zz, :, cols_of(k)]
        slot = zz * 2 + (1 - y if flipped else y)
        return remote(
            part.at[slot, core, :, cols_of(k)], landing,
            sum_z_sem.at[0, way, number, zz], sum_z_sem.at[1, way, number, zz],
            (dp, me + 4 if upward else me - 4),
        )

    def sum_plane_copy(k):
        start, size, _ = chunks[k]
        return remote(
            part.at[z * 2 + y, core, :, cols_of(k)], from_plane.at[:, pl.ds(start % half, size)],
            sum_plane_sem.at[0, k], sum_plane_sem.at[1, k], plane_device,
        )

    def add_into(slot, k, term):
        total = part[slot, core, :, cols_of(k)].astype(jnp.float32) + term.astype(jnp.float32)
        part[slot, core, :, cols_of(k)] = total.astype(jnp.bfloat16)

    def multiply(k, i):
        start, size, _ = chunks[k]
        at = rows_of(seq[i])

        @pl.loop(0, size // TILE)
        def _(n):
            cols = pl.ds(pl.multiple_of(start + n * TILE, TILE), TILE)
            rows_out = lax.dot_general(
                grad_gate[at, :], gate_w[cols, :], CONTRACT_LAST,
                preferred_element_type=jnp.float32,
            ) + lax.dot_general(
                grad_up[at, :], up_w[cols, :], CONTRACT_LAST,
                preferred_element_type=jnp.float32,
            )
            part[pl.ds(seq[i] * 2, 2), :, :, cols] = rows_out.astype(jnp.bfloat16).reshape(
                2, 2, rows, TILE
            )

        sum_core_copy(k, i).start()

    def over_cores(k, i):
        zz = seq[i]
        sum_core_copy(k, i).wait_recv()
        slot = zz * 2 + 1 - y
        add_into(slot, k, from_core[slot, :, cols_of(k)])
        if not chunks[k][2]:
            sum_side_copy(k, zz).start()
        slot = zz * 2 + y
        add_into(slot, k, from_core[slot, :, cols_of(k)])
        if chunks[k][2]:
            for flipped in (True, False):
                pl.when((z == 0) & (zz > 0))(
                    lambda f=flipped: sum_z_copy(k, zz, True, f).start()
                )
                pl.when((z == depth - 1) & (zz < z))(
                    lambda f=flipped: sum_z_copy(k, zz, False, f).start()
                )

    def z_term(k, zz, upward, flipped):
        sum_z_copy(k, zz, upward, flipped).wait_recv()
        if flipped:
            size = chunks[k][1]
            at = pl.ds(crossed.index(k) * size, size)
            term = from_zb[0 if upward else 1, zz, :, at]
        else:
            term = from_z[0 if upward else 1, zz, :, cols_of(k)]
        add_into(zz * 2 + (1 - y if flipped else y), k, term)

    def pass_on(k, hop, flipped=False):
        def climb():
            for zz in reversed(range(hop + 1, depth)):
                z_term(k, zz, True, flipped)
                sum_z_copy(k, zz, True, flipped).start()

        def sink():
            for zz in range(depth - 1 - hop):
                z_term(k, zz, False, flipped)
                sum_z_copy(k, zz, False, flipped).start()

        pl.when(z == hop)(climb)
        pl.when(z == depth - 1 - hop)(sink)

    def own_plane(k, flipped=False):
        pl.when(z > 0)(lambda: z_term(k, z, True, flipped))
        pl.when(z < depth - 1)(lambda: z_term(k, z, False, flipped))

    def over_side(k, i):
        zz = seq[i]
        sum_side_copy(k, zz).wait_recv()
        add_into(zz * 2 + y, k, from_side[zz, :, cols_of(k)])
        pl.when((z == 0) & (zz > 0))(lambda: sum_z_copy(k, zz, True).start())
        pl.when((z == depth - 1) & (zz < z))(lambda: sum_z_copy(k, zz, False).start())

    def leave(k):
        pl.when(dp != chunks[k][0] // half)(lambda: sum_plane_copy(k).start())

    def finish(k):
        own_plane(k)
        leave(k)

    def crossed_own(k, flipped):
        own_plane(k, flipped)
        if flipped:
            sum_side_copy(k, z).start()

    def crossed_side(k):
        sum_side_copy(k, z).wait_recv()
        add_into(z * 2 + y, k, from_side[z, :, cols_of(k)])
        leave(k)

    def turn_coef():
        for i in range(depth):
            coef_copy(i).wait_recv()
        coef_t[...] = (coef[...] + far_coef[...].astype(jnp.float32)).T.astype(jnp.bfloat16)

    def project():
        @pl.loop(0, half // TILE)
        def _(n):
            cols = pl.ds(pl.multiple_of(dp * half + n * TILE, TILE), TILE)
            at = pl.ds(pl.multiple_of(n * TILE, TILE), TILE)
            front = jnp.dot(
                coef_t[0 : 2 * rank, :], x_all[:, cols], preferred_element_type=jnp.float32
            ).T.astype(jnp.bfloat16)
            proj[0, at, :] = front[:, 0:rank]
            proj[1, at, :] = front[:, rank : 2 * rank]
            proj[2, at, :] = jnp.dot(
                coef_t[2 * rank : 3 * rank, :], y_all[:, cols], preferred_element_type=jnp.float32
            ).T.astype(jnp.bfloat16)

    def sums_sent(k):
        start, _, z_first = chunks[k]
        pl.when(dp != start // half)(lambda: sum_plane_copy(k).wait_send())
        for i in range(depth):
            sum_core_copy(k, i).wait_send()
        if z_first:
            sum_side_copy(k, z).wait_send()
        for zz in range(depth):
            if not z_first:
                sum_side_copy(k, zz).wait_send()
            for flipped in (False, True) if z_first else (False,):
                pl.when(zz > z)(lambda zz=zz, f=flipped: sum_z_copy(k, zz, True, f).wait_send())
                pl.when(zz < z)(lambda zz=zz, f=flipped: sum_z_copy(k, zz, False, f).wait_send())

    proj_copy = pltpu.make_async_copy(proj, proj_out, local_sem.at[6])

    def give_projected():
        project()
        proj_copy.start()

    stages = {
        "ow": send_own, "za": take_z, "sa": take_side, "fa": take_far, "fx": inner_forward,
        "fy": inner_backward, "cf": send_coef, "gw": gather_sent,
        "mm": multiply, "co": over_cores, "sd": over_side, "pz": pass_on, "fi": finish,
        "bz": pass_on, "bo": crossed_own, "bs": crossed_side, "tc": turn_coef, "pj": give_projected, "rw": sums_sent,
    }
    for stage, *at in plan:
        stages[stage](*at)

    for k, (start, size, _) in enumerate(chunks):
        def take_plane(k=k, start=start, size=size):
            sum_plane_copy(k).wait_recv()
            at = pl.ds(start % half, size)
            total = part[z * 2 + y, core, :, cols_of(k)].astype(jnp.float32) + from_plane[
                :, at
            ].astype(jnp.float32)
            grad_out[:, at] = total.astype(jnp.bfloat16)

        pl.when(dp == start // half)(take_plane)

    for i in range(depth):
        coef_copy(i).wait_send()
    proj_copy.wait()


def dense_form(
    saved_inputs, output_grad, routes, route_gates, expert_gate, expert_up, expert_down, proj_basis
):
    expert_count = lax.axis_size("expert")
    group_count = lax.axis_size("dp")
    rows, width = saved_inputs.shape
    all_rows = rows * expert_count
    hidden_width = expert_gate.shape[2]
    rank = proj_basis.shape[2]
    depth = expert_count // 4
    half = width // group_count
    layout = gather_layout(width)
    chunks = column_chunks(half)
    crossed_width = sum(size for _, size, z_first in chunks if z_first)
    dma = pltpu.SemaphoreType.DMA
    bf16, f32 = jnp.bfloat16, jnp.float32
    whole = pl.BlockSpec(memory_space=pl.ANY)
    held = pl.BlockSpec(memory_space=pltpu.VMEM)
    token_grad, terms = pl.pallas_call(
        functools.partial(
            fused_kernel, depth, layout, chunks, step_order(depth, layout, chunks)
        ),
        out_shape=[
            jax.ShapeDtypeStruct((rows, half), bf16),
            jax.ShapeDtypeStruct((3, half, rank), bf16),
        ],
        in_specs=[whole, whole, held, held, whole, whole, whole, whole],
        out_specs=[held, whole],
        scratch_shapes=[
            pltpu.VMEM((3, half, rank), bf16),
            pltpu.VMEM((all_rows, width), bf16),
            pltpu.VMEM((all_rows, width + LANES), bf16),
            pltpu.VMEM((width, hidden_width), bf16),
            pltpu.VMEM((width, hidden_width), bf16),
            pltpu.VMEM((hidden_width, width), bf16),
            pltpu.VMEM((hidden_width, rank), bf16),
            pltpu.VMEM((4 * rows, hidden_width), f32),
            pltpu.VMEM((4 * rows, hidden_width), f32),
            pltpu.VMEM((all_rows, hidden_width), bf16),
            pltpu.VMEM((all_rows, hidden_width), bf16),
            pltpu.VMEM((4 * rows, hidden_width), bf16),
            pltpu.VMEM((all_rows, 3 * rank), f32),
            pltpu.VMEM((all_rows, 3 * rank), bf16),
            pltpu.VMEM((all_rows, 3 * rank), bf16),
            pltpu.VMEM((3 * rank, all_rows), bf16),
            pltpu.VMEM((2 * depth, 2, rows, width), bf16),
            pltpu.VMEM((2 * depth, rows, width), bf16),
            pltpu.VMEM((depth, rows, width), bf16),
            pltpu.VMEM((2, depth, rows, width), bf16),
            pltpu.VMEM((2, depth, rows, crossed_width), bf16),
            pltpu.VMEM((rows, half), bf16),
            dma((len(layout) + 2, expert_count)),
            dma((len(layout), 2 * depth)),
            dma((len(layout), 2 * depth)),
            dma((len(layout), depth)),
            dma((2, 2 * depth)),
            dma((len(layout) + 2, 2 * depth)),
            dma((7,)),
            dma((2, depth)),
            dma((2, len(chunks), depth)),
            dma((2, len(chunks), depth)),
            dma((2, 2, len(chunks) + 2, depth)),
            dma((2, len(chunks))),
        ],
        compiler_params=pltpu.CompilerParams(
            collective_id=0, has_side_effects=True, vmem_limit_bytes=60 * 1024 * 1024
        ),
    )(
        saved_inputs, output_grad, routes.T, route_gates.T,
        expert_gate[0], expert_up[0], expert_down[0], proj_basis[0],
    )
    return (token_grad, terms.astype(f32).transpose(1, 0, 2)[None])


def on_device(*arrays):
    if lax.axis_size("expert") <= 2 * arrays[2].shape[1]:
        return dense_form(*arrays)
    return slot_form(*arrays)


def solution(mesh):
    placed = (
        P("expert", None),
        P("expert", None),
        P("expert", None),
        P("expert", None),
        P("expert", None, "dp"),
        P("expert", None, "dp"),
        P("expert", "dp", None),
        P("expert", "dp", None),
    )
    return jax.shard_map(
        on_device,
        mesh=mesh,
        in_specs=placed,
        out_specs=(P("expert", "dp"), P("expert", "dp", None, None)),
        check_vma=False,
    )
```
